32 devices in a mesh: dp: 8 (over z, x), seq: 4 (over y, core).
Axes of the slice: x: 2, y: 2, z: 4, core: 2. Of those that a mesh axis runs over, the one named last changes fastest.
Arguments:
- layer_input: bfloat16 [20480, 768], P(('dp', 'seq')), may hold values from -6 to 6
- segment_ids: int32 [8, 2560], P('dp'), may hold values from 0 to 2, never falling along the last dimension, each value on 1 to 2048 neighbouring positions
- cotangent: bfloat16 [20480, 768], P(('dp', 'seq')), may hold values from -6 to 6
- attn_gain: bfloat16 [768], replicated, may hold values from 0.25 to 1.75
- attn_shift: bfloat16 [768], replicated, may hold values from -1.796875 to 1.796875
- query_weight: bfloat16 [768, 768], P(None, 'seq'), may hold values from -0.21875 to 0.21875
- query_bias: bfloat16 [768], P('seq'), may hold values from -1.796875 to 1.796875
- key_weight: bfloat16 [768, 768], P(None, 'seq'), may hold values from -0.21875 to 0.21875
- value_weight: bfloat16 [768, 768], P(None, 'seq'), may hold values from -0.21875 to 0.21875
- value_bias: bfloat16 [768], P('seq'), may hold values from -0.1796875 to 0.1796875
- out_weight: bfloat16 [768, 768], P('seq'), may hold values from -6 to 6
- out_bias: bfloat16 [768], replicated, may hold values from -1.796875 to 1.796875
- ffn_gain: bfloat16 [768], replicated, may hold values from 0.25 to 1.75
- ffn_shift: bfloat16 [768], replicated, may hold values from -1.796875 to 1.796875
- up_weight: bfloat16 [768, 3072], P(None, 'seq'), may hold values from -0.21875 to 0.21875
- up_bias: bfloat16 [3072], P('seq'), may hold values from -1.796875 to 1.796875
- down_weight: bfloat16 [3072, 768], P('seq'), may hold values from -0.109375 to 0.109375
- down_bias: bfloat16 [768], replicated, may hold values from -1.796875 to 1.796875
Outputs:
- layer_output: bfloat16 [20480, 768], P(('dp', 'seq'))
- input_grad: float32 [20480, 768], P(('dp', 'seq'))
- grad_attn_gain: float32 [768], replicated
- grad_attn_shift: float32 [768], replicated
- grad_query_weight: float32 [768, 768], P(None, 'seq')
- grad_query_bias: float32 [768], P('seq')
- grad_key_weight: float32 [768, 768], P(None, 'seq')
- grad_value_weight: float32 [768, 768], P(None, 'seq')
- grad_value_bias: float32 [768], P('seq')
- grad_out_weight: float32 [768, 768], P('seq')
- grad_out_bias: float32 [768], replicated
- grad_ffn_gain: float32 [768], replicated
- grad_ffn_shift: float32 [768], replicated
- grad_up_weight: float32 [768, 3072], P(None, 'seq')
- grad_up_bias: float32 [3072], P('seq')
- grad_down_weight: float32 [3072, 768], P('seq')
- grad_down_bias: float32 [768], replicated
The draws below stay inside these ranges and needn't reach their ends.
Inputs may be any that keep to these rules, and one draw needn't show every extreme that they name: `segment_ids`: along a row the ids never fall; each of the 3 ids covers 1 to 2048 consecutive tokens, and some document has exactly 2048 tokens.
All inputs are finite; a program needn't handle non-finite values.
Results may differ from the reference program's by a relative error of at most 0.014.
Values may be sent and summed in bfloat16 or wider, within the bound.
A program may use at most 192 MiB of HBM per device.

```python
import functools
import math
import jax
import jax.numpy as jnp
import numpy as np
from jax import lax

D = 768
HEADS = 12
HEAD = 64
FF = 3072
ROW_TOK = 2560
MOST = 2048
ROWS = 8
DOCS = 3
TOKENS = 20480


def steps_of(key, shape, pieces, least, high):
    def one(dim, blocks):
        heights = jax.random.uniform(jax.random.fold_in(jax.random.fold_in(key, 6), dim), (blocks,), jnp.float32, least / len(pieces), high / len(pieces))
        return jnp.repeat(jnp.exp(heights), shape[dim] // blocks).reshape((-1,) + (1,) * (len(shape) - dim - 1))

    factor_of = one(*pieces[0])
    for cut in pieces[1:]:
        factor_of = factor_of * one(*cut)
    return factor_of


def split_up(number_of, total, reach, slope):
    portions = [(1 << 20) // math.isqrt(rank ** slope) + 1 for rank in range(2, number_of + 1)]
    rest, counts = total - reach - (number_of - 1), [1] * (number_of - 1)
    while rest > 0:
        free = [i for i in range(number_of - 1) if counts[i] < reach]
        mass, budget = sum([portions[i] for i in free]), rest
        for i in free:
            extra = min(reach - counts[i], max(1, budget * portions[i] // mass), rest)
            counts[i] = counts[i] + extra
            rest = rest - extra
    return np.array([reach] + counts)


def uneven(rng, number_of, total, most, skew):
    if number_of == 2:
        one = jax.random.randint(rng, (), max(1, total - most), min(most, total - 1) + 1)
        return jnp.stack([one, total - one])
    lengths = jnp.asarray(split_up(number_of, total, most, skew), jnp.int32)
    twos = (number_of - 1) // 2
    donor, taker = lengths[1:1 + 2 * twos:2], lengths[2:2 + 2 * twos:2]
    room = jnp.minimum(donor - 1, most - taker)
    moved = jax.random.randint(jax.random.fold_in(rng, 1), (twos,), 0, 1 << 20) % (room + 1)
    lengths = lengths.at[1:1 + 2 * twos:2].set(donor - moved).at[2:2 + 2 * twos:2].set(taker + moved)
    return lengths[jax.random.permutation(jax.random.fold_in(rng, 2), number_of)]


def gaussian(stream_key, dims, spread, most, pieces=(), held_as=jnp.bfloat16):
    drawn = jax.random.normal(stream_key, dims, jnp.float32) * spread
    if len(pieces) > 0:
        drawn = steps_of(stream_key, dims, pieces, -0.22, 0.18) * drawn
    return jnp.clip(drawn, min=-most, max=most).astype(held_as)


def setup_inputs(seed: int = 0) -> dict:
    streams_of = jax.random.split(jax.random.key(seed), 19)
    layer_input = gaussian(streams_of[0], (TOKENS, D), 1.0, 6.0, ((0, 32),))
    segment_ids = jax.vmap(lambda own: jnp.searchsorted(jnp.cumsum(uneven(own, DOCS, ROW_TOK, MOST, 2)), jnp.arange(ROW_TOK), side="right"))(jax.random.split(streams_of[1], ROWS)).reshape((ROWS, ROW_TOK)).astype(jnp.int32)
    cotangent = gaussian(streams_of[2], (TOKENS, D), 1.0, 6.0, ((0, 32),))
    attn_gain = jnp.clip(1.0 + 0.15 * jax.random.normal(streams_of[3], (D,), jnp.float32), 0.25, 1.75).astype(jnp.bfloat16)
    attn_shift = gaussian(streams_of[4], (D,), 0.3, 1.796875)
    query_weight = gaussian(streams_of[5], (D, D), D ** -0.5, 0.21875, ((1, 4),))
    query_bias = gaussian(streams_of[6], (D,), 0.3, 1.796875, ((0, 4),))
    key_weight = gaussian(streams_of[7], (D, D), D ** -0.5, 0.21875, ((1, 4),))
    value_weight = gaussian(streams_of[8], (D, D), D ** -0.5, 0.21875, ((1, 4),))
    value_bias = gaussian(streams_of[9], (D,), 0.03, 0.1796875, ((0, 4),))
    out_weight = gaussian(streams_of[10], (D, D), (D * 4 // MOST) ** -0.5, 6.0, ((0, 4),))
    out_bias = gaussian(streams_of[11], (D,), 0.3, 1.796875)
    ffn_gain = jnp.clip(1.0 + 0.15 * jax.random.normal(streams_of[12], (D,), jnp.float32), 0.25, 1.75).astype(jnp.bfloat16)
    ffn_shift = gaussian(streams_of[13], (D,), 0.3, 1.796875)
    up_weight = gaussian(streams_of[14], (D, FF), D ** -0.5, 0.21875, ((1, 4),))
    up_bias = gaussian(streams_of[15], (FF,), 0.3, 1.796875, ((0, 4),))
    down_weight = gaussian(streams_of[16], (FF, D), FF ** -0.5, 0.109375, ((0, 4),))
    down_bias = gaussian(streams_of[17], (D,), 0.3, 1.796875)
    return dict(layer_input=layer_input, segment_ids=segment_ids, cotangent=cotangent, attn_gain=attn_gain, attn_shift=attn_shift, query_weight=query_weight, query_bias=query_bias, key_weight=key_weight, value_weight=value_weight, value_bias=value_bias, out_weight=out_weight, out_bias=out_bias, ffn_gain=ffn_gain, ffn_shift=ffn_shift, up_weight=up_weight, up_bias=up_bias, down_weight=down_weight, down_bias=down_bias)


@jax.custom_vjp
def low(v):
    return lax.optimization_barrier(v.astype(jnp.bfloat16)).astype(jnp.float32)

@jax.custom_vjp
def low_back(v):
    return v

def low_keep(v):
    return (low(v), None)

def low_pass(kept, grad):
    return (grad,)

def back_keep(v):
    return (v, None)

def back_low(kept, grad):
    return (low(grad),)
low.defvjp(low_keep, low_pass)
low_back.defvjp(back_keep, back_low)
EPSILON = 1e-06
HIGHEST = lax.Precision.HIGHEST

def matmul(left_side, right_side):
    return jnp.dot(left_side, right_side, precision=HIGHEST, preferred_element_type=jnp.float32)

def layer_norm(values, gain_row, shift_row):
    average = lax.optimization_barrier(jnp.mean(values, axis=-1, keepdims=True))
    centered = values - average
    variance = lax.optimization_barrier(jnp.mean(centered * centered, axis=-1, keepdims=True))
    return centered * lax.rsqrt(variance + EPSILON) * gain_row + shift_row

def attend_head(triple, same_doc):
    query_head, key_head, value_head = triple
    raw_scores = low_back(matmul(query_head, key_head.T))
    scores = jnp.where(same_doc, raw_scores * HEAD ** (-0.5), -1e+30)
    weights = low(jax.nn.softmax(scores, axis=-1))
    return matmul(weights, value_head)

def row_layer(param_list, row_pair):
    row_input, row_segments = row_pair
    attn_gain, attn_shift, query_weight, query_bias, key_weight, value_weight, value_bias, out_weight, out_bias, ffn_gain, ffn_shift, up_weight, up_bias, down_weight, down_bias = param_list
    length = row_input.shape[0]
    normed = low(layer_norm(row_input, attn_gain, attn_shift))
    queries = low_back(low(matmul(normed, query_weight) + query_bias))
    key_rows = low_back(low(matmul(normed, key_weight)))
    value_rows = low_back(low(matmul(normed, value_weight) + value_bias))
    same_doc = row_segments[:, None] == row_segments[None, :]

    def by_head(matrix):
        return matrix.reshape(length, HEADS, HEAD).transpose(1, 0, 2)
    head_mixed = lax.map(jax.checkpoint(functools.partial(attend_head, same_doc=same_doc)), (by_head(queries), by_head(key_rows), by_head(value_rows)))
    mixed_rows = low_back(low(head_mixed.transpose(1, 0, 2).reshape(length, HEADS * HEAD)))
    branch = low_back(matmul(mixed_rows, out_weight) + out_bias)
    middle = row_input + branch
    normed_ffn = low(layer_norm(middle, ffn_gain, ffn_shift))
    hidden = low(jax.nn.gelu(low_back(matmul(normed_ffn, up_weight) + up_bias), approximate=False))
    return middle + matmul(hidden, down_weight) + down_bias

def reference(layer_input, segment_ids, cotangent, attn_gain, attn_shift, query_weight, query_bias, key_weight, value_weight, value_bias, out_weight, out_bias, ffn_gain, ffn_shift, up_weight, up_bias, down_weight, down_bias):
    param_list = tuple((argument_item.astype(jnp.float32) for argument_item in (attn_gain, attn_shift, query_weight, query_bias, key_weight, value_weight, value_bias, out_weight, out_bias, ffn_gain, ffn_shift, up_weight, up_bias, down_weight, down_bias)))
    inputs = layer_input.astype(jnp.float32)

    def forward(inputs_all, *params_all):
        row_blocks = inputs_all.reshape(ROWS, ROW_TOK, D)
        outputs_all = lax.map(jax.checkpoint(functools.partial(row_layer, params_all)), (row_blocks, segment_ids))
        return outputs_all.reshape(TOKENS, D)
    outputs, pullback = jax.vjp(forward, inputs, *param_list)
    grad_input, grad_attn_gain, grad_attn_shift, grad_query_weight, grad_query_bias, grad_key_weight, grad_value_weight, grad_value_bias, grad_out_weight, grad_out_bias, grad_ffn_gain, grad_ffn_shift, grad_up_weight, grad_up_bias, grad_down_weight, grad_down_bias = pullback(cotangent.astype(jnp.float32))
    return (outputs.astype(jnp.bfloat16), grad_input, grad_attn_gain, grad_attn_shift, grad_query_weight, grad_query_bias, grad_key_weight, grad_value_weight, grad_value_bias, grad_out_weight, grad_out_bias, grad_ffn_gain, grad_ffn_shift, grad_up_weight, grad_up_bias, grad_down_weight, grad_down_bias)
```

```python
import functools

import jax
import jax.numpy as jnp
from jax import lax
from jax.experimental import pallas as pl
from jax.experimental.pallas import tpu as pltpu
from jax.sharding import PartitionSpec as P

HEAD = 64
SCALE = HEAD ** (-0.5)
LOG_SCALE = SCALE * 1.4426950408889634
LONGEST = 2048
NN = (((1,), (0,)), ((), ()))
NT = (((1,), (1,)), ((), ()))


EPSILON = 1e-06


def layer_norm(values, gain_row, shift_row):
    average = jnp.mean(values, axis=-1, keepdims=True)
    centered = values - average
    variance = jnp.mean(centered * centered, axis=-1, keepdims=True)
    return centered * lax.rsqrt(variance + EPSILON) * gain_row + shift_row


def exact_gelu(values):
    return jax.nn.gelu(values, approximate=False)


def matmul(left_side, right_side):
    return jnp.dot(left_side, right_side, preferred_element_type=jnp.float32)


def contract_rows(left_side, right_side):
    return lax.dot_general(
        left_side, right_side, (((0,), (0,)), ((), ())), preferred_element_type=jnp.float32
    )


def outer_back(left_side, right_side):
    return lax.dot_general(
        left_side, right_side, (((1,), (1,)), ((), ())), preferred_element_type=jnp.float32
    )


def rotation(segments, longest):
    zeros = jnp.sum((segments == 0).astype(jnp.int32))
    ones = jnp.sum((segments == 1).astype(jnp.int32))
    twos = segments.shape[0] - zeros - ones
    offset = jnp.where(zeros == longest, 0, jnp.where(ones == longest, zeros, zeros + ones))
    border = jnp.where(zeros == longest, ones, jnp.where(ones == longest, twos, zeros))
    return jnp.stack([offset, border])


def dot(left_side, right_side, dims):
    return lax.dot_general(left_side, right_side, dims, preferred_element_type=jnp.float32)


def keep_head(head, values):
    lane = lax.broadcasted_iota(jnp.int32, values.shape, 1)
    inside = (lane >= head * HEAD) & (lane < (head + 1) * HEAD)
    return jnp.where(inside, values, jnp.zeros_like(values))


def forward_kernel(
    rows_of, keys_of, head_count, spans, q_ref, k_ref, v_ref, mixed_ref, mixed_rot_ref, log_ref, q_rot, k_rot, v_heads
):
    length, width = q_ref.shape
    small = length - LONGEST
    offset, border = spans[0], spans[1]

    def rotated(ref):
        return pltpu.roll(ref[...].astype(jnp.float32), length - offset, 0).astype(jnp.bfloat16)

    q_rot[...] = rotated(q_ref)
    k_rot[...] = rotated(k_ref)
    v_all = rotated(v_ref)
    for head in range(head_count):
        v_heads[head] = jnp.concatenate(
            [keep_head(head, v_all), jnp.full((length, 256 - width), 1, jnp.bfloat16)], axis=1
        )

    def block(row, key_base, key_count, masked):
        rows = pl.ds(row, rows_of)
        total = jnp.zeros((rows_of, width), jnp.float32)
        logs = []
        for head in range(head_count):
            q_head = keep_head(head, q_rot[rows, :])
            top, parts = None, []
            for chunk in range(key_count // keys_of):
                keys = pl.ds(key_base + chunk * keys_of, keys_of)
                scores = dot(q_head, k_rot[keys, :], NT)
                if masked:
                    shape = (rows_of, keys_of)
                    row_id = lax.broadcasted_iota(jnp.int32, shape, 0) + (row - LONGEST)
                    key_id = lax.broadcasted_iota(jnp.int32, shape, 1) + chunk * keys_of
                    scores = jnp.where((row_id < border) == (key_id < border), scores, -1e30)
                high = jnp.max(scores, axis=1, keepdims=True)
                top = high if top is None else jnp.maximum(top, high)
                parts.append(scores)
            summed = jnp.zeros((rows_of, 256), jnp.float32)
            for chunk, scores in enumerate(parts):
                keys = pl.ds(key_base + chunk * keys_of, keys_of)
                weights = jnp.exp2((scores - top) * LOG_SCALE).astype(jnp.bfloat16)
                summed = summed + dot(weights, v_heads[head, keys, :], NN)
            norm = summed[:, 255:256]
            total = total + summed[:, :width] * (1.0 / norm)
            logs.append(top * LOG_SCALE + jnp.log2(norm))
        mixed_rot_ref[rows, :] = total
        logs.append(jnp.zeros((rows_of, 128 - head_count), jnp.float32))
        log_ref[rows, :] = jnp.concatenate(logs, axis=1)

    def large(index, nothing):
        block(pl.multiple_of(index * rows_of, rows_of), 0, LONGEST, False)
        return nothing

    def little(index, nothing):
        block(pl.multiple_of(LONGEST + index * rows_of, rows_of), LONGEST, small, True)
        return nothing

    lax.fori_loop(0, LONGEST // rows_of, large, 0)
    lax.fori_loop(0, small // rows_of, little, 0)
    mixed_ref[...] = pltpu.roll(mixed_rot_ref[...], offset, 0).astype(jnp.bfloat16)


def attend_forward(spans, queries, key_rows, value_rows):
    length, width = queries.shape
    head_count = width // HEAD
    vmem = pl.BlockSpec(memory_space=pltpu.VMEM)
    return pl.pallas_call(
        functools.partial(forward_kernel, 512, 512, head_count),
        out_shape=(
            jax.ShapeDtypeStruct((length, width), jnp.bfloat16),
            jax.ShapeDtypeStruct((length, width), jnp.float32),
            jax.ShapeDtypeStruct((length, 128), jnp.float32),
        ),
        in_specs=[pl.BlockSpec(memory_space=pltpu.SMEM), vmem, vmem, vmem],
        out_specs=(vmem, vmem, vmem),
        scratch_shapes=[
            pltpu.VMEM((length, width), jnp.bfloat16),
            pltpu.VMEM((length, width), jnp.bfloat16),
            pltpu.VMEM((head_count, length, 256), jnp.bfloat16),
        ],
        compiler_params=pltpu.CompilerParams(vmem_limit_bytes=60 << 20),
        name="attend_forward",
    )(spans, queries, key_rows, value_rows)


def backward_kernel(
    keys_of,
    rows_of,
    head_count,
    spans,
    q_ref,
    k_ref,
    v_ref,
    d_ref,
    mixed_rot_ref,
    log_ref,
    dq_ref,
    dk_ref,
    dv_ref,
    q_turned,
    d_turned,
    k_rot,
    v_rot,
    k_turned,
    q_heads,
    d_heads,
    dq_turned,
    dk_rot,
    dv_rot,
    log_rows,
    deltas,
):
    length, width = q_ref.shape
    small = length - LONGEST
    offset, border = spans[0], spans[1]
    low, full = jnp.bfloat16, jnp.float32

    def rotated(ref):
        return pltpu.roll(ref[...].astype(full), length - offset, 0)

    q_all = rotated(q_ref)
    q_turned[...] = jnp.transpose(q_all).astype(low)
    k_all = rotated(k_ref)
    k_rot[...] = k_all.astype(low)
    k_turned[...] = jnp.transpose(k_all).astype(low)
    v_rot[...] = rotated(v_ref).astype(low)
    d_all = rotated(d_ref)
    d_turned[...] = jnp.transpose(d_all).astype(low)
    for head in range(head_count):
        q_heads[head] = keep_head(head, q_all.astype(low))
        d_heads[head] = keep_head(head, d_all.astype(low))
    products = jnp.transpose(d_all * mixed_rot_ref[...])
    for head in range(head_count):
        deltas[head : head + 1, :] = jnp.sum(products[head * HEAD : (head + 1) * HEAD, :], axis=0, keepdims=True)
    log_rows[...] = jnp.transpose(log_ref[...])[0:8, :]
    dq_turned[...] = jnp.zeros_like(dq_turned)

    def block(key_row, row_base, row_count, masked):
        keys = pl.ds(key_row, keys_of)
        dk_sum = jnp.zeros((keys_of, width), full)
        dv_sum = jnp.zeros((keys_of, width), full)
        for head in range(head_count):
            k_head = keep_head(head, k_rot[keys, :])
            v_head = keep_head(head, v_rot[keys, :])
            lanes = slice(head * HEAD, (head + 1) * HEAD)
            k_side = k_turned[lanes, keys]
            for chunk in range(row_count // rows_of):
                start = row_base + chunk * rows_of
                rows = slice(start, start + rows_of)
                scores = dot(k_head, q_turned[:, rows], NN)
                dprobs = dot(v_head, d_turned[:, rows], NN)
                probs = jnp.exp2(scores * LOG_SCALE - log_rows[head : head + 1, rows])
                if masked:
                    shape = (keys_of, rows_of)
                    key_id = lax.broadcasted_iota(jnp.int32, shape, 0) + (key_row - LONGEST)
                    row_id = lax.broadcasted_iota(jnp.int32, shape, 1) + chunk * rows_of
                    probs = jnp.where((row_id < border) == (key_id < border), probs, 0.0)
                dv_sum = dv_sum + dot(probs.astype(low), d_heads[head, rows, :], NN)
                draw = (probs * (dprobs - deltas[head : head + 1, rows])).astype(low)
                dk_sum = dk_sum + dot(draw, q_heads[head, rows, :], NN)
                dq_turned[lanes, rows] += dot(k_side, draw, NN)
        dk_rot[keys, :] = dk_sum * SCALE
        dv_rot[keys, :] = dv_sum

    def large(index, nothing):
        block(pl.multiple_of(index * keys_of, keys_of), 0, LONGEST, False)
        return nothing

    def little(index, nothing):
        block(pl.multiple_of(LONGEST + index * keys_of, keys_of), LONGEST, small, True)
        return nothing

    lax.fori_loop(0, LONGEST // keys_of, large, 0)
    lax.fori_loop(0, small // keys_of, little, 0)
    dq_ref[...] = pltpu.roll(jnp.transpose(dq_turned[...] * SCALE), offset, 0).astype(low)
    dk_ref[...] = pltpu.roll(dk_rot[...], offset, 0).astype(low)
    dv_ref[...] = pltpu.roll(dv_rot[...], offset, 0).astype(low)


def attend_backward(spans, queries, key_rows, value_rows, grad_mixed, mixed_rot, log_totals):
    length, width = queries.shape
    head_count = width // HEAD
    vmem = pl.BlockSpec(memory_space=pltpu.VMEM)
    low, full = jnp.bfloat16, jnp.float32
    return pl.pallas_call(
        functools.partial(backward_kernel, 256, 512, head_count),
        out_shape=(jax.ShapeDtypeStruct((length, width), low),) * 3,
        in_specs=[pl.BlockSpec(memory_space=pltpu.SMEM)] + [vmem] * 6,
        out_specs=(vmem,) * 3,
        scratch_shapes=[
            pltpu.VMEM((width, length), low),
            pltpu.VMEM((width, length), low),
            pltpu.VMEM((length, width), low),
            pltpu.VMEM((length, width), low),
            pltpu.VMEM((width, length), low),
            pltpu.VMEM((head_count, length, width), low),
            pltpu.VMEM((head_count, length, width), low),
            pltpu.VMEM((width, length), full),
            pltpu.VMEM((length, width), full),
            pltpu.VMEM((length, width), full),
            pltpu.VMEM((8, length), full),
            pltpu.VMEM((8, length), full),
        ],
        compiler_params=pltpu.CompilerParams(vmem_limit_bytes=60 << 20),
        name="attend_backward",
    )(spans, queries, key_rows, value_rows, grad_mixed, mixed_rot, log_totals)


def local(
    layer_input,
    segment_ids,
    cotangent,
    attn_gain,
    attn_shift,
    query_weight,
    query_bias,
    key_weight,
    value_weight,
    value_bias,
    out_weight,
    out_bias,
    ffn_gain,
    ffn_shift,
    up_weight,
    up_bias,
    down_weight,
    down_bias,
):
    low_type = jnp.bfloat16
    spans = rotation(segment_ids[0], LONGEST)
    inputs = layer_input.astype(jnp.float32)
    normed_one, norm_one_back = jax.vjp(
        layer_norm, inputs, attn_gain.astype(jnp.float32), attn_shift.astype(jnp.float32)
    )
    normed_low = normed_one.astype(low_type)
    normed_rows = lax.all_gather(normed_low, "seq", axis=0, tiled=True)
    queries = (matmul(normed_rows, query_weight) + query_bias).astype(low_type)
    key_rows = matmul(normed_rows, key_weight).astype(low_type)
    value_rows = (matmul(normed_rows, value_weight) + value_bias).astype(low_type)
    mixed_low, mixed_rot, log_totals = attend_forward(spans, queries, key_rows, value_rows)
    middle = inputs + (
        lax.psum_scatter(matmul(mixed_low, out_weight), "seq", scatter_dimension=0, tiled=True)
        + out_bias
    )
    normed_two, norm_two_back = jax.vjp(
        layer_norm, middle, ffn_gain.astype(jnp.float32), ffn_shift.astype(jnp.float32)
    )
    normed_rows_two, cotangent_rows = (
        lax.all_gather(normed_two.astype(low_type), "seq", axis=0, tiled=True),
        lax.all_gather(cotangent, "seq", axis=0, tiled=True),
    )
    pre_act = matmul(normed_rows_two, up_weight) + up_bias
    hidden_float, gelu_back = jax.vjp(exact_gelu, pre_act)
    hidden_low = hidden_float.astype(low_type)
    layer_output = (
        middle
        + lax.psum_scatter(
            matmul(hidden_low, down_weight).astype(jnp.bfloat16),
            "seq",
            scatter_dimension=0,
            tiled=True,
        ).astype(jnp.float32)
        + down_bias
    ).astype(low_type)
    grad_output = cotangent.astype(jnp.float32)
    grad_down_weight = contract_rows(hidden_low, cotangent_rows)
    grad_down_bias = jnp.sum(grad_output, axis=0)
    grad_pre = gelu_back(outer_back(cotangent_rows, down_weight))[0].astype(low_type)
    grad_up_bias = jnp.sum(grad_pre.astype(jnp.float32), axis=0)
    grad_up_weight = contract_rows(normed_rows_two, grad_pre)
    grad_normed_two = lax.psum_scatter(
        outer_back(grad_pre, up_weight), "seq", scatter_dimension=0, tiled=True
    )
    grad_mid_part, grad_ffn_gain, grad_ffn_shift = norm_two_back(grad_normed_two)
    grad_middle = grad_output + grad_mid_part
    grad_branch = grad_middle.astype(low_type)
    grad_out_bias = jnp.sum(grad_branch.astype(jnp.float32), axis=0)
    branch_rows = lax.all_gather(grad_branch, "seq", axis=0, tiled=True)
    grad_out_weight = contract_rows(mixed_low, branch_rows)
    grad_mixed = outer_back(branch_rows, out_weight).astype(low_type)
    grad_q_low, grad_k_low, grad_v_low = attend_backward(
        spans, queries, key_rows, value_rows, grad_mixed, mixed_rot, log_totals
    )
    grad_query_weight = contract_rows(normed_rows, grad_q_low)
    grad_key_weight = contract_rows(normed_rows, grad_k_low)
    grad_value_weight = contract_rows(normed_rows, grad_v_low)
    grad_query_bias = jnp.sum(grad_q_low.astype(jnp.float32), axis=0)
    grad_value_bias = jnp.sum(grad_v_low.astype(jnp.float32), axis=0)
    part_q = outer_back(grad_q_low, query_weight)
    part_k = outer_back(grad_k_low, key_weight)
    part_v = outer_back(grad_v_low, value_weight)
    grad_normed_one = lax.psum_scatter(
        (part_q + part_k + part_v).astype(jnp.bfloat16), "seq", scatter_dimension=0, tiled=True
    ).astype(jnp.float32)
    grad_in_part, grad_attn_gain, grad_attn_shift = norm_one_back(grad_normed_one)
    input_grad = grad_middle + grad_in_part
    (
        grad_query_weight,
        grad_key_weight,
        grad_value_weight,
        grad_out_weight,
        grad_up_weight,
        grad_down_weight,
        grad_query_bias,
        grad_value_bias,
        grad_up_bias,
    ) = lax.psum(
        (
            grad_query_weight,
            grad_key_weight,
            grad_value_weight,
            grad_out_weight,
            grad_up_weight,
            grad_down_weight,
            grad_query_bias,
            grad_value_bias,
            grad_up_bias,
        ),
        "dp",
    )
    (
        grad_attn_gain,
        grad_attn_shift,
        grad_out_bias,
        grad_ffn_gain,
        grad_ffn_shift,
        grad_down_bias,
    ) = lax.psum(
        (
            grad_attn_gain,
            grad_attn_shift,
            grad_out_bias,
            grad_ffn_gain,
            grad_ffn_shift,
            grad_down_bias,
        ),
        ("dp", "seq"),
    )
    return (
        layer_output,
        input_grad,
        grad_attn_gain,
        grad_attn_shift,
        grad_query_weight,
        grad_query_bias,
        grad_key_weight,
        grad_value_weight,
        grad_value_bias,
        grad_out_weight,
        grad_out_bias,
        grad_ffn_gain,
        grad_ffn_shift,
        grad_up_weight,
        grad_up_bias,
        grad_down_weight,
        grad_down_bias,
    )


def solution(mesh):
    return jax.shard_map(
        local,
        mesh=mesh,
        in_specs=(
            P(("dp", "seq"), None),
            P("dp", None),
            P(("dp", "seq"), None),
            P(),
            P(),
            P(None, "seq"),
            P("seq"),
            P(None, "seq"),
            P(None, "seq"),
            P("seq"),
            P("seq", None),
            P(),
            P(),
            P(),
            P(None, "seq"),
            P("seq"),
            P("seq", None),
            P(),
        ),
        out_specs=(
            P(("dp", "seq"), None),
            P(("dp", "seq"), None),
            P(),
            P(),
            P(None, "seq"),
            P("seq"),
            P(None, "seq"),
            P(None, "seq"),
            P("seq"),
            P("seq", None),
            P(),
            P(),
            P(),
            P(None, "seq"),
            P("seq"),
            P("seq", None),
            P(),
        ),
        check_vma=False,
    )
```

```python
import functools

import jax
import jax.numpy as jnp
from jax import lax
from jax.experimental import pallas as pl
from jax.experimental.pallas import tpu as pltpu
from jax.sharding import PartitionSpec as P

HEAD = 64
SCALE = HEAD ** (-0.5)
LOG_SCALE = SCALE * 1.4426950408889634
LONGEST = 2048
EPSILON = 1e-06
NN = (((1,), (0,)), ((), ()))
NT = (((1,), (1,)), ((), ()))
TN = (((0,), (0,)), ((), ()))
MESH = pl.DeviceIdType.MESH
LOW = jnp.bfloat16
FULL = jnp.float32
VMEM = pl.BlockSpec(memory_space=pltpu.VMEM)
SMEM = pl.BlockSpec(memory_space=pltpu.SMEM)
ANY = pl.BlockSpec(memory_space=pl.ANY)
DMA = pltpu.SemaphoreType.DMA


def flip(index, bit):
    size = 1 << bit
    return index + size - 2 * size * lax.rem(lax.div(index, size), 2)


class Team:
    def __init__(self):
        self.row = lax.axis_index("dp")
        self.me = lax.axis_index("seq")
        self.sibling = flip(self.me, 0)
        self.far = flip(self.me, 1)
        self.diagonal = flip(self.sibling, 1)

    def device(self, index):
        return (self.row, index)

    def greet(self, others):
        barrier = pltpu.get_barrier_semaphore()
        for other in others:
            pl.semaphore_signal(barrier, inc=1, device_id=self.device(other), device_id_type=MESH)
        pl.semaphore_wait(barrier, len(others))

    def copy(self, source, target, send, receive, other):
        return pltpu.make_async_remote_copy(
            src_ref=source,
            dst_ref=target,
            send_sem=send,
            recv_sem=receive,
            device_id=self.device(other),
            device_id_type=MESH,
        )


def rows_at(start, count, multiple):
    return pl.ds(pl.multiple_of(start, multiple), count)


def standardize(values):
    average = jnp.mean(values, axis=-1, keepdims=True)
    centered = values - average
    variance = jnp.mean(centered * centered, axis=-1, keepdims=True)
    inverse = lax.rsqrt(variance + EPSILON)
    return centered * inverse, inverse


def norm_back(grad, gain_row, standard, inverse):
    scaled = grad * gain_row
    mean_one = jnp.mean(scaled, axis=-1, keepdims=True)
    mean_two = jnp.mean(scaled * standard, axis=-1, keepdims=True)
    return inverse * (scaled - mean_one - standard * mean_two)


def column_sums(values):
    return jnp.sum(values, axis=0, keepdims=True)


def rotation(segments, longest):
    zeros = jnp.sum((segments == 0).astype(jnp.int32))
    ones = jnp.sum((segments == 1).astype(jnp.int32))
    twos = segments.shape[0] - zeros - ones
    offset = jnp.where(zeros == longest, 0, jnp.where(ones == longest, zeros, zeros + ones))
    border = jnp.where(zeros == longest, ones, jnp.where(ones == longest, twos, zeros))
    return jnp.stack([offset, border])


def dot(left_side, right_side, dims):
    return lax.dot_general(left_side, right_side, dims, preferred_element_type=jnp.float32)


def keep_head(head, values):
    lane = lax.broadcasted_iota(jnp.int32, values.shape, 1)
    inside = (lane >= head * HEAD) & (lane < (head + 1) * HEAD)
    return jnp.where(inside, values, jnp.zeros_like(values))


class Spread:
    def __init__(self, team, source, target, sems, local_sem):
        self.team, self.source, self.target, self.sems, self.local_sem = team, source, target, sems, local_sem
        self.size = source.shape[0]

    def place(self, owner):
        return self.target.at[rows_at(owner * self.size, self.size, self.size)]

    def across(self):
        here = self.place(self.team.me)
        return self.team.copy(self.source, here, self.sems.at[0], self.sems.at[1], self.team.far)

    def near(self):
        here = self.place(self.team.me)
        return self.team.copy(self.source, here, self.sems.at[2], self.sems.at[3], self.team.sibling)

    def passed(self):
        there = self.place(self.team.far)
        return self.team.copy(there, there, self.sems.at[4], self.sems.at[5], self.team.sibling)

    def kept(self):
        return pltpu.make_async_copy(self.source, self.place(self.team.me), self.local_sem)

    def start(self):
        self.across().start()
        self.near().start()
        self.kept().start()

    def middle(self):
        self.across().wait_recv()
        self.passed().start()

    def finish(self):
        self.across().wait_send()
        self.near().wait()
        self.passed().wait()
        self.kept().wait()


EXTRA = 72


def rotate(ref, shift, length, put):
    width = ref.shape[2]
    sub = lax.broadcasted_iota(jnp.int32, (32, 8, width), 1)

    def one(index, nothing):
        start = lax.rem(shift + index * 256, length)
        group = lax.div(start, 8)
        skip = start - group * 8
        turned = pltpu.roll(ref[pl.ds(group, 33)], lax.rem(8 - skip, 8), 1)
        block = jnp.where(sub < 8 - skip, turned[:32], turned[1:])
        put(index, block.reshape(256, width))
        return nothing

    lax.fori_loop(0, length // 256, one, 0)


def wrap(ref, length):
    ref[length // 8 : length // 8 + EXTRA] = ref[0:EXTRA]


def rotate_into(source, target, buffer, shift):
    length, width = source.shape
    buffer[0 : length // 8] = source[...].astype(FULL).reshape(length // 8, 8, width)
    wrap(buffer, length)

    def put(index, block):
        target[rows_at(index * 256, 256, 256), :] = block.astype(LOW)

    rotate(buffer, shift, length, put)


def forward_kernel(
    rows_of,
    keys_of,
    head_count,
    spans,
    q_ref,
    k_ref,
    v_ref,
    cot_ref,
    wo_ref,
    mixed_ref,
    mixed_rot_ref,
    log_ref,
    cot_all,
    wo_all,
    q_rot,
    k_rot,
    v_rot,
    v_heads,
    buffer,
    cot_sems,
    wo_sems,
    local_sems,
):
    length, width = q_ref.shape
    team = Team()
    spreads = (
        Spread(team, wo_ref, wo_all, wo_sems, local_sems.at[0]),
        Spread(team, cot_ref, cot_all, cot_sems, local_sems.at[1]),
    )
    team.greet((team.sibling, team.far))
    for spread in spreads:
        spread.start()
    small = length - LONGEST
    offset, border = spans[0], spans[1]

    rotate_into(q_ref, q_rot, buffer, offset)
    rotate_into(k_ref, k_rot, buffer, offset)
    rotate_into(v_ref, v_rot, buffer, offset)
    v_all = v_rot[...]
    for head in range(head_count):
        v_heads[head] = jnp.concatenate(
            [keep_head(head, v_all), jnp.full((length, 256 - width), 1, jnp.bfloat16)], axis=1
        )

    def block(row, key_base, key_count, masked):
        rows = pl.ds(row, rows_of)
        total = jnp.zeros((rows_of, width), jnp.float32)
        logs = []
        for head in range(head_count):
            q_head = keep_head(head, q_rot[rows, :])
            top, parts = None, []
            for chunk in range(key_count // keys_of):
                keys = pl.ds(key_base + chunk * keys_of, keys_of)
                scores = dot(q_head, k_rot[keys, :], NT)
                if masked:
                    shape = (rows_of, keys_of)
                    row_id = lax.broadcasted_iota(jnp.int32, shape, 0) + (row - LONGEST)
                    key_id = lax.broadcasted_iota(jnp.int32, shape, 1) + chunk * keys_of
                    scores = jnp.where((row_id < border) == (key_id < border), scores, -1e30)
                high = jnp.max(scores, axis=1, keepdims=True)
                top = high if top is None else jnp.maximum(top, high)
                parts.append(scores)
            summed = jnp.zeros((rows_of, 256), jnp.float32)
            for chunk, scores in enumerate(parts):
                keys = pl.ds(key_base + chunk * keys_of, keys_of)
                weights = jnp.exp2((scores - top) * LOG_SCALE).astype(jnp.bfloat16)
                summed = summed + dot(weights, v_heads[head, keys, :], NN)
            norm = summed[:, 255:256]
            total = total + summed[:, :width] * (1.0 / norm)
            logs.append(top * LOG_SCALE + jnp.log2(norm))
        mixed_rot_ref[pl.ds(lax.div(row, 8), rows_of // 8)] = total.reshape(rows_of // 8, 8, width)
        logs.append(jnp.zeros((rows_of, 128 - head_count), jnp.float32))
        log_ref[rows, :] = jnp.concatenate(logs, axis=1)

    def large(index, nothing):
        block(pl.multiple_of(index * rows_of, rows_of), 0, LONGEST, False)
        return nothing

    def little(index, nothing):
        block(pl.multiple_of(LONGEST + index * rows_of, rows_of), LONGEST, small, True)
        return nothing

    lax.fori_loop(0, LONGEST // rows_of, large, 0)
    for spread in spreads:
        spread.middle()
    lax.fori_loop(0, small // rows_of, little, 0)
    for spread in spreads:
        spread.finish()
    wrap(mixed_rot_ref, length)

    def put(index, block_rows):
        mixed_ref[rows_at(index * 256, 256, 256), :] = block_rows.astype(LOW)

    rotate(mixed_rot_ref, length - offset, length, put)


def attend_forward(spans, queries, key_rows, value_rows, cotangent, out_weight):
    length, width = queries.shape
    head_count = width // HEAD
    return pl.pallas_call(
        functools.partial(forward_kernel, 512, 512, head_count),
        out_shape=(
            jax.ShapeDtypeStruct((length, width), jnp.bfloat16),
            jax.ShapeDtypeStruct((length // 8 + EXTRA, 8, width), jnp.float32),
            jax.ShapeDtypeStruct((length, 128), jnp.float32),
            jax.ShapeDtypeStruct((length, cotangent.shape[1]), LOW),
            jax.ShapeDtypeStruct((4 * out_weight.shape[0], out_weight.shape[1]), LOW),
            jax.ShapeDtypeStruct((length, width), LOW),
            jax.ShapeDtypeStruct((length, width), LOW),
            jax.ShapeDtypeStruct((length, width), LOW),
        ),
        in_specs=[SMEM, VMEM, VMEM, VMEM, VMEM, VMEM],
        out_specs=(VMEM, VMEM, VMEM, ANY, ANY, VMEM, VMEM, VMEM),
        scratch_shapes=[
            pltpu.VMEM((head_count, length, 256), jnp.bfloat16),
            pltpu.VMEM((length // 8 + EXTRA, 8, width), FULL),
            DMA((6,)),
            DMA((6,)),
            DMA((2,)),
        ],
        compiler_params=pltpu.CompilerParams(
            collective_id=1, has_side_effects=True, vmem_limit_bytes=60 << 20
        ),
        name="attend_forward",
    )(spans, queries, key_rows, value_rows, cotangent, out_weight)


class Plane:
    def __init__(self, size):
        self.me, self.lane = lax.axis_index("dp"), lax.axis_index("seq")
        self.bits = size.bit_length() - 1

    def partner(self, bit):
        return (flip(self.me, bit), self.lane)

    def digit(self, bit):
        return lax.rem(lax.div(self.me, 1 << bit), 2)


class Total:
    def __init__(self, plane, source, wire, part, sends, receives, sems):
        self.plane, self.source, self.wire, self.part = plane, source, wire, part
        self.sends, self.receives, self.sems = sends, receives, sems
        self.halvings, self.whole = halvings_of(plane.bits)
        self.stages = 2 * self.halvings + self.whole
        rows = source.shape[0]
        self.bases, self.sizes = [0], [rows]
        for bit in range(self.halvings):
            half = self.sizes[-1] // 2
            self.bases.append(self.bases[-1] + plane.digit(bit) * half)
            self.sizes.append(half)
        self.step = rows >> self.halvings

    def place(self, level):
        return rows_at(self.bases[level], self.sizes[level], self.step)

    def inner(self, level):
        return rows_at(self.bases[level] - self.bases[1], self.sizes[level], self.step)

    def remote(self, source, target, stage, bit):
        return pltpu.make_async_remote_copy(
            src_ref=source,
            dst_ref=target,
            send_sem=self.sems.at[0, stage],
            recv_sem=self.sems.at[1, stage],
            device_id=self.plane.partner(bit),
            device_id_type=MESH,
        )

    def other(self, stage):
        half = self.sizes[stage + 1]
        return self.bases[stage] + (1 - self.plane.digit(stage)) * half, half

    def copy_of(self, stage):
        if stage == 0:
            start, half = self.other(0)
            return self.remote(self.source.at[rows_at(start, half, self.step)], self.receives[0], 0, 0)
        if stage < self.halvings + self.whole:
            return self.remote(self.sends[stage - 1], self.receives[stage], stage, stage)
        bit = 2 * self.halvings + self.whole - 1 - stage
        here = self.wire.at[self.place(bit + 1)]
        return self.remote(here, here, stage, bit)

    def start(self, stage):
        if 0 < stage < self.halvings:
            start, half = self.other(stage)
            rows = rows_at(start - self.bases[1], half, self.step)
            self.sends[stage - 1][...] = self.part[rows, :].astype(LOW)
        elif self.halvings <= stage < self.halvings + self.whole:
            self.sends[stage - 1][...] = self.part[self.inner(self.halvings), :].astype(LOW)
        elif stage == self.halvings + self.whole:
            self.wire[self.place(self.halvings), :] = self.part[self.inner(self.halvings), :].astype(LOW)
        self.copy_of(stage).start()

    def finish(self, stage):
        self.copy_of(stage).wait()
        if stage == 0:
            self.part[...] = self.source[self.place(1), :].astype(FULL) + self.receives[0][...].astype(FULL)
        elif stage < self.halvings:
            self.part[self.inner(stage + 1), :] += self.receives[stage][...].astype(FULL)
        elif stage < self.halvings + self.whole:
            value = self.sends[stage - 1][...].astype(FULL) + self.receives[stage][...].astype(FULL)
            self.part[self.inner(self.halvings), :] = value


def halvings_of(bits):
    halvings = min(bits, 3)
    return halvings, bits - halvings


def total_scratch(size, rows, width):
    bits = size.bit_length() - 1
    halvings, whole = halvings_of(bits)
    shapes = [(rows >> (stage + 1), width) for stage in range(halvings)] + [(rows >> halvings, width)] * whole
    kinds = [pltpu.VMEM(dims, LOW) for dims in shapes]
    return [pltpu.VMEM((rows // 2, width), FULL), kinds[1:], kinds, DMA((2, halvings + bits))]


class Schedule:
    def __init__(self, totals):
        self.totals = totals
        self.count = len(totals) - 1 + totals[0].stages

    def active(self, time):
        return [
            (total, time - index) for index, total in enumerate(self.totals) if 0 <= time - index < total.stages
        ]

    def start(self, time):
        for total, stage in self.active(time):
            total.start(stage)

    def finish(self, time):
        for total, stage in self.active(time):
            total.finish(stage)

    def step(self, time):
        if time > 0:
            self.finish(time - 1)
        self.start(time)


def greet_all(team, plane):
    barrier = pltpu.get_barrier_semaphore()
    others = [plane.partner(bit) for bit in range(plane.bits)]
    others += [team.device(team.sibling), team.device(team.far)]
    for other in others:
        pl.semaphore_signal(barrier, inc=1, device_id=other, device_id_type=MESH)
    pl.semaphore_wait(barrier, len(others))
    return others


def backward_kernel(
    keys_of,
    rows_of,
    head_count,
    size,
    spans,
    q_rot,
    k_rot,
    v_rot,
    d_ref,
    mixed_rot_ref,
    log_ref,
    up_part,
    down_part,
    wo_part,
    out_far,
    dq_ref,
    dk_ref,
    dv_ref,
    up_sum,
    down_sum,
    wo_sum,
    out_in,
    d_rot,
    q_turned,
    d_turned,
    k_turned,
    q_heads,
    d_heads,
    dq_turned,
    dk_rot,
    dv_rot,
    log_rows,
    deltas,
    wires,
    total_parts,
    wo_near,
    wo_far,
    wo_sems,
    out_sems,
    keep_sems,
    dq_side,
):
    length, width = q_rot.shape
    small = length - LONGEST
    offset, border = spans[0], spans[1]
    low, full = jnp.bfloat16, jnp.float32
    team, plane = Team(), Plane(size)
    columns = wo_sum.shape[0]
    half = up_part.shape[0] // 2
    totals = []
    for index, source in enumerate((up_part, up_part, down_part, down_part)):
        rows = pl.ds((index % 2) * half, half)
        totals.append(Total(plane, source.at[rows], wires.at[index], *total_parts[index]))
    schedule = Schedule(totals)
    greet_all(team, plane)
    schedule.step(0)
    out_copy = team.copy(out_far, out_in, out_sems.at[0], out_sems.at[1], team.far)
    out_copy.start()

    def wo_rows(owner):
        return rows_at(owner * columns, columns, 64)

    wo_copies = [
        team.copy(wo_part.at[wo_rows(owner)], wo_near.at[slot], wo_sems.at[0, slot], wo_sems.at[1, slot], team.sibling)
        for slot, owner in enumerate((team.sibling, team.diagonal))
    ]
    for copy in wo_copies:
        copy.start()
    wo_across = team.copy(wo_far.at[0], wo_far.at[1], wo_sems.at[0, 2], wo_sems.at[1, 2], team.far)

    rotate_into(d_ref, d_rot, dq_turned, offset)
    q_all, k_all, d_all = q_rot[...], k_rot[...], d_rot[...]
    q_turned[...] = jnp.transpose(q_all)
    k_turned[...] = jnp.transpose(k_all)
    d_turned[...] = jnp.transpose(d_all)
    for head in range(head_count):
        q_heads[head] = keep_head(head, q_all)
        d_heads[head] = keep_head(head, d_all)
    products = jnp.transpose(d_all.astype(full) * mixed_rot_ref[0 : length // 8].reshape(length, width))
    for head in range(head_count):
        deltas[head : head + 1, :] = jnp.sum(products[head * HEAD : (head + 1) * HEAD, :], axis=0, keepdims=True)
    log_rows[...] = jnp.transpose(log_ref[...])[0:8, :]
    dq_side[...] = jnp.zeros_like(dq_side)

    def block(key_row, row_base, row_count, masked):
        keys = pl.ds(key_row, keys_of)
        dk_sum = jnp.zeros((keys_of, width), full)
        dv_sum = jnp.zeros((keys_of, width), full)
        for head in range(head_count):
            k_head = keep_head(head, k_rot[keys, :])
            v_head = keep_head(head, v_rot[keys, :])
            lanes = slice(head * HEAD, (head + 1) * HEAD)
            k_side = k_turned[lanes, keys]
            for chunk in range(row_count // rows_of):
                start = row_base + chunk * rows_of
                rows = slice(start, start + rows_of)
                scores = dot(k_head, q_turned[:, rows], NN)
                dprobs = dot(v_head, d_turned[:, rows], NN)
                probs = jnp.exp2(scores * LOG_SCALE - log_rows[head : head + 1, rows])
                if masked:
                    shape = (keys_of, rows_of)
                    key_id = lax.broadcasted_iota(jnp.int32, shape, 0) + (key_row - LONGEST)
                    row_id = lax.broadcasted_iota(jnp.int32, shape, 1) + chunk * rows_of
                    probs = jnp.where((row_id < border) == (key_id < border), probs, 0.0)
                dv_sum = dv_sum + dot(probs.astype(low), d_heads[head, rows, :], NN)
                draw = (probs * (dprobs - deltas[head : head + 1, rows])).astype(low)
                dk_sum = dk_sum + dot(draw, q_heads[head, rows, :], NN)
                dq_side[lanes, rows] += dot(k_side, draw, NN)
        groups = pl.ds(lax.div(key_row, 8), keys_of // 8)
        dk_rot[groups] = (dk_sum * SCALE).reshape(keys_of // 8, 8, width)
        dv_rot[groups] = dv_sum.reshape(keys_of // 8, 8, width)

    def large(index, nothing):
        for time in range(1, schedule.count):

            @pl.when(index == time - 1)
            def _(time=time):
                schedule.step(time)
                if time == 1:
                    for copy in wo_copies:
                        copy.wait()
                    wo_far[0] = (wo_part[wo_rows(team.far), :].astype(full) + wo_near[1].astype(full)).astype(low)
                    wo_across.start()

        block(pl.multiple_of(index * keys_of, keys_of), 0, LONGEST, False)
        return nothing

    def little(index, nothing):
        block(pl.multiple_of(LONGEST + index * keys_of, keys_of), LONGEST, small, True)
        return nothing

    trips = LONGEST // keys_of
    lax.fori_loop(0, trips, large, 0)
    for time in range(trips + 1, schedule.count):
        schedule.step(time)
    lax.fori_loop(0, small // keys_of, little, 0)

    def unrotate(buffer, target):
        wrap(buffer, length)

        def put(index, block_rows):
            target[rows_at(index * 256, 256, 256), :] = block_rows.astype(low)

        rotate(buffer, length - offset, length, put)

    unrotate(dk_rot, dk_ref)
    unrotate(dv_rot, dv_ref)
    dq_turned[0 : length // 8] = jnp.transpose(dq_side[...] * SCALE).reshape(length // 8, 8, width)
    unrotate(dq_turned, dq_ref)
    schedule.finish(schedule.count - 1)
    keeps = []
    for index, target in enumerate((up_sum, up_sum, down_sum, down_sum)):
        rows = pl.ds((index % 2) * half, half)
        keeps.append(pltpu.make_async_copy(wires.at[index], target.at[rows], keep_sems.at[index]))
    for keep in keeps:
        keep.start()
    wo_across.wait()
    mine = wo_part[wo_rows(team.me), :].astype(full) + wo_near[0].astype(full)
    wo_sum[...] = (mine + wo_far[1].astype(full)).astype(low)
    out_copy.wait()
    for keep in keeps:
        keep.wait()


def attend_backward(
    size, spans, q_rot, k_rot, v_rot, grad_mixed, mixed_rot, log_totals, up_part, down_part, wo_part, out_far
):
    length, width = q_rot.shape
    head_count = width // HEAD
    low, full = jnp.bfloat16, jnp.float32
    half = (up_part.shape[0] // 2, up_part.shape[1])
    wo_shape = (wo_part.shape[0] // 4, wo_part.shape[1])

    def shape(dims):
        return jax.ShapeDtypeStruct(dims, low)

    grouped = (length // 8 + EXTRA, 8, width)
    return pl.pallas_call(
        functools.partial(backward_kernel, 256, 512, head_count, size),
        out_shape=(shape((length, width)),) * 3
        + (shape(up_part.shape), shape(down_part.shape), shape(wo_shape), shape(out_far.shape)),
        in_specs=[SMEM] + [VMEM] * 9 + [ANY],
        out_specs=(VMEM,) * 3 + (ANY, ANY, VMEM, ANY),
        scratch_shapes=[
            pltpu.VMEM((length, width), low),
            pltpu.VMEM((width, length), low),
            pltpu.VMEM((width, length), low),
            pltpu.VMEM((width, length), low),
            pltpu.VMEM((head_count, length, width), low),
            pltpu.VMEM((head_count, length, width), low),
            pltpu.VMEM(grouped, full),
            pltpu.VMEM(grouped, full),
            pltpu.VMEM(grouped, full),
            pltpu.VMEM((8, length), full),
            pltpu.VMEM((8, length), full),
            pltpu.VMEM((4, *half), low),
            [total_scratch(size, *half) for unused in range(4)],
            pltpu.VMEM((2, *wo_shape), low),
            pltpu.VMEM((2, *wo_shape), low),
            DMA((2, 3)),
            DMA((2,)),
            DMA((4,)),
            pltpu.VMEM((width, length), full),
        ],
        compiler_params=pltpu.CompilerParams(
            collective_id=3, has_side_effects=True, vmem_limit_bytes=63 << 20
        ),
        name="attend_backward",
    )(spans, q_rot, k_rot, v_rot, grad_mixed, mixed_rot, log_totals, up_part, down_part, wo_part, out_far)


def project_kernel(
    part,
    x_ref,
    gain,
    shift,
    wq,
    bq,
    wk,
    wv,
    bv,
    x_all,
    normed,
    q_ref,
    k_ref,
    v_ref,
    landing,
    far_send,
    far_recv,
    near_send,
    near_recv,
    pass_send,
    pass_recv,
    keep_sem,
):
    team = Team()
    own = x_ref.shape[0]
    count = own // part

    def piece(owner, index):
        return rows_at(owner * own + index * part, part, part)

    def far_copy(index):
        source = x_ref.at[rows_at(index * part, part, part)]
        return team.copy(
            source, landing.at[piece(team.me, index)], far_send.at[index], far_recv.at[index], team.far
        )

    def pass_copy(index):
        place = landing.at[piece(team.far, index)]
        return team.copy(place, place, pass_send.at[index], pass_recv.at[index], team.sibling)

    near = team.copy(
        x_ref, landing.at[rows_at(team.me * own, own, own)], near_send, near_recv, team.sibling
    )

    def keep(owner, source, slot):
        return pltpu.make_async_copy(source, x_all.at[rows_at(owner * own, own, own)], keep_sem.at[slot])

    team.greet((team.sibling, team.far))
    for index in range(count):
        far_copy(index).start()
    near.start()
    keep(team.me, x_ref, 0).start()

    def project(owner, index, values):
        standard, unused = standardize(values.astype(FULL))
        low = (standard * gain[...].astype(FULL) + shift[...].astype(FULL)).astype(LOW)
        rows = piece(owner, index)
        normed[rows, :] = low
        q_ref[rows, :] = (dot(low, wq[...], NT) + bq[...].astype(FULL)).astype(LOW)
        k_ref[rows, :] = dot(low, wk[...], NT).astype(LOW)
        v_ref[rows, :] = (dot(low, wv[...], NT) + bv[...].astype(FULL)).astype(LOW)

    def mine(index, nothing):
        project(team.me, index, x_ref[rows_at(index * part, part, part), :])
        return nothing

    lax.fori_loop(0, count, mine, 0)
    near.wait()

    def next_to(index, nothing):
        project(team.sibling, index, landing[piece(team.sibling, index), :])
        return nothing

    lax.fori_loop(0, count, next_to, 0)

    def across(index, nothing):
        far_copy(index).wait_recv()
        pass_copy(index).start()
        project(team.far, index, landing[piece(team.far, index), :])
        pass_copy(index).wait_recv()
        project(team.diagonal, index, landing[piece(team.diagonal, index), :])
        return nothing

    lax.fori_loop(0, count, across, 0)
    for slot, owner in ((1, team.sibling), (2, team.far), (3, team.diagonal)):
        keep(owner, landing.at[rows_at(owner * own, own, own)], slot).start()
    for slot, owner in ((1, team.sibling), (2, team.far), (3, team.diagonal)):
        keep(owner, landing.at[rows_at(owner * own, own, own)], slot).wait()
    keep(team.me, x_ref, 0).wait()
    for index in range(count):
        far_copy(index).wait_send()
        pass_copy(index).wait_send()


def gather_and_project(x, gain, shift, wq, bq, wk, wv, bv):
    own, width = x.shape
    length, columns, part = 4 * own, wq.shape[0], 128
    count = own // part
    narrow = jax.ShapeDtypeStruct((length, columns), LOW)
    wide = jax.ShapeDtypeStruct((length, width), LOW)
    return pl.pallas_call(
        functools.partial(project_kernel, part),
        out_shape=(wide, wide, narrow, narrow, narrow),
        in_specs=[VMEM] * 8,
        out_specs=(ANY, VMEM, VMEM, VMEM, VMEM),
        scratch_shapes=[
            pltpu.VMEM((length, width), LOW),
            DMA((count,)),
            DMA((count,)),
            DMA,
            DMA,
            DMA((count,)),
            DMA((count,)),
            DMA((4,)),
        ],
        compiler_params=pltpu.CompilerParams(
            collective_id=0, has_side_effects=True, vmem_limit_bytes=48 << 20
        ),
        name="gather_and_project",
    )(x, gain, shift, wq, bq, wk, wv, bv)


class Reduction:
    def __init__(self, team, near_out, near_in, far_out, far_in, sems):
        self.team = team
        self.near_out, self.near_in, self.far_out, self.far_in = near_out, near_in, far_out, far_in
        self.sems = sems

    def near(self, pair):
        return self.team.copy(
            self.near_out.at[pair],
            self.near_in.at[pair],
            self.sems.at[0, pair],
            self.sems.at[1, pair],
            self.team.sibling,
        )

    def across(self, pair):
        return self.team.copy(
            self.far_out.at[pair], self.far_in.at[pair], self.sems.at[2, pair], self.sems.at[3, pair], self.team.far
        )

    def give(self, pair, values):
        self.near_out[pair] = values.astype(LOW)
        self.near(pair).start()

    def combine(self, pair, values):
        self.near(pair).wait_recv()
        return values + self.near_in[pair].astype(FULL)

    def send(self, pair, values):
        self.far_out[pair] = values.astype(LOW)
        self.across(pair).start()

    def arrived(self, pair):
        self.across(pair).wait_recv()
        return self.far_in[pair].astype(FULL)

    def finish(self, pairs):
        for pair in range(pairs):
            self.near(pair).wait_send()
            if pair < pairs // 2:
                self.across(pair).wait_send()


def owner_at(team_me, step):
    half = lax.div(step, 4)
    odd = lax.rem(step, 2)
    one = flip(team_me, 0)
    base = one + odd * (team_me - one)
    return lax.rem(base + 2 * (1 - half), 4)


def part_at(step):
    return lax.rem(lax.div(step, 2), 2)


def ffn_kernel(
    part,
    mixed_ref,
    x_all,
    cot_all,
    wo,
    up,
    down,
    up_bias,
    out_bias,
    gain,
    shift,
    down_bias,
    out_far,
    out_own,
    grad_middle,
    grad_mixed,
    grad_up,
    grad_down,
    grad_wo,
    sums,
    middle_own,
    pieces,
    normed_all,
    hidden_all,
    gpre_all,
    out_slots,
    out_near,
    own_sum,
    near_out,
    near_in,
    far_out,
    far_in,
    mixed_out,
    far_sems,
    near_sems,
    pass_sems,
    slot_sems,
    red_sems,
    a2a_sems,
):
    team = Team()
    length = mixed_ref.shape[0]
    width = x_all.shape[1]
    columns = mixed_ref.shape[1]
    own = length // 4
    steps = length // part

    def rows_of(owner, index):
        return rows_at(owner * own + index * part, part, part)

    def step_rows(device, step):
        return rows_of(owner_at(device, step), part_at(step))

    def far_copy(step):
        rows = step_rows(team.far, step)
        return team.copy(
            mixed_ref.at[rows], pieces.at[1, rows], far_sems.at[0, step], far_sems.at[1, step], team.far
        )

    def near_copy(step):
        rows = step_rows(team.sibling, step)
        return team.copy(
            mixed_ref.at[rows], pieces.at[0, rows], near_sems.at[0, step], near_sems.at[1, step], team.sibling
        )

    def pass_copy(step):
        rows = step_rows(team.me, step)
        other = step + 1 - 2 * lax.rem(step, 2)
        return team.copy(
            pieces.at[1, rows], pieces.at[2, rows], pass_sems.at[0, step], pass_sems.at[1, other], team.sibling
        )

    def pass_arrival(step):
        rows = step_rows(team.me, step)
        return team.copy(
            pieces.at[1, rows], pieces.at[2, rows], pass_sems.at[0, step], pass_sems.at[1, step], team.sibling
        )

    reduction = Reduction(team, near_out, near_in, far_out, far_in, red_sems)

    def slot_copy(pair):
        slot = lax.rem(pair, 2)
        return team.copy(
            out_slots.at[slot], out_near.at[pair], slot_sems.at[0, slot], slot_sems.at[1, pair], team.sibling
        )

    team.greet((team.sibling, team.far, team.diagonal))

    def begin(step, nothing):
        far_copy(step).start()
        near_copy(step).start()
        return nothing

    lax.fori_loop(0, steps, begin, 0)
    sums[...] = jnp.zeros_like(sums)
    gain_row, shift_row = gain[...].astype(FULL), shift[...].astype(FULL)
    bias_row, up_row = out_bias[...].astype(FULL), up_bias[...].astype(FULL)
    down_row = down_bias[...].astype(FULL)

    def compute(step, keep_middle):
        rows = step_rows(team.me, step)

        def weights(owner):
            return wo[rows_at(owner * columns, columns, 64), :]

        branch = dot(mixed_ref[rows, :], weights(team.me), NN)
        branch = branch + dot(pieces[0, rows, :], weights(team.sibling), NN)
        branch = branch + dot(pieces[1, rows, :], weights(team.far), NN)
        branch = branch + dot(pieces[2, rows, :], weights(team.diagonal), NN)
        middle = x_all[rows, :].astype(FULL) + (branch + bias_row)
        if keep_middle:

            @pl.when(step >= steps // 2)
            def _():
                middle_own[rows_at(part_at(step) * part, part, part), :] = middle

        standard, unused = standardize(middle)
        low = (standard * gain_row + shift_row).astype(LOW)
        normed_all[rows, :] = low
        pre = dot(low, up[...], NN) + up_row
        bell = 0.5 * (1.0 + lax.erf(pre * 0.7071067811865476))
        hidden = (pre * bell).astype(LOW)
        hidden_all[rows, :] = hidden
        slope = bell + pre * (jnp.exp(pre * pre * -0.5) * 0.3989422804014327)

        out = dot(hidden, down[...], NN)
        pair = lax.div(step, 2)
        if keep_middle:
            slot_copy(pair).wait_recv()
            out = out + out_near[pair].astype(FULL)
            place = rows_at(part_at(step) * part, part, part)

            @pl.when(step < steps // 2)
            def _():
                out_far[place, :] = out.astype(LOW)

            @pl.when(step >= steps // 2)
            def _():
                out_own[place, :] = middle + out + down_row
        else:

            @pl.when(pair >= 2)
            def _():
                slot_copy(pair - 2).wait_send()

            out_slots[lax.rem(pair, 2)] = out.astype(LOW)
            slot_copy(pair).start()
        grad_pre = (dot(cot_all[rows, :], down[...], NT) * slope).astype(LOW)
        gpre_all[rows, :] = grad_pre
        sums[4:5, :] += column_sums(grad_pre.astype(FULL))
        return dot(grad_pre, up[...], NT)

    def pair_step(pair, nothing):
        first, second = 2 * pair, 2 * pair + 1
        for step in (first, second):
            far_copy(step).wait_recv()
            pass_copy(step).start()
            near_copy(step).wait_recv()
        pass_arrival(first).wait_recv()
        reduction.give(pair, compute(first, False))
        pass_arrival(second).wait_recv()
        values = reduction.combine(pair, compute(second, True))

        @pl.when(pair < steps // 4)
        def _():
            reduction.send(pair, values)

        @pl.when(pair >= steps // 4)
        def _():
            own_sum[rows_at(part_at(second) * part, part, part), :] = values

        return nothing

    lax.fori_loop(0, steps // 2, pair_step, 0)
    block = 256
    for start in range(0, width, block):
        lanes = slice(start, start + block)
        grad_up[lanes, :] = dot(normed_all[:, lanes], gpre_all[...], TN).astype(LOW)
        grad_down[lanes, :] = dot(hidden_all[:, lanes], cot_all[...], TN).astype(LOW)

    wo_sums = []
    for index in range(own // part):
        rows = pl.ds(index * part, part)
        grad = own_sum[rows, :] + reduction.arrived(index)
        standard, inverse = standardize(middle_own[rows, :])
        incoming = cot_all[rows_of(team.me, index), :].astype(FULL)
        grad_mid = incoming + norm_back(grad, gain_row, standard, inverse)
        grad_middle[rows, :] = grad_mid
        branch_low = grad_mid.astype(LOW)
        sums[0:1, :] += column_sums(grad * standard)
        sums[1:2, :] += column_sums(grad)
        sums[2:3, :] += column_sums(branch_low.astype(FULL))
        sums[3:4, :] += column_sums(incoming)
        for slot, owner in enumerate((team.sibling, team.far, team.diagonal)):
            side = wo[rows_at(owner * columns, columns, 64), :]
            mixed_out[slot, rows, :] = dot(branch_low, side, NT).astype(LOW)
        side = wo[rows_at(team.me * columns, columns, 64), :]
        grad_mixed[rows_of(team.me, index), :] = dot(branch_low, side, NT).astype(LOW)
        own_rows = rows_of(team.me, index)
        for source, owner in (
            (mixed_ref.at[own_rows], team.me),
            (pieces.at[0, own_rows], team.sibling),
            (pieces.at[1, own_rows], team.far),
            (pieces.at[2, own_rows], team.diagonal),
        ):
            place = rows_at(owner * columns, columns, 64)
            wo_sums.append((place, dot(source[...], branch_low, TN)))
    for slot in range(4):
        place = wo_sums[slot][0]
        grad_wo[place, :] = sum(value for unused, value in wo_sums[slot::4]).astype(LOW)

    here = grad_mixed.at[rows_at(team.me * own, own, own)]
    exchanges = [
        team.copy(mixed_out.at[slot], here, a2a_sems.at[0, slot], a2a_sems.at[1, slot], owner)
        for slot, owner in enumerate((team.sibling, team.far, team.diagonal))
    ]
    for exchange in exchanges:
        exchange.start()
    for exchange in exchanges:
        exchange.wait()

    def end(step, nothing):
        far_copy(step).wait_send()
        near_copy(step).wait_send()
        pass_copy(step).wait_send()
        return nothing

    lax.fori_loop(0, steps, end, 0)
    for pair in (steps // 2 - 2, steps // 2 - 1):
        slot_copy(pair).wait_send()
    reduction.finish(steps // 2)


def ffn(mixed, x_all, cot_all, wo, up, down, up_bias, out_bias, gain, shift, down_bias):
    length, columns = mixed.shape
    width = x_all.shape[1]
    hidden = up.shape[1]
    own, part = length // 4, 320
    steps = length // part
    pairs = steps // 2

    def shape(dims, kind):
        return jax.ShapeDtypeStruct(dims, kind)

    return pl.pallas_call(
        functools.partial(ffn_kernel, part),
        out_shape=(
            shape((own, width), LOW),
            shape((own, width), FULL),
            shape((own, width), FULL),
            shape((length, columns), LOW),
            shape((width, hidden), LOW),
            shape((hidden, width), LOW),
            shape((width, width), LOW),
            shape((8, width), FULL),
        ),
        in_specs=[VMEM] * 11,
        out_specs=(VMEM,) * 8,
        scratch_shapes=[
            pltpu.VMEM((own, width), FULL),
            pltpu.VMEM((3, length, columns), LOW),
            pltpu.VMEM((length, width), LOW),
            pltpu.VMEM((length, hidden), LOW),
            pltpu.VMEM((length, hidden), LOW),
            pltpu.VMEM((2, part, width), LOW),
            pltpu.VMEM((pairs, part, width), LOW),
            pltpu.VMEM((own, width), FULL),
            pltpu.VMEM((pairs, part, width), LOW),
            pltpu.VMEM((pairs, part, width), LOW),
            pltpu.VMEM((pairs // 2, part, width), LOW),
            pltpu.VMEM((pairs // 2, part, width), LOW),
            pltpu.VMEM((3, own, columns), LOW),
            DMA((2, steps)),
            DMA((2, steps)),
            DMA((2, steps)),
            DMA((2, pairs)),
            DMA((4, pairs)),
            DMA((2, 3)),
        ],
        compiler_params=pltpu.CompilerParams(
            collective_id=2, has_side_effects=True, vmem_limit_bytes=63 << 20
        ),
        name="ffn",
    )(mixed, x_all, cot_all, wo, up, down, up_bias, out_bias, gain, shift, down_bias)


def last_kernel(
    part,
    size,
    dq_ref,
    dk_ref,
    dv_ref,
    wq,
    wk,
    wv,
    normed_all,
    x_all,
    grad_middle,
    gain,
    wo_sum,
    wide,
    input_grad,
    grad_sum,
    vectors,
    own_grad,
    near_out,
    near_in,
    far_out,
    far_in,
    red_sems,
    sources,
    wires,
    total_parts,
    packed,
    packed_in,
    vec_sems,
    keep_sems,
):
    team, plane = Team(), Plane(size)
    length, columns = dq_ref.shape
    width = normed_all.shape[1]
    own = length // 4
    pairs = length // part // 2
    grads = Reduction(team, near_out, near_in, far_out, far_in, red_sems)
    slabs = sources.shape[0]
    lanes_of = width // slabs
    totals = [Total(plane, sources.at[slab], wires.at[slab], *total_parts[slab]) for slab in range(slabs)]
    schedule = Schedule(totals)
    others = greet_all(team, plane)
    for slab in range(slabs):
        lanes = slice(slab * lanes_of, (slab + 1) * lanes_of)
        for index, source in enumerate((dq_ref, dk_ref, dv_ref)):
            value = dot(source[...], normed_all[:, lanes], TN)
            sources[slab, index * columns : (index + 1) * columns, :] = value.astype(LOW)
        sources[slab, 3 * columns : 4 * columns, :] = wo_sum[:, lanes]
        if slab < 2:
            schedule.step(slab)
    gain_row = gain[...].astype(FULL)
    packed[...] = jnp.zeros_like(packed)
    packed[0:4, :] = wide[0:4, :]
    packed[8:9, :] = wide[4:5, :]
    packed[9:10, 0:columns] = column_sums(dq_ref[...].astype(FULL))
    packed[10:11, 0:columns] = column_sums(dv_ref[...].astype(FULL))

    def step_rows(step):
        return rows_at(owner_at(team.me, step) * own + part_at(step) * part, part, part)

    def compute(step):
        rows = step_rows(step)
        total = dot(dq_ref[rows, :], wq[...], NN) + dot(dk_ref[rows, :], wk[...], NN)
        return total + dot(dv_ref[rows, :], wv[...], NN)

    def pair_step(pair, nothing):
        first, second = 2 * pair, 2 * pair + 1
        grads.give(pair, compute(first))
        standard, unused = standardize(x_all[step_rows(second), :].astype(FULL))
        values = grads.combine(pair, compute(second))
        packed[4:5, :] += column_sums(values * standard)
        packed[5:6, :] += column_sums(values)

        @pl.when(pair < pairs // 2)
        def _():
            grads.send(pair, values)

        @pl.when(pair >= pairs // 2)
        def _():
            own_grad[rows_at(part_at(second) * part, part, part), :] = values

        @pl.when(pair == 1)
        def _():
            schedule.step(2)

        return nothing

    lax.fori_loop(0, pairs, pair_step, 0)

    def vector_copy(step):
        return pltpu.make_async_remote_copy(
            src_ref=packed.at[pl.ds(16 * step, 16)],
            dst_ref=packed_in.at[step],
            send_sem=vec_sems.at[0, step],
            recv_sem=vec_sems.at[1, step],
            device_id=others[step],
            device_id_type=MESH,
        )

    def finish_rows(index):
        rows = pl.ds(index * part, part)
        grad = own_grad[rows, :] + grads.arrived(index)
        standard, inverse = standardize(x_all[rows_at(team.me * own + index * part, part, part), :].astype(FULL))
        input_grad[rows, :] = grad_middle[rows, :] + norm_back(grad, gain_row, standard, inverse)

    begin = 3
    for time in range(begin, max(schedule.count, begin + len(others))):
        if time < schedule.count:
            schedule.step(time)
        step = time - begin
        if step < len(others):
            vector_copy(step).start()
            vector_copy(step).wait()
            here = packed[16 * step : 16 * (step + 1), :]
            keep = 16 if step < plane.bits else 8
            row = lax.broadcasted_iota(jnp.int32, here.shape, 0)
            added = here + jnp.where(row < keep, packed_in[step], 0.0)
            packed[16 * (step + 1) : 16 * (step + 2), :] = added
        if time - begin in (2, 4):
            finish_rows((time - begin) // 2 - 1)
    vectors[...] = packed[16 * len(others) : 16 * (len(others) + 1), :]
    schedule.finish(schedule.count - 1)
    keeps = []
    for slab in range(slabs):
        lanes = pl.ds(slab * lanes_of, lanes_of)
        keeps.append(pltpu.make_async_copy(wires.at[slab], grad_sum.at[:, lanes], keep_sems.at[slab]))
    for keep in keeps:
        keep.start()
    for keep in keeps:
        keep.wait()
    grads.finish(pairs)


def last(size, dq, dk, dv, wq, wk, wv, normed_all, x_all, grad_middle, gain, wo_sum, wide):
    length, columns = dq.shape
    own, width = grad_middle.shape
    part, slabs = 320, 3
    pairs = length // part // 2
    bits = size.bit_length() - 1
    slab = (4 * columns, width // slabs)

    def shape(dims, kind):
        return jax.ShapeDtypeStruct(dims, kind)

    return pl.pallas_call(
        functools.partial(last_kernel, part, size),
        out_shape=(
            shape((own, width), FULL),
            shape((4 * columns, width), LOW),
            shape((16, width), FULL),
        ),
        in_specs=[VMEM] * 12,
        out_specs=(VMEM, ANY, VMEM),
        scratch_shapes=[
            pltpu.VMEM((own, width), FULL),
            pltpu.VMEM((pairs, part, width), LOW),
            pltpu.VMEM((pairs, part, width), LOW),
            pltpu.VMEM((pairs // 2, part, width), LOW),
            pltpu.VMEM((pairs // 2, part, width), LOW),
            DMA((4, pairs)),
            pltpu.VMEM((slabs, *slab), LOW),
            pltpu.VMEM((slabs, *slab), LOW),
            [total_scratch(size, *slab) for unused in range(slabs)],
            pltpu.VMEM((16 * (bits + 3), width), FULL),
            pltpu.VMEM((bits + 2, 16, width), FULL),
            DMA((2, bits + 2)),
            DMA((slabs,)),
        ],
        compiler_params=pltpu.CompilerParams(
            collective_id=4, has_side_effects=True, vmem_limit_bytes=60 << 20
        ),
        name="last",
    )(dq, dk, dv, wq, wk, wv, normed_all, x_all, grad_middle, gain, wo_sum, wide)


def local(
    size,
    layer_input,
    segment_ids,
    cotangent,
    attn_gain,
    attn_shift,
    query_weight,
    query_bias,
    key_weight,
    value_weight,
    value_bias,
    out_weight,
    out_bias,
    ffn_gain,
    ffn_shift,
    up_weight,
    up_bias,
    down_weight,
    down_bias,
):
    def row(vector):
        return vector.reshape(1, -1)

    spans = rotation(segment_ids[0], LONGEST)
    query_side, key_side, value_side = query_weight.T, key_weight.T, value_weight.T
    x_all, normed_rows, queries, key_rows, value_rows = gather_and_project(
        layer_input,
        row(attn_gain),
        row(attn_shift),
        query_side,
        row(query_bias),
        key_side,
        value_side,
        row(value_bias),
    )
    mixed, mixed_rot, log_totals, cotangent_rows, out_all, q_rot, k_rot, v_rot = attend_forward(
        spans, queries, key_rows, value_rows, cotangent, out_weight
    )
    out_far, out_own, grad_middle, grad_mixed, up_part, down_part, out_part, sums = ffn(
        mixed,
        x_all,
        cotangent_rows,
        out_all,
        up_weight,
        down_weight,
        row(up_bias),
        row(out_bias),
        row(ffn_gain),
        row(ffn_shift),
        row(down_bias),
    )
    dq, dk, dv, grad_up, grad_down, wo_sum, out_in = attend_backward(
        size, spans, q_rot, k_rot, v_rot, grad_mixed, mixed_rot, log_totals, up_part, down_part, out_part, out_far
    )
    layer_output = (out_own + out_in.astype(FULL)).astype(LOW)
    input_grad, grads, vectors = last(
        size,
        dq,
        dk,
        dv,
        query_side,
        key_side,
        value_side,
        normed_rows,
        x_all,
        grad_middle,
        row(attn_gain),
        wo_sum,
        sums,
    )
    columns = query_side.shape[0]
    grads = grads.astype(FULL)
    return (
        layer_output,
        input_grad,
        vectors[4],
        vectors[5],
        grads[0:columns].T,
        vectors[9, 0:columns],
        grads[columns : 2 * columns].T,
        grads[2 * columns : 3 * columns].T,
        vectors[10, 0:columns],
        grads[3 * columns :],
        vectors[2],
        vectors[0],
        vectors[1],
        grad_up.astype(FULL),
        vectors[8],
        grad_down.astype(FULL),
        vectors[3],
    )


def solution(mesh):
    return jax.shard_map(
        functools.partial(local, mesh.shape["dp"]),
        mesh=mesh,
        in_specs=(
            P(("dp", "seq"), None),
            P("dp", None),
            P(("dp", "seq"), None),
            P(),
            P(),
            P(None, "seq"),
            P("seq"),
            P(None, "seq"),
            P(None, "seq"),
            P("seq"),
            P("seq", None),
            P(),
            P(),
            P(),
            P(None, "seq"),
            P("seq"),
            P("seq", None),
            P(),
        ),
        out_specs=(
            P(("dp", "seq"), None),
            P(("dp", "seq"), None),
            P(),
            P(),
            P(None, "seq"),
            P("seq"),
            P(None, "seq"),
            P(None, "seq"),
            P("seq"),
            P("seq", None),
            P(),
            P(),
            P(),
            P(None, "seq"),
            P("seq"),
            P("seq", None),
            P(),
        ),
        check_vma=False,
    )
```

```python
import functools

import jax
import jax.numpy as jnp
from jax import lax
from jax.experimental import pallas as pl
from jax.experimental.pallas import tpu as pltpu
from jax.sharding import PartitionSpec as P

HEAD = 64
SCALE = HEAD ** (-0.5)
LOG_SCALE = SCALE * 1.4426950408889634
LONGEST = 2048
EPSILON = 1e-06
NN = (((1,), (0,)), ((), ()))
NT = (((1,), (1,)), ((), ()))
TN = (((0,), (0,)), ((), ()))
MESH = pl.DeviceIdType.MESH
LOW = jnp.bfloat16
FULL = jnp.float32
VMEM = pl.BlockSpec(memory_space=pltpu.VMEM)
SMEM = pl.BlockSpec(memory_space=pltpu.SMEM)
ANY = pl.BlockSpec(memory_space=pl.ANY)
DMA = pltpu.SemaphoreType.DMA


def flip(index, bit):
    size = 1 << bit
    return index + size - 2 * size * lax.rem(lax.div(index, size), 2)


class Team:
    def __init__(self):
        self.row = lax.axis_index("dp")
        self.me = lax.axis_index("seq")
        self.sibling = flip(self.me, 0)
        self.far = flip(self.me, 1)
        self.diagonal = flip(self.sibling, 1)

    def device(self, index):
        return (self.row, index)

    def greet(self, others, *more):
        barrier = pltpu.get_barrier_semaphore()
        devices = [self.device(other) for other in others] + list(more)
        for device in devices:
            pl.semaphore_signal(barrier, inc=1, device_id=device, device_id_type=MESH)
        pl.semaphore_wait(barrier, len(devices))

    def copy(self, source, target, send, receive, other):
        return pltpu.make_async_remote_copy(
            src_ref=source,
            dst_ref=target,
            send_sem=send,
            recv_sem=receive,
            device_id=self.device(other),
            device_id_type=MESH,
        )


def rows_at(start, count, multiple):
    return pl.ds(pl.multiple_of(start, multiple), count)


def standardize(values):
    average = jnp.mean(values, axis=-1, keepdims=True)
    centered = values - average
    variance = jnp.mean(centered * centered, axis=-1, keepdims=True)
    inverse = lax.rsqrt(variance + EPSILON)
    return centered * inverse, inverse


def norm_back(grad, gain_row, standard, inverse):
    scaled = grad * gain_row
    mean_one = jnp.mean(scaled, axis=-1, keepdims=True)
    mean_two = jnp.mean(scaled * standard, axis=-1, keepdims=True)
    return inverse * (scaled - mean_one - standard * mean_two)


def column_sums(values):
    return jnp.sum(values, axis=0, keepdims=True)


def first_at_least(segments, value):
    length = segments.shape[1]

    def halve(unused, ends):
        low, high = ends
        middle = jnp.minimum(lax.div(low + high, 2), length - 1)
        below = segments[0, middle] < value
        open_yet = low < high
        return (
            jnp.where(open_yet & below, middle + 1, low),
            jnp.where(open_yet & jnp.logical_not(below), middle, high),
        )

    return lax.fori_loop(0, length.bit_length(), halve, (jnp.int32(0), jnp.int32(length)))[0]


def rotation(segments):
    length = segments.shape[1]
    one, two = first_at_least(segments, 1), first_at_least(segments, 2)
    offset = jnp.where(one == LONGEST, 0, jnp.where(two - one == LONGEST, one, two))
    border = jnp.where(one == LONGEST, two - one, jnp.where(two - one == LONGEST, length - two, one))
    return offset, border


def as_row(ref):
    return ref[...].astype(FULL).reshape(1, -1)


def dot(left_side, right_side, dims):
    return lax.dot_general(left_side, right_side, dims, preferred_element_type=jnp.float32)


def keep_head(head, values):
    lane = lax.broadcasted_iota(jnp.int32, values.shape, 1)
    inside = (lane >= head * HEAD) & (lane < (head + 1) * HEAD)
    return jnp.where(inside, values, jnp.zeros_like(values))


class Spread:
    def __init__(self, team, source, target, rows_of, sems):
        self.team, self.source, self.target, self.rows_of, self.sems = team, source, target, rows_of, sems

    def place(self, owner):
        return self.target.at[self.rows_of(owner)]

    def across(self):
        here = self.place(self.team.me)
        return self.team.copy(self.source, here, self.sems.at[0], self.sems.at[1], self.team.far)

    def near(self):
        here = self.place(self.team.me)
        return self.team.copy(self.source, here, self.sems.at[2], self.sems.at[3], self.team.sibling)

    def passed(self):
        there = self.place(self.team.far)
        return self.team.copy(there, there, self.sems.at[4], self.sems.at[5], self.team.sibling)

    def kept(self):
        return pltpu.make_async_copy(self.source, self.place(self.team.me), self.sems.at[6])

    def start(self):
        self.across().start()
        self.near().start()
        self.kept().start()

    def middle(self):
        self.across().wait_recv()
        self.passed().start()

    def sent(self):
        self.across().wait_send()
        self.near().wait_send()
        self.passed().wait_send()


EXTRA = 72


def rotated_block(ref, shift, length, index):
    width = ref.shape[2]
    sub = lax.broadcasted_iota(jnp.int32, (32, 8, width), 1)
    start = lax.rem(shift + index * 256, length)
    group = lax.div(start, 8)
    skip = start - group * 8
    turned = pltpu.roll(ref[pl.ds(group, 33)], lax.rem(8 - skip, 8), 1)
    return jnp.where(sub < 8 - skip, turned[:32], turned[1:]).reshape(256, width)


def rotate(ref, shift, length, put):
    def one(index, nothing):
        put(index, rotated_block(ref, shift, length, index))
        return nothing

    lax.fori_loop(0, length // 256, one, 0)


def wrap(ref, length):
    ref[length // 8 : length // 8 + EXTRA] = ref[0:EXTRA]


def rotate_into(source, target, buffer, shift):
    length, width = source.shape
    buffer[0 : length // 8] = source[...].astype(FULL).reshape(length // 8, 8, width)
    wrap(buffer, length)

    def put(index, block):
        target[rows_at(index * 256, 256, 256), :] = block.astype(LOW)

    rotate(buffer, shift, length, put)


def forward_kernel(
    rows_of,
    keys_of,
    head_count,
    spans,
    q_ref,
    k_ref,
    v_ref,
    wo_ref,
    mixed_ref,
    mixed_rot_ref,
    log_ref,
    pieces,
    wo_all,
    q_rot,
    k_rot,
    v_rot,
    v_heads,
    buffer,
    wo_sems,
    far_sems,
    near_sems,
    pass_sems,
):
    length, width = q_ref.shape
    team = Team()
    spread = Spread(team, wo_ref, wo_all, lambda owner: rows_at(owner * width, width, 64), wo_sems)

    def far_copy(index):
        rows = rows_at(index * 256, 256, 256)
        return team.copy(
            mixed_ref.at[rows], pieces.at[1, rows], far_sems.at[0, index], far_sems.at[1, index], team.far
        )

    def near_copy(index):
        rows = rows_at(index * 256, 256, 256)
        return team.copy(
            mixed_ref.at[rows], pieces.at[0, rows], near_sems.at[0, index], near_sems.at[1, index], team.sibling
        )

    def pass_copy(index):
        rows = rows_at(index * 256, 256, 256)
        return team.copy(
            pieces.at[1, rows], pieces.at[2, rows], pass_sems.at[0, index], pass_sems.at[1, index], team.sibling
        )

    team.greet((team.sibling, team.far))
    spread.start()
    small = length - LONGEST
    offset, border = rotation(spans)

    rotate_into(q_ref, q_rot, buffer, offset)
    rotate_into(k_ref, k_rot, buffer, offset)
    rotate_into(v_ref, v_rot, buffer, offset)
    v_all = v_rot[...]
    for head in range(head_count):
        v_heads[head] = jnp.concatenate(
            [keep_head(head, v_all), jnp.full((length, 256 - width), 1, jnp.bfloat16)], axis=1
        )

    def block(row, key_base, key_count, masked):
        rows = pl.ds(row, rows_of)
        total = jnp.zeros((rows_of, width), jnp.float32)
        logs = []
        for head in range(head_count):
            q_head = keep_head(head, q_rot[rows, :])
            top, parts = None, []
            for chunk in range(key_count // keys_of):
                keys = pl.ds(key_base + chunk * keys_of, keys_of)
                scores = dot(q_head, k_rot[keys, :], NT)
                if masked:
                    shape = (rows_of, keys_of)
                    row_id = lax.broadcasted_iota(jnp.int32, shape, 0) + (row - LONGEST)
                    key_id = lax.broadcasted_iota(jnp.int32, shape, 1) + chunk * keys_of
                    scores = jnp.where((row_id < border) == (key_id < border), scores, -1e30)
                high = jnp.max(scores, axis=1, keepdims=True)
                top = high if top is None else jnp.maximum(top, high)
                parts.append(scores)
            summed = jnp.zeros((rows_of, 256), jnp.float32)
            for chunk, scores in enumerate(parts):
                keys = pl.ds(key_base + chunk * keys_of, keys_of)
                weights = jnp.exp2((scores - top) * LOG_SCALE).astype(jnp.bfloat16)
                summed = summed + dot(weights, v_heads[head, keys, :], NN)
            norm = summed[:, 255:256]
            total = total + summed[:, :width] * (1.0 / norm)
            logs.append(top * LOG_SCALE + jnp.log2(norm))
        mixed_rot_ref[pl.ds(lax.div(row, 8), rows_of // 8)] = total.reshape(rows_of // 8, 8, width)
        logs.append(jnp.zeros((rows_of, 128 - head_count), jnp.float32))
        log_ref[rows, :] = jnp.concatenate(logs, axis=1)

    def send(index):
        rows = rows_at(index * 256, 256, 256)
        mixed_ref[rows, :] = rotated_block(mixed_rot_ref, length - offset, length, index).astype(LOW)
        far_copy(index).start()
        near_copy(index).start()

    def pass_on(index):
        far_copy(index).wait_recv()
        pass_copy(index).start()

    def little(index, nothing):
        block(pl.multiple_of(LONGEST + index * rows_of, rows_of), LONGEST, small, True)
        return nothing

    lax.fori_loop(0, small // rows_of, little, 0)
    lag, trips = 2, LONGEST // rows_of

    def large(index, nothing):
        block(pl.multiple_of(index * rows_of, rows_of), 0, LONGEST, False)

        @pl.when(index == 0)
        def _():
            mixed_rot_ref[length // 8 : length // 8 + 32] = mixed_rot_ref[0:32]

        send(index)

        @pl.when(index == trips // 2)
        def _():
            spread.middle()

        @pl.when(index >= lag)
        def _():
            pass_on(index - lag)

        return nothing

    lax.fori_loop(0, trips, large, 0)
    blocks = length // 256
    for index in range(trips, blocks):
        send(index)
    for index in range(trips - lag, blocks):
        pass_on(index)
    for index in range(blocks):
        near_copy(index).wait()
        far_copy(index).wait_send()
        pass_copy(index).wait()
    spread.sent()
    spread.near().wait_recv()
    spread.passed().wait_recv()
    spread.kept().wait()


def attend_forward(spans, queries, key_rows, value_rows, out_weight):
    length, width = queries.shape
    head_count = width // HEAD
    return pl.pallas_call(
        functools.partial(forward_kernel, 256, 512, head_count),
        out_shape=(
            jax.ShapeDtypeStruct((length, width), jnp.bfloat16),
            jax.ShapeDtypeStruct((length // 8 + EXTRA, 8, width), jnp.float32),
            jax.ShapeDtypeStruct((length, 128), jnp.float32),
            jax.ShapeDtypeStruct((3, length, width), LOW),
            jax.ShapeDtypeStruct((4 * out_weight.shape[0], out_weight.shape[1]), LOW),
            jax.ShapeDtypeStruct((length, width), LOW),
            jax.ShapeDtypeStruct((length, width), LOW),
            jax.ShapeDtypeStruct((length, width), LOW),
        ),
        in_specs=[SMEM, VMEM, VMEM, VMEM, VMEM],
        out_specs=(VMEM, VMEM, VMEM, ANY, ANY, VMEM, VMEM, VMEM),
        scratch_shapes=[
            pltpu.VMEM((head_count, length, 256), jnp.bfloat16),
            pltpu.VMEM((length // 8 + EXTRA, 8, width), FULL),
            DMA((7,)),
            DMA((2, length // 256)),
            DMA((2, length // 256)),
            DMA((2, length // 256)),
        ],
        compiler_params=pltpu.CompilerParams(
            collective_id=1, has_side_effects=True, vmem_limit_bytes=60 << 20
        ),
        name="attend_forward",
    )(spans, queries, key_rows, value_rows, out_weight)


class Plane:
    def __init__(self, size):
        self.me, self.lane = lax.axis_index("dp"), lax.axis_index("seq")
        self.size, self.bits = size, size.bit_length() - 1
        self.ranks = min(4, size // 2)
        self.side, self.rank = lax.rem(self.me, 2), lax.rem(lax.div(self.me, 2), self.ranks)
        self.extra = (size // 2 // self.ranks).bit_length() - 1

    def device(self, index):
        return (index, self.lane)

    def partner(self, bit):
        return self.device(flip(self.me, bit))

    def digit(self, bit):
        return lax.rem(lax.div(self.me, 1 << bit), 2)

    def other_rank(self, offset):
        return lax.rem(self.rank + offset, self.ranks)

    def ranked(self, offset):
        return self.device(self.me + 2 * (self.other_rank(offset) - self.rank))

    def remote(self, source, target, sems, index, device):
        return pltpu.make_async_remote_copy(
            src_ref=source,
            dst_ref=target,
            send_sem=sems.at[0, index],
            recv_sem=sems.at[1, index],
            device_id=device,
            device_id_type=MESH,
        )


class Halving:
    def __init__(self, plane, part, wire, first, sends, receives, sems):
        self.plane, self.part, self.wire, self.first = plane, part, wire, first
        self.sends, self.receives, self.sems = sends, receives, sems
        self.halvings, self.whole = halvings_of(plane.bits)
        self.stages = 2 * self.halvings + self.whole + 1
        half = part.shape[0]
        self.bases, self.sizes = [0], [half]
        for level in range(self.halvings):
            size = self.sizes[-1] // 2
            self.bases.append(self.bases[-1] + plane.digit(level + 1) * size)
            self.sizes.append(size)
        self.step = self.sizes[-1]
        self.shift = plane.side * half

    def inner(self, level):
        return rows_at(self.bases[level], self.sizes[level], self.step)

    def place(self, level):
        return rows_at(self.shift + self.bases[level], self.sizes[level], self.step)

    def copies(self, stage):
        plane = self.plane
        if stage < self.halvings + self.whole:
            return [
                plane.remote(self.sends[stage], self.receives[stage], self.sems, stage, plane.partner(stage + 1))
            ]
        level = 2 * self.halvings + self.whole - stage
        here = self.wire.at[self.place(level)]
        return [plane.remote(here, here, self.sems, stage, plane.partner(level))]

    def start(self, stage):
        if stage < self.halvings:
            size = self.sizes[stage + 1]
            first = self.bases[stage] + (1 - self.plane.digit(stage + 1)) * size
            self.sends[stage][...] = self.part[rows_at(first, size, self.step), :].astype(LOW)
        elif stage < self.halvings + self.whole:
            self.sends[stage][...] = self.part[self.inner(self.halvings), :].astype(LOW)
        elif stage == self.halvings + self.whole:
            self.wire[self.place(self.halvings), :] = self.part[self.inner(self.halvings), :].astype(LOW)
        for copy in self.copies(stage):
            copy.start()

    def finish(self, stage):
        for copy in self.copies(stage):
            copy.wait()
        if stage < self.halvings:
            self.part[self.inner(stage + 1), :] += self.receives[stage][...].astype(FULL)
        elif stage < self.halvings + self.whole:
            value = self.sends[stage][...].astype(FULL) + self.receives[stage][...].astype(FULL)
            self.part[self.inner(self.halvings), :] = value


def halvings_of(bits):
    halvings = min(bits - 1, 2)
    return halvings, bits - 1 - halvings


def halving_scratch(size, half, width):
    bits = size.bit_length() - 1
    halvings, whole = halvings_of(bits)
    shapes = [(half >> (stage + 1), width) for stage in range(halvings)] + [(half >> halvings, width)] * whole
    kinds = [pltpu.VMEM(dims, LOW) for dims in shapes]
    return [kinds, list(kinds), DMA((2, 2 * halvings + whole + 1))]


class Direct:
    first = 0

    def __init__(self, plane, source, wire, part, received, sends, receives, sems):
        self.plane, self.source, self.wire, self.part = plane, source, wire, part
        self.received, self.sends, self.receives, self.sems = received, sends, receives, sems
        self.half = source.shape[0] // 2
        self.piece = self.half // plane.ranks
        self.stages = 4 + plane.extra

    def side_rows(self, side):
        return rows_at(side * self.half, self.half, self.half)

    def rank_rows(self, rank):
        return rows_at(rank * self.piece, self.piece, self.piece)

    def own_rows(self):
        start = self.plane.side * self.half + self.plane.rank * self.piece
        return rows_at(start, self.piece, self.piece)

    def copies(self, stage):
        plane = self.plane
        if stage == 0:
            source = self.source.at[self.side_rows(1 - plane.side)]
            return [plane.remote(source, self.received, self.sems, 0, plane.partner(0))]
        if stage == self.stages - 1:
            here = self.wire.at[self.side_rows(plane.side)]
            return [plane.remote(here, here, self.sems, 1, plane.partner(0))]
        if 1 < stage < self.stages - 2:
            slot = plane.ranks + stage - 3
            index = 2 * plane.ranks + stage - 2
            device = plane.partner(plane.bits - plane.extra + stage - 2)
            return [plane.remote(self.sends.at[slot], self.receives.at[slot], self.sems, index, device)]
        copies = []
        for offset in range(1, plane.ranks):
            device = plane.ranked(offset)
            if stage == 1:
                slot = offset - 1
                copies.append(
                    plane.remote(self.sends.at[slot], self.receives.at[slot], self.sems, 1 + offset, device)
                )
            else:
                here = self.wire.at[self.own_rows()]
                copies.append(plane.remote(here, here, self.sems, plane.ranks + offset, device))
        return copies

    def start(self, stage):
        plane = self.plane
        if stage == 1:
            for offset in range(1, plane.ranks):
                rows = self.rank_rows(plane.other_rank(offset))
                self.sends[offset - 1] = self.part[rows, :].astype(LOW)
        elif 1 < stage < self.stages - 2:
            self.sends[plane.ranks + stage - 3] = self.part[self.rank_rows(plane.rank), :].astype(LOW)
        elif stage == self.stages - 2:
            self.wire[self.own_rows(), :] = self.part[self.rank_rows(plane.rank), :].astype(LOW)
        for copy in self.copies(stage):
            copy.start()

    def finish(self, stage):
        plane = self.plane
        for copy in self.copies(stage):
            copy.wait()
        if stage == 0:
            received = self.received[...].astype(FULL)
            self.part[...] = self.source[self.side_rows(plane.side), :].astype(FULL) + received
        elif stage == 1:
            value = self.part[self.rank_rows(plane.rank), :]
            for slot in range(plane.ranks - 1):
                value = value + self.receives[slot].astype(FULL)
            self.part[self.rank_rows(plane.rank), :] = value
        elif stage < self.stages - 2:
            slot = plane.ranks + stage - 3
            value = self.sends[slot].astype(FULL) + self.receives[slot].astype(FULL)
            self.part[self.rank_rows(plane.rank), :] = value


def direct_scratch(size, rows, width):
    ranks = min(4, size // 2)
    extra = (size // 2 // ranks).bit_length() - 1
    half = rows // 2
    pieces = pltpu.VMEM((ranks - 1 + extra, half // ranks, width), LOW)
    return [
        pltpu.VMEM((half, width), FULL),
        pltpu.VMEM((half, width), LOW),
        pieces,
        pieces,
        DMA((2, 2 * ranks + extra)),
    ]


class Events:
    def __init__(self, totals):
        self.totals = totals
        last = totals[0].stages - 1
        self.waiting = sorted(
            (2 * (stage - total.first) + index, index, stage)
            for index, total in enumerate(totals)
            for stage in range(total.first, last)
        )

    def start(self):
        for total in self.totals:
            total.start(total.first)

    def take(self, limit):
        ready = [event for event in self.waiting if event[0] < limit]
        self.waiting = [event for event in self.waiting if event[0] >= limit]
        for unused, index, stage in ready:
            self.totals[index].finish(stage)
            self.totals[index].start(stage + 1)

    def next(self, count):
        if self.waiting[:count]:
            self.take(self.waiting[min(count, len(self.waiting)) - 1][0] + 1)

    def end(self):
        self.take(1 << 20)
        for total in self.totals:
            total.finish(total.stages - 1)


def greet_all(team, plane, direct):
    barrier = pltpu.get_barrier_semaphore()
    others = [plane.partner(bit) for bit in range(plane.bits)]
    others += [team.device(team.sibling), team.device(team.far)]
    greeted = list(others)
    if direct:
        greeted = [plane.partner(0), team.device(team.sibling), team.device(team.far)]
        greeted += [plane.partner(plane.bits - plane.extra + index) for index in range(plane.extra)]
        greeted += [plane.ranked(offset) for offset in range(1, plane.ranks)]
    for other in greeted:
        pl.semaphore_signal(barrier, inc=1, device_id=other, device_id_type=MESH)
    pl.semaphore_wait(barrier, len(greeted))
    return others


def backward_kernel(
    keys_of,
    rows_of,
    head_count,
    size,
    spans,
    q_rot,
    k_rot,
    v_rot,
    d_ref,
    mixed_rot_ref,
    log_ref,
    up_part,
    down_part,
    wo_part,
    out_far,
    dq_ref,
    dk_ref,
    dv_ref,
    up_sum,
    down_sum,
    wo_sum,
    out_in,
    d_rot,
    q_turned,
    d_turned,
    k_turned,
    q_heads,
    d_heads,
    dq_turned,
    dk_rot,
    dv_rot,
    log_rows,
    deltas,
    parts,
    wires,
    total_parts,
    wo_near,
    wo_far,
    wo_sems,
    out_sems,
    keep_sems,
    dq_side,
):
    length, width = q_rot.shape
    small = length - LONGEST
    offset, border = rotation(spans)
    low, full = jnp.bfloat16, jnp.float32
    team, plane = Team(), Plane(size)
    columns = wo_sum.shape[0]
    lanes_of = up_part.shape[1] // 2
    totals, loads = [], []
    for index, source in enumerate((up_part, up_part, down_part, down_part)):
        lanes = pl.ds((index % 2) * lanes_of, lanes_of)
        total = Halving(plane, parts.at[index], wires.at[index], 1 + index // 2, *total_parts[index])
        place = parts.at[index, total.inner(1 + index // 2)]
        loads.append(pltpu.make_async_copy(source.at[:, lanes], place, keep_sems.at[index]))
        totals.append(total)
    for load in loads:
        load.start()
    events = Events(totals)
    greet_all(team, plane, False)
    for load in loads:
        load.wait()
    events.start()
    out_copy = team.copy(out_far, out_in, out_sems.at[0], out_sems.at[1], team.far)
    out_copy.start()

    def wo_rows(owner):
        return rows_at(owner * columns, columns, 64)

    wo_copies = [
        team.copy(wo_part.at[wo_rows(owner)], wo_near.at[slot], wo_sems.at[0, slot], wo_sems.at[1, slot], team.sibling)
        for slot, owner in enumerate((team.sibling, team.diagonal))
    ]
    for copy in wo_copies:
        copy.start()
    wo_across = team.copy(wo_far.at[0], wo_far.at[1], wo_sems.at[0, 2], wo_sems.at[1, 2], team.far)

    rotate_into(d_ref, d_rot, dq_turned, offset)
    q_all, k_all, d_all = q_rot[...], k_rot[...], d_rot[...]
    q_turned[...] = jnp.transpose(q_all)
    k_turned[...] = jnp.transpose(k_all)
    d_turned[...] = jnp.transpose(d_all)
    for head in range(head_count):
        q_heads[head] = keep_head(head, q_all)
        d_heads[head] = keep_head(head, d_all)
    products = jnp.transpose(d_all.astype(full) * mixed_rot_ref[0 : length // 8].reshape(length, width))
    for head in range(head_count):
        deltas[head : head + 1, :] = jnp.sum(products[head * HEAD : (head + 1) * HEAD, :], axis=0, keepdims=True)
    log_rows[...] = jnp.transpose(log_ref[...])[0:8, :]
    dq_side[...] = jnp.zeros_like(dq_side)

    def block(key_row, row_base, row_count, masked, before):
        keys = pl.ds(key_row, keys_of)
        dk_sum = jnp.zeros((keys_of, width), full)
        dv_sum = jnp.zeros((keys_of, width), full)
        for head in range(head_count):
            before(head)
            k_head = keep_head(head, k_rot[keys, :])
            v_head = keep_head(head, v_rot[keys, :])
            lanes = slice(head * HEAD, (head + 1) * HEAD)
            k_side = k_turned[lanes, keys]
            for chunk in range(row_count // rows_of):
                start = row_base + chunk * rows_of
                rows = slice(start, start + rows_of)
                scores = dot(k_head, q_turned[:, rows], NN)
                dprobs = dot(v_head, d_turned[:, rows], NN)
                probs = jnp.exp2(scores * LOG_SCALE - log_rows[head : head + 1, rows])
                if masked:
                    shape = (keys_of, rows_of)
                    key_id = lax.broadcasted_iota(jnp.int32, shape, 0) + (key_row - LONGEST)
                    row_id = lax.broadcasted_iota(jnp.int32, shape, 1) + chunk * rows_of
                    probs = jnp.where((row_id < border) == (key_id < border), probs, 0.0)
                dv_sum = dv_sum + dot(probs.astype(low), d_heads[head, rows, :], NN)
                draw = (probs * (dprobs - deltas[head : head + 1, rows])).astype(low)
                dk_sum = dk_sum + dot(draw, q_heads[head, rows, :], NN)
                dq_side[lanes, rows] += dot(k_side, draw, NN)
        groups = pl.ds(lax.div(key_row, 8), keys_of // 8)
        dk_rot[groups] = (dk_sum * SCALE).reshape(keys_of // 8, 8, width)
        dv_rot[groups] = dv_sum.reshape(keys_of // 8, 8, width)

    trips = LONGEST // keys_of

    def gather_wo():
        for copy in wo_copies:
            copy.wait()
        wo_far[0] = (wo_part[wo_rows(team.far), :].astype(full) + wo_near[1].astype(full)).astype(low)
        wo_across.start()

    def large(index, nothing):
        def before(head):
            for trip in range(trips):
                slot = trip * head_count + head
                limit = (slot + 1) // 2
                earlier = slot // 2
                if limit > earlier:

                    @pl.when(index == trip)
                    def _(limit=limit, slot=slot):
                        events.waiting = [event for event in everything if event[0] >= earlier]
                        events.take(limit)
                        if slot == 1:
                            gather_wo()

        block(pl.multiple_of(index * keys_of, keys_of), 0, LONGEST, False, before)
        return nothing

    def little(index, nothing):
        block(
            pl.multiple_of(LONGEST + index * keys_of, keys_of), LONGEST, small, True, lambda head: None
        )
        return nothing

    everything = list(events.waiting)
    lax.fori_loop(0, trips, large, 0)
    slots = trips * head_count
    events.waiting = [event for event in everything if event[0] >= slots // 2]
    lax.fori_loop(0, small // keys_of, little, 0)

    def unrotate(buffer, target):
        wrap(buffer, length)

        def put(index, block_rows):
            target[rows_at(index * 256, 256, 256), :] = block_rows.astype(low)

        rotate(buffer, length - offset, length, put)

    unrotate(dk_rot, dk_ref)
    unrotate(dv_rot, dv_ref)
    dq_turned[0 : length // 8] = jnp.transpose(dq_side[...] * SCALE).reshape(length // 8, 8, width)
    unrotate(dq_turned, dq_ref)
    events.end()
    keeps = []
    for index, target in enumerate((up_sum, up_sum, down_sum, down_sum)):
        lanes = pl.ds((index % 2) * lanes_of, lanes_of)
        keeps.append(pltpu.make_async_copy(wires.at[index], target.at[:, lanes], keep_sems.at[index]))
    for keep in keeps:
        keep.start()
    wo_across.wait()
    mine = wo_part[wo_rows(team.me), :].astype(full) + wo_near[0].astype(full)
    wo_sum[...] = (mine + wo_far[1].astype(full)).astype(low)
    out_copy.wait()
    for keep in keeps:
        keep.wait()


def attend_backward(
    size, spans, q_rot, k_rot, v_rot, grad_mixed, mixed_rot, log_totals, up_part, down_part, wo_part, out_far
):
    length, width = q_rot.shape
    head_count = width // HEAD
    low, full = jnp.bfloat16, jnp.float32
    half = (2 * up_part.shape[0], up_part.shape[1] // 2)
    whole = (4 * up_part.shape[0], up_part.shape[1])
    wo_shape = (wo_part.shape[0] // 4, wo_part.shape[1])

    def shape(dims):
        return jax.ShapeDtypeStruct(dims, low)

    grouped = (length // 8 + EXTRA, 8, width)
    return pl.pallas_call(
        functools.partial(backward_kernel, 256, 512, head_count, size),
        out_shape=(shape((length, width)),) * 3
        + (shape(whole), shape(whole), shape(wo_shape), shape(out_far.shape)),
        in_specs=[SMEM] + [VMEM] * 6 + [ANY, ANY, VMEM, ANY],
        out_specs=(VMEM,) * 3 + (ANY, ANY, VMEM, ANY),
        scratch_shapes=[
            pltpu.VMEM((length, width), low),
            pltpu.VMEM((width, length), low),
            pltpu.VMEM((width, length), low),
            pltpu.VMEM((width, length), low),
            pltpu.VMEM((head_count, length, width), low),
            pltpu.VMEM((head_count, length, width), low),
            pltpu.VMEM(grouped, full),
            pltpu.VMEM(grouped, full),
            pltpu.VMEM(grouped, full),
            pltpu.VMEM((8, length), full),
            pltpu.VMEM((8, length), full),
            pltpu.VMEM((4, *half), full),
            pltpu.VMEM((4, 2 * half[0], half[1]), low),
            [halving_scratch(size, *half) for unused in range(4)],
            pltpu.VMEM((2, *wo_shape), low),
            pltpu.VMEM((2, *wo_shape), low),
            DMA((2, 3)),
            DMA((2,)),
            DMA((4,)),
            pltpu.VMEM((width, length), full),
        ],
        compiler_params=pltpu.CompilerParams(
            collective_id=3, has_side_effects=True, vmem_limit_bytes=63 << 20
        ),
        name="attend_backward",
    )(spans, q_rot, k_rot, v_rot, grad_mixed, mixed_rot, log_totals, up_part, down_part, wo_part, out_far)


def project_kernel(
    part,
    x_ref,
    gain,
    shift,
    wq,
    bq,
    wk,
    wv,
    bv,
    x_all,
    normed,
    q_ref,
    k_ref,
    v_ref,
    landing,
    far_send,
    far_recv,
    near_send,
    near_recv,
    pass_send,
    pass_recv,
    keep_sem,
):
    team = Team()
    own = x_ref.shape[0]
    count = own // part

    def piece(owner, index):
        return rows_at(owner * own + index * part, part, part)

    def far_copy(index):
        source = x_ref.at[rows_at(index * part, part, part)]
        return team.copy(
            source, landing.at[piece(team.me, index)], far_send.at[index], far_recv.at[index], team.far
        )

    def pass_copy(index):
        place = landing.at[piece(team.far, index)]
        return team.copy(place, place, pass_send.at[index], pass_recv.at[index], team.sibling)

    near = team.copy(
        x_ref, landing.at[rows_at(team.me * own, own, own)], near_send, near_recv, team.sibling
    )

    def keep(owner, source, slot):
        return pltpu.make_async_copy(source, x_all.at[rows_at(owner * own, own, own)], keep_sem.at[slot])

    team.greet((team.sibling, team.far))
    for index in range(count):
        far_copy(index).start()
    near.start()
    keep(team.me, x_ref, 0).start()

    gain_row, shift_row, bq_row, bv_row = as_row(gain), as_row(shift), as_row(bq), as_row(bv)

    def project(owner, index, values):
        standard, unused = standardize(values.astype(FULL))
        low = (standard * gain_row + shift_row).astype(LOW)
        rows = piece(owner, index)
        normed[rows, :] = low
        q_ref[rows, :] = (dot(low, wq[...], NT) + bq_row).astype(LOW)
        k_ref[rows, :] = dot(low, wk[...], NT).astype(LOW)
        v_ref[rows, :] = (dot(low, wv[...], NT) + bv_row).astype(LOW)

    def mine(index, nothing):
        project(team.me, index, x_ref[rows_at(index * part, part, part), :])
        return nothing

    lax.fori_loop(0, count, mine, 0)
    near.wait()

    def next_to(index, nothing):
        project(team.sibling, index, landing[piece(team.sibling, index), :])
        return nothing

    lax.fori_loop(0, count, next_to, 0)

    def across(index, nothing):
        far_copy(index).wait_recv()
        pass_copy(index).start()
        project(team.far, index, landing[piece(team.far, index), :])
        pass_copy(index).wait_recv()
        project(team.diagonal, index, landing[piece(team.diagonal, index), :])
        return nothing

    lax.fori_loop(0, count, across, 0)
    for slot, owner in ((1, team.sibling), (2, team.far), (3, team.diagonal)):
        keep(owner, landing.at[rows_at(owner * own, own, own)], slot).start()
    for slot, owner in ((1, team.sibling), (2, team.far), (3, team.diagonal)):
        keep(owner, landing.at[rows_at(owner * own, own, own)], slot).wait()
    keep(team.me, x_ref, 0).wait()
    for index in range(count):
        far_copy(index).wait_send()
        pass_copy(index).wait_send()


def gather_and_project(x, gain, shift, wq, bq, wk, wv, bv):
    own, width = x.shape
    length, columns, part = 4 * own, wq.shape[0], 128
    count = own // part
    narrow = jax.ShapeDtypeStruct((length, columns), LOW)
    wide = jax.ShapeDtypeStruct((length, width), LOW)
    return pl.pallas_call(
        functools.partial(project_kernel, part),
        out_shape=(wide, wide, narrow, narrow, narrow),
        in_specs=[VMEM] * 8,
        out_specs=(ANY, VMEM, VMEM, VMEM, VMEM),
        scratch_shapes=[
            pltpu.VMEM((length, width), LOW),
            DMA((count,)),
            DMA((count,)),
            DMA,
            DMA,
            DMA((count,)),
            DMA((count,)),
            DMA((4,)),
        ],
        compiler_params=pltpu.CompilerParams(
            collective_id=0, has_side_effects=True, vmem_limit_bytes=48 << 20
        ),
        name="gather_and_project",
    )(x, gain, shift, wq, bq, wk, wv, bv)


class Reduction:
    def __init__(self, team, near_out, near_in, far_out, far_in, sems):
        self.team = team
        self.near_out, self.near_in, self.far_out, self.far_in = near_out, near_in, far_out, far_in
        self.sems = sems

    def near(self, pair):
        return self.team.copy(
            self.near_out.at[pair % 2],
            self.near_in.at[pair],
            self.sems.at[0, pair],
            self.sems.at[1, pair],
            self.team.sibling,
        )

    def across(self, pair):
        return self.team.copy(
            self.far_out.at[pair], self.far_in.at[pair], self.sems.at[2, pair], self.sems.at[3, pair], self.team.far
        )

    def give(self, pair, values):
        @pl.when(pair >= 2)
        def _():
            self.near(pair - 2).wait_send()

        self.near_out[pair % 2] = values.astype(LOW)
        self.near(pair).start()

    def combine(self, pair, values):
        self.near(pair).wait_recv()
        return values + self.near_in[pair].astype(FULL)

    def send(self, pair, values):
        self.far_out[pair] = values.astype(LOW)
        self.across(pair).start()

    def arrived(self, pair):
        self.across(pair).wait_recv()
        return self.far_in[pair].astype(FULL)

    def finish(self, pairs):
        for pair in range(pairs // 2):
            self.across(pair).wait_send()
        for pair in (pairs - 2, pairs - 1):
            self.near(pair).wait_send()


def owner_at(team_me, step):
    half = lax.div(step, 4)
    odd = lax.rem(step, 2)
    one = flip(team_me, 0)
    base = one + odd * (team_me - one)
    return lax.rem(base + 2 * (1 - half), 4)


def part_at(step):
    return lax.rem(lax.div(step, 2), 2)


def ffn_kernel(
    part,
    size,
    mixed_ref,
    pieces,
    x_all,
    cot_ref,
    wo,
    up,
    down,
    up_bias,
    out_bias,
    gain,
    shift,
    down_bias,
    out_far,
    out_own,
    grad_middle,
    grad_mixed,
    up_part,
    down_part,
    grad_wo,
    sums,
    middle_own,
    up_half,
    down_half,
    halves_out,
    halves_in,
    half_sems,
    halving_parts,
    keep_sems,
    cot_all,
    normed_all,
    hidden_all,
    gpre_all,
    out_slots,
    out_near,
    own_sum,
    near_out,
    near_in,
    far_out,
    far_in,
    mixed_out,
    cot_sems,
    slot_sems,
    red_sems,
    a2a_sems,
):
    team = Team()
    length = mixed_ref.shape[0]
    width = x_all.shape[1]
    columns = mixed_ref.shape[1]
    own = length // 4
    steps = length // part

    def rows_of(owner, index):
        return rows_at(owner * own + index * part, part, part)

    def step_rows(device, step):
        return rows_of(owner_at(device, step), part_at(step))

    spreads = [
        Spread(
            team,
            cot_ref.at[pl.ds(index * part, part)],
            cot_all,
            lambda owner, index=index: rows_of(owner, index),
            cot_sems.at[index],
        )
        for index in range(own // part)
    ]
    reduction = Reduction(team, near_out, near_in, far_out, far_in, red_sems)

    def slot_copy(pair):
        slot = lax.rem(pair, 2)
        return team.copy(
            out_slots.at[slot], out_near.at[pair], slot_sems.at[0, slot], slot_sems.at[1, pair], team.sibling
        )

    plane = Plane(size)
    team.greet((team.sibling, team.far, team.diagonal), *[plane.partner(bit) for bit in range(3)])

    for spread in spreads:
        spread.start()
    sums[...] = jnp.zeros_like(sums)
    gain_row, shift_row, bias_row = as_row(gain), as_row(shift), as_row(out_bias)
    up_row, down_row = as_row(up_bias), as_row(down_bias)

    def forward(step, keep_middle):
        rows = step_rows(team.me, step)

        def weights(owner):
            return wo[rows_at(owner * columns, columns, 64), :]

        branch = dot(mixed_ref[rows, :], weights(team.me), NN)
        branch = branch + dot(pieces[0, rows, :], weights(team.sibling), NN)
        branch = branch + dot(pieces[1, rows, :], weights(team.far), NN)
        branch = branch + dot(pieces[2, rows, :], weights(team.diagonal), NN)
        middle = x_all[rows, :].astype(FULL) + (branch + bias_row)
        if keep_middle:

            @pl.when(step >= steps // 2)
            def _():
                middle_own[rows_at(part_at(step) * part, part, part), :] = middle

        standard, unused = standardize(middle)
        low = (standard * gain_row + shift_row).astype(LOW)
        normed_all[rows, :] = low
        pre = dot(low, up[...], NN) + up_row
        bell = 0.5 * (1.0 + lax.erf(pre * 0.7071067811865476))
        hidden = (pre * bell).astype(LOW)
        hidden_all[rows, :] = hidden
        slope = bell + pre * (jnp.exp(pre * pre * -0.5) * 0.3989422804014327)
        gpre_all[rows, :] = slope.astype(LOW)

        out = dot(hidden, down[...], NN)
        pair = lax.div(step, 2)
        if keep_middle:
            slot_copy(pair).wait_recv()
            out = out + out_near[pair].astype(FULL)
            place = rows_at(part_at(step) * part, part, part)

            @pl.when(step < steps // 2)
            def _():
                out_far[place, :] = out.astype(LOW)

            @pl.when(step >= steps // 2)
            def _():
                out_own[place, :] = middle + out + down_row
        else:

            @pl.when(pair >= 2)
            def _():
                slot_copy(pair - 2).wait_send()

            out_slots[lax.rem(pair, 2)] = out.astype(LOW)
            slot_copy(pair).start()
    def backward(step):
        rows = step_rows(team.me, step)
        slope = gpre_all[rows, :].astype(FULL)
        grad_pre = (dot(cot_all[rows, :], down[...], NT) * slope).astype(LOW)
        gpre_all[rows, :] = grad_pre
        sums[4:5, :] += column_sums(grad_pre.astype(FULL))
        return dot(grad_pre, up[...], NT)

    def pair_forward(pair, nothing):
        forward(2 * pair, False)
        forward(2 * pair + 1, True)
        return nothing

    def pair_backward(pair, nothing):
        first, second = 2 * pair, 2 * pair + 1
        for index, spread in enumerate(spreads):

            @pl.when(pair == index)
            def _(spread=spread):
                spread.middle()
                spread.passed().wait_recv()

        @pl.when(pair == len(spreads))
        def _():
            for spread in spreads:
                spread.near().wait_recv()
                spread.kept().wait()
            side_half(1)

        reduction.give(pair, backward(first))
        values = reduction.combine(pair, backward(second))

        @pl.when(pair < steps // 4)
        def _():
            reduction.send(pair, values)

        @pl.when(pair >= steps // 4)
        def _():
            own_sum[rows_at(part_at(second) * part, part, part), :] = values

        return nothing

    half = width // 2
    up_total = Halving(plane, up_half, None, 0, *halving_parts[0])
    down_total = Halving(plane, down_half, None, 0, *halving_parts[1])
    up_keep = pltpu.make_async_copy(up_half.at[up_total.inner(1)], up_part, keep_sems.at[0])
    down_keep = pltpu.make_async_copy(down_half.at[down_total.inner(2)], down_part, keep_sems.at[1])
    halves = (normed_all, gpre_all, up_half), (hidden_all, cot_all, down_half)
    side_copies = [
        plane.remote(halves_out.at[index], halves_in.at[index], half_sems, index, plane.partner(0))
        for index in range(2)
    ]
    def side_half(index):
        left, right, unused = halves[index]
        lanes = rows_at((1 - plane.side) * half, half, half)
        halves_out[index] = dot(left[:, lanes], right[...], TN).astype(LOW)
        side_copies[index].start()

    lax.fori_loop(0, steps // 2, pair_forward, 0)
    lax.fori_loop(0, steps // 2, pair_backward, 0)
    side_half(0)

    def own_half(index):
        left, right, target = halves[index]
        target[...] = dot(left[:, rows_at(plane.side * half, half, half)], right[...], TN)

    def add_side(index):
        side_copies[index].wait()
        halves[index][2][...] += halves_in[index].astype(FULL)

    own_half(1)
    own_half(0)
    add_side(1)
    down_total.start(0)

    wo_sums = []
    for index in range(own // part):
        rows = pl.ds(index * part, part)
        grad = own_sum[rows, :] + reduction.arrived(index)
        standard, inverse = standardize(middle_own[rows, :])
        incoming = cot_all[rows_of(team.me, index), :].astype(FULL)
        grad_mid = incoming + norm_back(grad, gain_row, standard, inverse)
        grad_middle[rows, :] = grad_mid
        branch_low = grad_mid.astype(LOW)
        sums[0:1, :] += column_sums(grad * standard)
        sums[1:2, :] += column_sums(grad)
        sums[2:3, :] += column_sums(branch_low.astype(FULL))
        sums[3:4, :] += column_sums(incoming)
        for slot, owner in enumerate((team.sibling, team.far, team.diagonal)):
            side = wo[rows_at(owner * columns, columns, 64), :]
            mixed_out[slot, rows, :] = dot(branch_low, side, NT).astype(LOW)
        side = wo[rows_at(team.me * columns, columns, 64), :]
        grad_mixed[rows_of(team.me, index), :] = dot(branch_low, side, NT).astype(LOW)
        own_rows = rows_of(team.me, index)
        for source, owner in (
            (mixed_ref.at[own_rows], team.me),
            (pieces.at[0, own_rows], team.sibling),
            (pieces.at[1, own_rows], team.far),
            (pieces.at[2, own_rows], team.diagonal),
        ):
            place = rows_at(owner * columns, columns, 64)
            wo_sums.append((place, dot(source[...], branch_low, TN)))
    for slot in range(4):
        place = wo_sums[slot][0]
        grad_wo[place, :] = sum(value for unused, value in wo_sums[slot::4]).astype(LOW)

    here = grad_mixed.at[rows_at(team.me * own, own, own)]
    exchanges = [
        team.copy(mixed_out.at[slot], here, a2a_sems.at[0, slot], a2a_sems.at[1, slot], owner)
        for slot, owner in enumerate((team.sibling, team.far, team.diagonal))
    ]
    for exchange in exchanges:
        exchange.start()
    down_total.finish(0)
    down_total.start(1)
    add_side(0)
    up_total.start(0)
    down_total.finish(1)
    down_keep.start()
    for exchange in exchanges:
        exchange.wait()
    up_total.finish(0)
    up_keep.start()
    down_keep.wait()
    up_keep.wait()

    for spread in spreads:
        spread.sent()
    for pair in (steps // 2 - 2, steps // 2 - 1):
        slot_copy(pair).wait_send()
    reduction.finish(steps // 2)


def ffn(size, mixed, pieces, x_all, cotangent, wo, up, down, up_bias, out_bias, gain, shift, down_bias):
    length, columns = mixed.shape
    width = x_all.shape[1]
    hidden = up.shape[1]
    own, part = length // 4, 320
    steps = length // part
    pairs = steps // 2

    def shape(dims, kind):
        return jax.ShapeDtypeStruct(dims, kind)

    return pl.pallas_call(
        functools.partial(ffn_kernel, part, size),
        out_shape=(
            shape((own, width), LOW),
            shape((own, width), FULL),
            shape((own, width), FULL),
            shape((length, columns), LOW),
            shape((width // 4, hidden), FULL),
            shape((hidden // 8, width), FULL),
            shape((width, width), LOW),
            shape((8, width), FULL),
        ),
        in_specs=[VMEM] * 12,
        out_specs=(VMEM,) * 4 + (ANY, ANY, VMEM, VMEM),
        scratch_shapes=[
            pltpu.VMEM((own, width), FULL),
            pltpu.VMEM((width // 2, hidden), FULL),
            pltpu.VMEM((hidden // 2, width), FULL),
            pltpu.VMEM((2, width // 2, width), LOW),
            pltpu.VMEM((2, width // 2, width), LOW),
            DMA((2, 2)),
            [halving_scratch(size, width // 2, width) for unused in range(2)],
            DMA((2,)),
            pltpu.VMEM((length, width), LOW),
            pltpu.VMEM((length, width), LOW),
            pltpu.VMEM((length, hidden), LOW),
            pltpu.VMEM((length, hidden), LOW),
            pltpu.VMEM((2, part, width), LOW),
            pltpu.VMEM((pairs, part, width), LOW),
            pltpu.VMEM((own, width), FULL),
            pltpu.VMEM((2, part, width), LOW),
            pltpu.VMEM((pairs, part, width), LOW),
            pltpu.VMEM((pairs // 2, part, width), LOW),
            pltpu.VMEM((pairs // 2, part, width), LOW),
            pltpu.VMEM((3, own, columns), LOW),
            DMA((own // part, 7)),
            DMA((2, pairs)),
            DMA((4, pairs)),
            DMA((2, 3)),
        ],
        compiler_params=pltpu.CompilerParams(
            collective_id=2, has_side_effects=True, vmem_limit_bytes=63 << 20
        ),
        name="ffn",
    )(mixed, pieces, x_all, cotangent, wo, up, down, up_bias, out_bias, gain, shift, down_bias)


def last_kernel(
    part,
    size,
    dq_ref,
    dk_ref,
    dv_ref,
    wq,
    wk,
    wv,
    normed_all,
    x_all,
    grad_middle,
    gain,
    wo_sum,
    wide,
    input_grad,
    grad_sum,
    vectors,
    own_grad,
    near_out,
    near_in,
    far_out,
    far_in,
    red_sems,
    sources,
    wires,
    total_parts,
    packed,
    packed_in,
    vec_sems,
    keep_sems,
):
    team, plane = Team(), Plane(size)
    length, columns = dq_ref.shape
    width = normed_all.shape[1]
    own = length // 4
    pairs = length // part // 2
    grads = Reduction(team, near_out, near_in, far_out, far_in, red_sems)
    slabs = sources.shape[0]
    lanes_of = width // slabs
    totals = [Direct(plane, sources.at[slab], wires.at[slab], *total_parts[slab]) for slab in range(slabs)]
    others = greet_all(team, plane, True)
    events = Events(totals)
    for slab in range(slabs):
        lanes = slice(slab * lanes_of, (slab + 1) * lanes_of)
        for index, source in enumerate((dq_ref, dk_ref, dv_ref)):
            value = dot(source[...], normed_all[:, lanes], TN)
            sources[slab, index * columns : (index + 1) * columns, :] = value.astype(LOW)
        sources[slab, 3 * columns : 4 * columns, :] = wo_sum[:, lanes]
        totals[slab].start(0)
    gain_row = as_row(gain)
    packed[...] = jnp.zeros_like(packed)
    packed[0:4, :] = wide[0:4, :]
    packed[8:9, :] = wide[4:5, :]
    packed[9:10, 0:columns] = column_sums(dq_ref[...].astype(FULL))
    packed[10:11, 0:columns] = column_sums(dv_ref[...].astype(FULL))

    def step_rows(step):
        return rows_at(owner_at(team.me, step) * own + part_at(step) * part, part, part)

    def compute(step):
        rows = step_rows(step)
        total = dot(dq_ref[rows, :], wq[...], NN) + dot(dk_ref[rows, :], wk[...], NN)
        return total + dot(dv_ref[rows, :], wv[...], NN)

    for pair in range(pairs):
        first, second = 2 * pair, 2 * pair + 1
        grads.give(pair, compute(first))
        standard, unused = standardize(x_all[step_rows(second), :].astype(FULL))
        if pair >= 1:
            events.next(1)
        values = grads.combine(pair, compute(second))
        packed[4:5, :] += column_sums(values * standard)
        packed[5:6, :] += column_sums(values)
        if pair < pairs // 2:
            grads.send(pair, values)
        else:
            own_grad[rows_at(part_at(second) * part, part, part), :] = values
        if pair >= 2:
            events.next(1)

    def vector_copy(step):
        return pltpu.make_async_remote_copy(
            src_ref=packed.at[pl.ds(16 * step, 16)],
            dst_ref=packed_in.at[step],
            send_sem=vec_sems.at[0, step],
            recv_sem=vec_sems.at[1, step],
            device_id=others[step],
            device_id_type=MESH,
        )

    def finish_rows(index):
        rows = pl.ds(index * part, part)
        grad = own_grad[rows, :] + grads.arrived(index)
        standard, inverse = standardize(x_all[rows_at(team.me * own + index * part, part, part), :].astype(FULL))
        input_grad[rows, :] = grad_middle[rows, :] + norm_back(grad, gain_row, standard, inverse)

    for step in range(len(others)):
        vector_copy(step).start()
        events.next(1)
        vector_copy(step).wait()
        here = packed[16 * step : 16 * (step + 1), :]
        keep = 16 if step < plane.bits else 8
        row = lax.broadcasted_iota(jnp.int32, here.shape, 0)
        added = here + jnp.where(row < keep, packed_in[step], 0.0)
        packed[16 * (step + 1) : 16 * (step + 2), :] = added
    vectors[...] = packed[16 * len(others) : 16 * (len(others) + 1), :]
    events.take(1 << 20)
    for index in range(own // part):
        finish_rows(index)
    events.end()
    keeps = []
    for slab in range(slabs):
        lanes = pl.ds(slab * lanes_of, lanes_of)
        keeps.append(pltpu.make_async_copy(wires.at[slab], grad_sum.at[:, lanes], keep_sems.at[slab]))
    for keep in keeps:
        keep.start()
    for keep in keeps:
        keep.wait()
    grads.finish(pairs)


def last(size, dq, dk, dv, wq, wk, wv, normed_all, x_all, grad_middle, gain, wo_sum, wide):
    length, columns = dq.shape
    own, width = grad_middle.shape
    part, slabs = 320, 3
    pairs = length // part // 2
    bits = size.bit_length() - 1
    slab = (4 * columns, width // slabs)

    def shape(dims, kind):
        return jax.ShapeDtypeStruct(dims, kind)

    return pl.pallas_call(
        functools.partial(last_kernel, part, size),
        out_shape=(
            shape((own, width), FULL),
            shape((4 * columns, width), LOW),
            shape((16, width), FULL),
        ),
        in_specs=[VMEM] * 12,
        out_specs=(VMEM, ANY, VMEM),
        scratch_shapes=[
            pltpu.VMEM((own, width), FULL),
            pltpu.VMEM((2, part, width), LOW),
            pltpu.VMEM((pairs, part, width), LOW),
            pltpu.VMEM((pairs // 2, part, width), LOW),
            pltpu.VMEM((pairs // 2, part, width), LOW),
            DMA((4, pairs)),
            pltpu.VMEM((slabs, *slab), LOW),
            pltpu.VMEM((slabs, *slab), LOW),
            [direct_scratch(size, *slab) for unused in range(slabs)],
            pltpu.VMEM((16 * (bits + 3), width), FULL),
            pltpu.VMEM((bits + 2, 16, width), FULL),
            DMA((2, bits + 2)),
            DMA((slabs,)),
        ],
        compiler_params=pltpu.CompilerParams(
            collective_id=4, has_side_effects=True, vmem_limit_bytes=60 << 20
        ),
        name="last",
    )(dq, dk, dv, wq, wk, wv, normed_all, x_all, grad_middle, gain, wo_sum, wide)


def local(
    size,
    layer_input,
    segment_ids,
    cotangent,
    attn_gain,
    attn_shift,
    query_weight,
    query_bias,
    key_weight,
    value_weight,
    value_bias,
    out_weight,
    out_bias,
    ffn_gain,
    ffn_shift,
    up_weight,
    up_bias,
    down_weight,
    down_bias,
):
    query_side, key_side, value_side = query_weight.T, key_weight.T, value_weight.T
    x_all, normed_rows, queries, key_rows, value_rows = gather_and_project(
        layer_input,
        attn_gain,
        attn_shift,
        query_side,
        query_bias,
        key_side,
        value_side,
        value_bias,
    )
    mixed, mixed_rot, log_totals, pieces, out_all, q_rot, k_rot, v_rot = attend_forward(
        segment_ids, queries, key_rows, value_rows, out_weight
    )
    out_far, out_own, grad_middle, grad_mixed, up_part, down_part, out_part, sums = ffn(
        size,
        mixed,
        pieces,
        x_all,
        cotangent,
        out_all,
        up_weight,
        down_weight,
        up_bias,
        out_bias,
        ffn_gain,
        ffn_shift,
        down_bias,
    )
    dq, dk, dv, grad_up, grad_down, wo_sum, out_in = attend_backward(
        size, segment_ids, q_rot, k_rot, v_rot, grad_mixed, mixed_rot, log_totals, up_part, down_part, out_part, out_far
    )
    layer_output = (out_own + out_in.astype(FULL)).astype(LOW)
    input_grad, grads, vectors = last(
        size,
        dq,
        dk,
        dv,
        query_side,
        key_side,
        value_side,
        normed_rows,
        x_all,
        grad_middle,
        attn_gain,
        wo_sum,
        sums,
    )
    columns = query_side.shape[0]
    grads = grads.astype(FULL)
    return (
        layer_output,
        input_grad,
        vectors[4],
        vectors[5],
        grads[0:columns].T,
        vectors[9, 0:columns],
        grads[columns : 2 * columns].T,
        grads[2 * columns : 3 * columns].T,
        vectors[10, 0:columns],
        grads[3 * columns :],
        vectors[2],
        vectors[0],
        vectors[1],
        grad_up.astype(FULL),
        vectors[8],
        grad_down.astype(FULL),
        vectors[3],
    )


def solution(mesh):
    return jax.shard_map(
        functools.partial(local, mesh.shape["dp"]),
        mesh=mesh,
        in_specs=(
            P(("dp", "seq"), None),
            P("dp", None),
            P(("dp", "seq"), None),
            P(),
            P(),
            P(None, "seq"),
            P("seq"),
            P(None, "seq"),
            P(None, "seq"),
            P("seq"),
            P("seq", None),
            P(),
            P(),
            P(),
            P(None, "seq"),
            P("seq"),
            P("seq", None),
            P(),
        ),
        out_specs=(
            P(("dp", "seq"), None),
            P(("dp", "seq"), None),
            P(),
            P(),
            P(None, "seq"),
            P("seq"),
            P(None, "seq"),
            P(None, "seq"),
            P("seq"),
            P("seq", None),
            P(),
            P(),
            P(),
            P(None, "seq"),
            P("seq"),
            P("seq", None),
            P(),
        ),
        check_vma=False,
    )
```

```python
import functools

import jax
import jax.numpy as jnp
from jax import lax
from jax.experimental import pallas as pl
from jax.experimental.pallas import tpu as pltpu
from jax.sharding import PartitionSpec as P

HEAD = 64
SCALE = HEAD ** (-0.5)
LOG_SCALE = SCALE * 1.4426950408889634
LONGEST = 2048
EPSILON = 1e-06
NN = (((1,), (0,)), ((), ()))
NT = (((1,), (1,)), ((), ()))
TN = (((0,), (0,)), ((), ()))
MESH = pl.DeviceIdType.MESH
LOW = jnp.bfloat16
FULL = jnp.float32
VMEM = pl.BlockSpec(memory_space=pltpu.VMEM)
SMEM = pl.BlockSpec(memory_space=pltpu.SMEM)
ANY = pl.BlockSpec(memory_space=pl.ANY)
DMA = pltpu.SemaphoreType.DMA


def flip(index, bit):
    size = 1 << bit
    return index + size - 2 * size * lax.rem(lax.div(index, size), 2)


class Team:
    def __init__(self):
        self.row = lax.axis_index("dp")
        self.me = lax.axis_index("seq")
        self.sibling = flip(self.me, 0)
        self.far = flip(self.me, 1)
        self.diagonal = flip(self.sibling, 1)

    def device(self, index):
        return (self.row, index)

    def greet(self, others, *more):
        barrier = pltpu.get_barrier_semaphore()
        devices = [self.device(other) for other in others] + list(more)
        for device in devices:
            pl.semaphore_signal(barrier, inc=1, device_id=device, device_id_type=MESH)
        pl.semaphore_wait(barrier, len(devices))

    def copy(self, source, target, send, receive, other):
        return pltpu.make_async_remote_copy(
            src_ref=source,
            dst_ref=target,
            send_sem=send,
            recv_sem=receive,
            device_id=self.device(other),
            device_id_type=MESH,
        )


def rows_at(start, count, multiple):
    return pl.ds(pl.multiple_of(start, multiple), count)


def standardize(values):
    average = jnp.mean(values, axis=-1, keepdims=True)
    centered = values - average
    variance = jnp.mean(centered * centered, axis=-1, keepdims=True)
    inverse = lax.rsqrt(variance + EPSILON)
    return centered * inverse, inverse


def norm_back(grad, gain_row, standard, inverse):
    scaled = grad * gain_row
    mean_one = jnp.mean(scaled, axis=-1, keepdims=True)
    mean_two = jnp.mean(scaled * standard, axis=-1, keepdims=True)
    return inverse * (scaled - mean_one - standard * mean_two)


def column_sums(values):
    return jnp.sum(values, axis=0, keepdims=True)


def first_at_least(segments, value):
    length = segments.shape[1]

    def halve(unused, ends):
        low, high = ends
        middle = jnp.minimum(lax.div(low + high, 2), length - 1)
        below = segments[0, middle] < value
        open_yet = low < high
        return (
            jnp.where(open_yet & below, middle + 1, low),
            jnp.where(open_yet & jnp.logical_not(below), middle, high),
        )

    return lax.fori_loop(0, length.bit_length(), halve, (jnp.int32(0), jnp.int32(length)))[0]


def rotation(segments):
    length = segments.shape[1]
    one, two = first_at_least(segments, 1), first_at_least(segments, 2)
    offset = jnp.where(one == LONGEST, 0, jnp.where(two - one == LONGEST, one, two))
    border = jnp.where(one == LONGEST, two - one, jnp.where(two - one == LONGEST, length - two, one))
    return offset, border


def as_row(ref):
    return ref[...].astype(FULL).reshape(1, -1)


def dot(left_side, right_side, dims):
    return lax.dot_general(left_side, right_side, dims, preferred_element_type=jnp.float32)


def keep_head(head, values):
    lane = lax.broadcasted_iota(jnp.int32, values.shape, 1)
    inside = (lane >= head * HEAD) & (lane < (head + 1) * HEAD)
    return jnp.where(inside, values, jnp.zeros_like(values))


class Spread:
    def __init__(self, team, source, target, rows_of, sems):
        self.team, self.source, self.target, self.rows_of, self.sems = team, source, target, rows_of, sems

    def place(self, owner):
        return self.target.at[self.rows_of(owner)]

    def across(self):
        here = self.place(self.team.me)
        return self.team.copy(self.source, here, self.sems.at[0], self.sems.at[1], self.team.far)

    def near(self):
        here = self.place(self.team.me)
        return self.team.copy(self.source, here, self.sems.at[2], self.sems.at[3], self.team.sibling)

    def passed(self):
        there = self.place(self.team.far)
        return self.team.copy(there, there, self.sems.at[4], self.sems.at[5], self.team.sibling)

    def kept(self):
        return pltpu.make_async_copy(self.source, self.place(self.team.me), self.sems.at[6])

    def start(self):
        self.across().start()
        self.near().start()
        self.kept().start()

    def middle(self):
        self.across().wait_recv()
        self.passed().start()

    def sent(self):
        self.across().wait_send()
        self.near().wait_send()
        self.passed().wait_send()


EXTRA = 72


def rotated_block(ref, shift, length, index):
    width = ref.shape[2]
    sub = lax.broadcasted_iota(jnp.int32, (32, 8, width), 1)
    start = lax.rem(shift + index * 256, length)
    group = lax.div(start, 8)
    skip = start - group * 8
    turned = pltpu.roll(ref[pl.ds(group, 33)], lax.rem(8 - skip, 8), 1)
    return jnp.where(sub < 8 - skip, turned[:32], turned[1:]).reshape(256, width)


def rotate(ref, shift, length, put):
    def one(index, nothing):
        put(index, rotated_block(ref, shift, length, index))
        return nothing

    lax.fori_loop(0, length // 256, one, 0)


def wrap(ref, length):
    ref[length // 8 : length // 8 + EXTRA] = ref[0:EXTRA]


def rotate_into(source, target, buffer, shift):
    length, width = source.shape
    buffer[0 : length // 8] = source[...].astype(FULL).reshape(length // 8, 8, width)
    wrap(buffer, length)

    def put(index, block):
        target[rows_at(index * 256, 256, 256), :] = block.astype(LOW)

    rotate(buffer, shift, length, put)


def forward_kernel(
    rows_of,
    keys_of,
    head_count,
    spans,
    q_ref,
    k_ref,
    v_ref,
    wo_ref,
    mixed_ref,
    mixed_rot_ref,
    log_ref,
    pieces,
    wo_all,
    q_rot,
    k_rot,
    v_rot,
    v_heads,
    buffer,
    wo_sems,
    far_sems,
    near_sems,
    pass_sems,
):
    length, width = q_ref.shape
    team = Team()
    spread = Spread(team, wo_ref, wo_all, lambda owner: rows_at(owner * width, width, 64), wo_sems)

    def far_copy(index):
        rows = rows_at(index * 256, 256, 256)
        return team.copy(
            mixed_ref.at[rows], pieces.at[1, rows], far_sems.at[0, index], far_sems.at[1, index], team.far
        )

    def near_copy(index):
        rows = rows_at(index * 256, 256, 256)
        return team.copy(
            mixed_ref.at[rows], pieces.at[0, rows], near_sems.at[0, index], near_sems.at[1, index], team.sibling
        )

    def pass_copy(index):
        rows = rows_at(index * 256, 256, 256)
        return team.copy(
            pieces.at[1, rows], pieces.at[2, rows], pass_sems.at[0, index], pass_sems.at[1, index], team.sibling
        )

    team.greet((team.sibling, team.far))
    spread.start()
    small = length - LONGEST
    offset, border = rotation(spans)

    rotate_into(q_ref, q_rot, buffer, offset)
    rotate_into(k_ref, k_rot, buffer, offset)
    rotate_into(v_ref, v_rot, buffer, offset)
    v_all = v_rot[...]
    for head in range(head_count):
        v_heads[head] = jnp.concatenate(
            [keep_head(head, v_all), jnp.full((length, 256 - width), 1, jnp.bfloat16)], axis=1
        )

    def block(row, key_base, key_count, masked):
        rows = pl.ds(row, rows_of)
        total = jnp.zeros((rows_of, width), jnp.float32)
        logs = []
        for head in range(head_count):
            q_head = keep_head(head, q_rot[rows, :])
            top, parts = None, []
            for chunk in range(key_count // keys_of):
                keys = pl.ds(key_base + chunk * keys_of, keys_of)
                scores = dot(q_head, k_rot[keys, :], NT)
                if masked:
                    shape = (rows_of, keys_of)
                    row_id = lax.broadcasted_iota(jnp.int32, shape, 0) + (row - LONGEST)
                    key_id = lax.broadcasted_iota(jnp.int32, shape, 1) + chunk * keys_of
                    scores = jnp.where((row_id < border) == (key_id < border), scores, -1e30)
                high = jnp.max(scores, axis=1, keepdims=True)
                top = high if top is None else jnp.maximum(top, high)
                parts.append(scores)
            summed = jnp.zeros((rows_of, 256), jnp.float32)
            for chunk, scores in enumerate(parts):
                keys = pl.ds(key_base + chunk * keys_of, keys_of)
                weights = jnp.exp2((scores - top) * LOG_SCALE).astype(jnp.bfloat16)
                summed = summed + dot(weights, v_heads[head, keys, :], NN)
            norm = summed[:, 255:256]
            total = total + summed[:, :width] * (1.0 / norm)
            logs.append(top * LOG_SCALE + jnp.log2(norm))
        mixed_rot_ref[pl.ds(lax.div(row, 8), rows_of // 8)] = total.reshape(rows_of // 8, 8, width)
        logs.append(jnp.zeros((rows_of, 128 - head_count), jnp.float32))
        log_ref[rows, :] = jnp.concatenate(logs, axis=1)

    def send(index):
        rows = rows_at(index * 256, 256, 256)
        mixed_ref[rows, :] = rotated_block(mixed_rot_ref, length - offset, length, index).astype(LOW)
        far_copy(index).start()
        near_copy(index).start()

    def pass_on(index):
        far_copy(index).wait_recv()
        pass_copy(index).start()

    def little(index, nothing):
        block(pl.multiple_of(LONGEST + index * rows_of, rows_of), LONGEST, small, True)
        return nothing

    lax.fori_loop(0, small // rows_of, little, 0)
    lag, trips = 2, LONGEST // rows_of

    def large(index, nothing):
        block(pl.multiple_of(index * rows_of, rows_of), 0, LONGEST, False)

        @pl.when(index == 0)
        def _():
            mixed_rot_ref[length // 8 : length // 8 + 32] = mixed_rot_ref[0:32]

        send(index)

        @pl.when(index == trips // 2)
        def _():
            spread.middle()

        @pl.when(index >= lag)
        def _():
            pass_on(index - lag)

        return nothing

    lax.fori_loop(0, trips, large, 0)
    blocks = length // 256
    for index in range(trips, blocks):
        send(index)
    for index in range(trips - lag, blocks):
        pass_on(index)
    for index in range(blocks):
        near_copy(index).wait()
        far_copy(index).wait_send()
        pass_copy(index).wait()
    spread.sent()
    spread.near().wait_recv()
    spread.passed().wait_recv()
    spread.kept().wait()


def attend_forward(spans, queries, key_rows, value_rows, out_weight):
    length, width = queries.shape
    head_count = width // HEAD
    return pl.pallas_call(
        functools.partial(forward_kernel, 256, 512, head_count),
        out_shape=(
            jax.ShapeDtypeStruct((length, width), jnp.bfloat16),
            jax.ShapeDtypeStruct((length // 8 + EXTRA, 8, width), jnp.float32),
            jax.ShapeDtypeStruct((length, 128), jnp.float32),
            jax.ShapeDtypeStruct((3, length, width), LOW),
            jax.ShapeDtypeStruct((4 * out_weight.shape[0], out_weight.shape[1]), LOW),
            jax.ShapeDtypeStruct((length, width), LOW),
            jax.ShapeDtypeStruct((length, width), LOW),
            jax.ShapeDtypeStruct((length, width), LOW),
        ),
        in_specs=[SMEM, VMEM, VMEM, VMEM, VMEM],
        out_specs=(VMEM, VMEM, VMEM, ANY, ANY, VMEM, VMEM, VMEM),
        scratch_shapes=[
            pltpu.VMEM((head_count, length, 256), jnp.bfloat16),
            pltpu.VMEM((length // 8 + EXTRA, 8, width), FULL),
            DMA((7,)),
            DMA((2, length // 256)),
            DMA((2, length // 256)),
            DMA((2, length // 256)),
        ],
        compiler_params=pltpu.CompilerParams(
            collective_id=1, has_side_effects=True, vmem_limit_bytes=60 << 20
        ),
        name="attend_forward",
    )(spans, queries, key_rows, value_rows, out_weight)


class Plane:
    def __init__(self, size):
        self.me, self.lane = lax.axis_index("dp"), lax.axis_index("seq")
        self.size, self.bits = size, size.bit_length() - 1
        self.ranks = min(4, size // 2)
        self.side, self.rank = lax.rem(self.me, 2), lax.rem(lax.div(self.me, 2), self.ranks)
        self.extra = (size // 2 // self.ranks).bit_length() - 1

    def device(self, index):
        return (index, self.lane)

    def partner(self, bit):
        return self.device(flip(self.me, bit))

    def digit(self, bit):
        return lax.rem(lax.div(self.me, 1 << bit), 2)

    def other_rank(self, offset):
        return lax.rem(self.rank + offset, self.ranks)

    def ranked(self, offset):
        return self.device(self.me + 2 * (self.other_rank(offset) - self.rank))

    def remote(self, source, target, sems, index, device):
        return pltpu.make_async_remote_copy(
            src_ref=source,
            dst_ref=target,
            send_sem=sems.at[0, index],
            recv_sem=sems.at[1, index],
            device_id=device,
            device_id_type=MESH,
        )


class Halving:
    def __init__(self, plane, part, wire, first, sends, receives, sems):
        self.plane, self.part, self.wire, self.first = plane, part, wire, first
        self.sends, self.receives, self.sems = sends, receives, sems
        self.halvings, self.whole = halvings_of(plane.bits)
        self.stages = 2 * self.halvings + self.whole + 1
        half = part.shape[0]
        self.bases, self.sizes = [0], [half]
        for level in range(self.halvings):
            size = self.sizes[-1] // 2
            self.bases.append(self.bases[-1] + plane.digit(level + 1) * size)
            self.sizes.append(size)
        self.step = self.sizes[-1]
        self.shift = plane.side * half

    def inner(self, level):
        return rows_at(self.bases[level], self.sizes[level], self.step)

    def place(self, level):
        return rows_at(self.shift + self.bases[level], self.sizes[level], self.step)

    def copies(self, stage):
        plane = self.plane
        if stage < self.halvings + self.whole:
            return [
                plane.remote(self.sends[stage], self.receives[stage], self.sems, stage, plane.partner(stage + 1))
            ]
        level = 2 * self.halvings + self.whole - stage
        here = self.wire.at[self.place(level)]
        return [plane.remote(here, here, self.sems, stage, plane.partner(level))]

    def start(self, stage):
        if stage < self.halvings:
            size = self.sizes[stage + 1]
            first = self.bases[stage] + (1 - self.plane.digit(stage + 1)) * size
            self.sends[stage][...] = self.part[rows_at(first, size, self.step), :].astype(LOW)
        elif stage < self.halvings + self.whole:
            self.sends[stage][...] = self.part[self.inner(self.halvings), :].astype(LOW)
        elif stage == self.halvings + self.whole:
            self.wire[self.place(self.halvings), :] = self.part[self.inner(self.halvings), :].astype(LOW)
        for copy in self.copies(stage):
            copy.start()

    def finish(self, stage):
        for copy in self.copies(stage):
            copy.wait()
        if stage < self.halvings:
            self.part[self.inner(stage + 1), :] += self.receives[stage][...].astype(FULL)
        elif stage < self.halvings + self.whole:
            value = self.sends[stage][...].astype(FULL) + self.receives[stage][...].astype(FULL)
            self.part[self.inner(self.halvings), :] = value


def halvings_of(bits):
    halvings = min(bits - 1, 2)
    return halvings, bits - 1 - halvings


def halving_scratch(size, half, width):
    bits = size.bit_length() - 1
    halvings, whole = halvings_of(bits)
    shapes = [(half >> (stage + 1), width) for stage in range(halvings)] + [(half >> halvings, width)] * whole
    kinds = [pltpu.VMEM(dims, LOW) for dims in shapes]
    return [kinds, list(kinds), DMA((2, 2 * halvings + whole + 1))]


class Direct:
    first = 0

    def __init__(self, plane, source, wire, part, received, sends, receives, sems):
        self.plane, self.source, self.wire, self.part = plane, source, wire, part
        self.received, self.sends, self.receives, self.sems = received, sends, receives, sems
        self.half = source.shape[0] // 2
        self.piece = self.half // plane.ranks
        self.stages = 4 + plane.extra

    def side_rows(self, side):
        return rows_at(side * self.half, self.half, self.half)

    def rank_rows(self, rank):
        return rows_at(rank * self.piece, self.piece, self.piece)

    def own_rows(self):
        start = self.plane.side * self.half + self.plane.rank * self.piece
        return rows_at(start, self.piece, self.piece)

    def copies(self, stage):
        plane = self.plane
        if stage == 0:
            source = self.source.at[self.side_rows(1 - plane.side)]
            return [plane.remote(source, self.received, self.sems, 0, plane.partner(0))]
        if stage == self.stages - 1:
            here = self.wire.at[self.side_rows(plane.side)]
            return [plane.remote(here, here, self.sems, 1, plane.partner(0))]
        if 1 < stage < self.stages - 2:
            slot = plane.ranks + stage - 3
            index = 2 * plane.ranks + stage - 2
            device = plane.partner(plane.bits - plane.extra + stage - 2)
            return [plane.remote(self.sends.at[slot], self.receives.at[slot], self.sems, index, device)]
        copies = []
        for offset in range(1, plane.ranks):
            device = plane.ranked(offset)
            if stage == 1:
                slot = offset - 1
                copies.append(
                    plane.remote(self.sends.at[slot], self.receives.at[slot], self.sems, 1 + offset, device)
                )
            else:
                here = self.wire.at[self.own_rows()]
                copies.append(plane.remote(here, here, self.sems, plane.ranks + offset, device))
        return copies

    def start(self, stage):
        plane = self.plane
        if stage == 1:
            for offset in range(1, plane.ranks):
                rows = self.rank_rows(plane.other_rank(offset))
                self.sends[offset - 1] = self.part[rows, :].astype(LOW)
        elif 1 < stage < self.stages - 2:
            self.sends[plane.ranks + stage - 3] = self.part[self.rank_rows(plane.rank), :].astype(LOW)
        elif stage == self.stages - 2:
            self.wire[self.own_rows(), :] = self.part[self.rank_rows(plane.rank), :].astype(LOW)
        for copy in self.copies(stage):
            copy.start()

    def finish(self, stage):
        plane = self.plane
        for copy in self.copies(stage):
            copy.wait()
        if stage == 0:
            received = self.received[...].astype(FULL)
            self.part[...] = self.source[self.side_rows(plane.side), :].astype(FULL) + received
        elif stage == 1:
            value = self.part[self.rank_rows(plane.rank), :]
            for slot in range(plane.ranks - 1):
                value = value + self.receives[slot].astype(FULL)
            self.part[self.rank_rows(plane.rank), :] = value
        elif stage < self.stages - 2:
            slot = plane.ranks + stage - 3
            value = self.sends[slot].astype(FULL) + self.receives[slot].astype(FULL)
            self.part[self.rank_rows(plane.rank), :] = value


def direct_scratch(size, rows, width):
    ranks = min(4, size // 2)
    extra = (size // 2 // ranks).bit_length() - 1
    half = rows // 2
    pieces = pltpu.VMEM((ranks - 1 + extra, half // ranks, width), LOW)
    return [
        pltpu.VMEM((half, width), FULL),
        pltpu.VMEM((half, width), LOW),
        pieces,
        pieces,
        DMA((2, 2 * ranks + extra)),
    ]


class Events:
    def __init__(self, totals):
        self.totals = totals
        last = totals[0].stages - 1
        self.waiting = sorted(
            (2 * (stage - total.first) + index, index, stage)
            for index, total in enumerate(totals)
            for stage in range(total.first, last)
        )

    def start(self):
        for total in self.totals:
            total.start(total.first)

    def take(self, limit):
        ready = [event for event in self.waiting if event[0] < limit]
        self.waiting = [event for event in self.waiting if event[0] >= limit]
        for unused, index, stage in ready:
            self.totals[index].finish(stage)
            self.totals[index].start(stage + 1)

    def next(self, count):
        if self.waiting[:count]:
            self.take(self.waiting[min(count, len(self.waiting)) - 1][0] + 1)

    def end(self):
        self.take(1 << 20)
        for total in self.totals:
            total.finish(total.stages - 1)


def greet_all(team, plane, direct):
    barrier = pltpu.get_barrier_semaphore()
    others = [plane.partner(bit) for bit in range(plane.bits)]
    others += [team.device(team.sibling), team.device(team.far)]
    greeted = list(others)
    if direct:
        greeted = [plane.partner(0), team.device(team.sibling), team.device(team.far)]
        greeted += [plane.partner(plane.bits - plane.extra + index) for index in range(plane.extra)]
        greeted += [plane.ranked(offset) for offset in range(1, plane.ranks)]
    for other in greeted:
        pl.semaphore_signal(barrier, inc=1, device_id=other, device_id_type=MESH)
    pl.semaphore_wait(barrier, len(greeted))
    return others


def backward_kernel(
    keys_of,
    rows_of,
    head_count,
    size,
    spans,
    q_rot,
    k_rot,
    v_rot,
    d_ref,
    mixed_rot_ref,
    log_ref,
    up_part,
    down_part,
    wo_part,
    out_far,
    dq_ref,
    dk_ref,
    dv_ref,
    up_sum,
    down_sum,
    wo_sum,
    out_in,
    d_rot,
    q_turned,
    d_turned,
    k_turned,
    q_heads,
    d_heads,
    dq_turned,
    dk_rot,
    dv_rot,
    log_rows,
    deltas,
    parts,
    wires,
    total_parts,
    wo_near,
    wo_far,
    wo_sems,
    out_sems,
    keep_sems,
    dq_side,
):
    length, width = q_rot.shape
    small = length - LONGEST
    offset, border = rotation(spans)
    low, full = jnp.bfloat16, jnp.float32
    team, plane = Team(), Plane(size)
    columns = wo_sum.shape[0]
    lanes_of = up_part.shape[1] // 2
    totals, loads = [], []
    for index, source in enumerate((up_part, up_part, down_part, down_part)):
        lanes = pl.ds((index % 2) * lanes_of, lanes_of)
        total = Halving(plane, parts.at[index], wires.at[index], index // 2 * 2, *total_parts[index])
        place = parts.at[index, total.inner(index // 2 * 2)]
        loads.append(pltpu.make_async_copy(source.at[:, lanes], place, keep_sems.at[index]))
        totals.append(total)
    for load in loads:
        load.start()
    events = Events(totals)
    greet_all(team, plane, False)
    for load in loads:
        load.wait()
    events.start()
    out_copy = team.copy(out_far, out_in, out_sems.at[0], out_sems.at[1], team.far)
    out_copy.start()

    def wo_rows(owner):
        return rows_at(owner * columns, columns, 64)

    wo_copies = [
        team.copy(wo_part.at[wo_rows(owner)], wo_near.at[slot], wo_sems.at[0, slot], wo_sems.at[1, slot], team.sibling)
        for slot, owner in enumerate((team.sibling, team.diagonal))
    ]
    for copy in wo_copies:
        copy.start()
    wo_across = team.copy(wo_far.at[0], wo_far.at[1], wo_sems.at[0, 2], wo_sems.at[1, 2], team.far)

    rotate_into(d_ref, d_rot, dq_turned, offset)
    q_all, k_all, d_all = q_rot[...], k_rot[...], d_rot[...]
    q_turned[...] = jnp.transpose(q_all)
    k_turned[...] = jnp.transpose(k_all)
    d_turned[...] = jnp.transpose(d_all)
    for head in range(head_count):
        q_heads[head] = keep_head(head, q_all)
        d_heads[head] = keep_head(head, d_all)
    products = jnp.transpose(d_all.astype(full) * mixed_rot_ref[0 : length // 8].reshape(length, width))
    for head in range(head_count):
        deltas[head : head + 1, :] = jnp.sum(products[head * HEAD : (head + 1) * HEAD, :], axis=0, keepdims=True)
    log_rows[...] = jnp.transpose(log_ref[...])[0:8, :]
    dq_side[...] = jnp.zeros_like(dq_side)

    def block(key_row, row_base, row_count, masked, before):
        keys = pl.ds(key_row, keys_of)
        dk_sum = jnp.zeros((keys_of, width), full)
        dv_sum = jnp.zeros((keys_of, width), full)
        for head in range(head_count):
            before(head)
            k_head = keep_head(head, k_rot[keys, :])
            v_head = keep_head(head, v_rot[keys, :])
            lanes = slice(head * HEAD, (head + 1) * HEAD)
            k_side = k_turned[lanes, keys]
            for chunk in range(row_count // rows_of):
                start = row_base + chunk * rows_of
                rows = slice(start, start + rows_of)
                scores = dot(k_head, q_turned[:, rows], NN)
                dprobs = dot(v_head, d_turned[:, rows], NN)
                probs = jnp.exp2(scores * LOG_SCALE - log_rows[head : head + 1, rows])
                if masked:
                    shape = (keys_of, rows_of)
                    key_id = lax.broadcasted_iota(jnp.int32, shape, 0) + (key_row - LONGEST)
                    row_id = lax.broadcasted_iota(jnp.int32, shape, 1) + chunk * rows_of
                    probs = jnp.where((row_id < border) == (key_id < border), probs, 0.0)
                dv_sum = dv_sum + dot(probs.astype(low), d_heads[head, rows, :], NN)
                draw = (probs * (dprobs - deltas[head : head + 1, rows])).astype(low)
                dk_sum = dk_sum + dot(draw, q_heads[head, rows, :], NN)
                dq_side[lanes, rows] += dot(k_side, draw, NN)
        groups = pl.ds(lax.div(key_row, 8), keys_of // 8)
        dk_rot[groups] = (dk_sum * SCALE).reshape(keys_of // 8, 8, width)
        dv_rot[groups] = dv_sum.reshape(keys_of // 8, 8, width)

    trips = LONGEST // keys_of

    def gather_wo():
        for copy in wo_copies:
            copy.wait()
        wo_far[0] = (wo_part[wo_rows(team.far), :].astype(full) + wo_near[1].astype(full)).astype(low)
        wo_across.start()

    def large(index, nothing):
        def before(head):
            for trip in range(trips):
                slot = trip * head_count + head
                limit = (slot + 1) // 2
                earlier = slot // 2
                if limit > earlier:

                    @pl.when(index == trip)
                    def _(limit=limit, slot=slot):
                        events.waiting = [event for event in everything if event[0] >= earlier]
                        events.take(limit)
                        if slot == 1:
                            gather_wo()

        block(pl.multiple_of(index * keys_of, keys_of), 0, LONGEST, False, before)
        return nothing

    def little(index, nothing):
        block(
            pl.multiple_of(LONGEST + index * keys_of, keys_of), LONGEST, small, True, lambda head: None
        )
        return nothing

    everything = list(events.waiting)
    lax.fori_loop(0, trips, large, 0)
    slots = trips * head_count
    events.waiting = [event for event in everything if event[0] >= slots // 2]
    lax.fori_loop(0, small // keys_of, little, 0)

    def unrotate(buffer, target):
        wrap(buffer, length)

        def put(index, block_rows):
            target[rows_at(index * 256, 256, 256), :] = block_rows.astype(low)

        rotate(buffer, length - offset, length, put)

    unrotate(dk_rot, dk_ref)
    unrotate(dv_rot, dv_ref)
    dq_turned[0 : length // 8] = jnp.transpose(dq_side[...] * SCALE).reshape(length // 8, 8, width)
    unrotate(dq_turned, dq_ref)
    events.end()
    keeps = []
    for index, target in enumerate((up_sum, up_sum, down_sum, down_sum)):
        lanes = pl.ds((index % 2) * lanes_of, lanes_of)
        keeps.append(pltpu.make_async_copy(wires.at[index], target.at[:, lanes], keep_sems.at[index]))
    for keep in keeps:
        keep.start()
    wo_across.wait()
    mine = wo_part[wo_rows(team.me), :].astype(full) + wo_near[0].astype(full)
    wo_sum[...] = (mine + wo_far[1].astype(full)).astype(low)
    out_copy.wait()
    for keep in keeps:
        keep.wait()


def attend_backward(
    size, spans, q_rot, k_rot, v_rot, grad_mixed, mixed_rot, log_totals, up_part, down_part, wo_part, out_far
):
    length, width = q_rot.shape
    head_count = width // HEAD
    low, full = jnp.bfloat16, jnp.float32
    half = (up_part.shape[0], up_part.shape[1] // 2)
    whole = (2 * up_part.shape[0], up_part.shape[1])
    wo_shape = (wo_part.shape[0] // 4, wo_part.shape[1])

    def shape(dims):
        return jax.ShapeDtypeStruct(dims, low)

    grouped = (length // 8 + EXTRA, 8, width)
    return pl.pallas_call(
        functools.partial(backward_kernel, 256, 512, head_count, size),
        out_shape=(shape((length, width)),) * 3
        + (shape(whole), shape(whole), shape(wo_shape), shape(out_far.shape)),
        in_specs=[SMEM] + [VMEM] * 6 + [ANY, ANY, VMEM, ANY],
        out_specs=(VMEM,) * 3 + (ANY, ANY, VMEM, ANY),
        scratch_shapes=[
            pltpu.VMEM((length, width), low),
            pltpu.VMEM((width, length), low),
            pltpu.VMEM((width, length), low),
            pltpu.VMEM((width, length), low),
            pltpu.VMEM((head_count, length, width), low),
            pltpu.VMEM((head_count, length, width), low),
            pltpu.VMEM(grouped, full),
            pltpu.VMEM(grouped, full),
            pltpu.VMEM(grouped, full),
            pltpu.VMEM((8, length), full),
            pltpu.VMEM((8, length), full),
            pltpu.VMEM((4, *half), full),
            pltpu.VMEM((4, 2 * half[0], half[1]), low),
            [halving_scratch(size, *half) for unused in range(4)],
            pltpu.VMEM((2, *wo_shape), low),
            pltpu.VMEM((2, *wo_shape), low),
            DMA((2, 3)),
            DMA((2,)),
            DMA((4,)),
            pltpu.VMEM((width, length), full),
        ],
        compiler_params=pltpu.CompilerParams(
            collective_id=3, has_side_effects=True, vmem_limit_bytes=63 << 20
        ),
        name="attend_backward",
    )(spans, q_rot, k_rot, v_rot, grad_mixed, mixed_rot, log_totals, up_part, down_part, wo_part, out_far)


def project_kernel(
    part,
    x_ref,
    gain,
    shift,
    wq,
    bq,
    wk,
    wv,
    bv,
    x_all,
    normed,
    q_ref,
    k_ref,
    v_ref,
    landing,
    far_send,
    far_recv,
    near_send,
    near_recv,
    pass_send,
    pass_recv,
    keep_sem,
):
    team = Team()
    own = x_ref.shape[0]
    count = own // part

    def piece(owner, index):
        return rows_at(owner * own + index * part, part, part)

    def far_copy(index):
        source = x_ref.at[rows_at(index * part, part, part)]
        return team.copy(
            source, landing.at[piece(team.me, index)], far_send.at[index], far_recv.at[index], team.far
        )

    def pass_copy(index):
        place = landing.at[piece(team.far, index)]
        return team.copy(place, place, pass_send.at[index], pass_recv.at[index], team.sibling)

    near = team.copy(
        x_ref, landing.at[rows_at(team.me * own, own, own)], near_send, near_recv, team.sibling
    )

    def keep(owner, source, slot):
        return pltpu.make_async_copy(source, x_all.at[rows_at(owner * own, own, own)], keep_sem.at[slot])

    team.greet((team.sibling, team.far))
    for index in range(count):
        far_copy(index).start()
    near.start()
    keep(team.me, x_ref, 0).start()

    gain_row, shift_row, bq_row, bv_row = as_row(gain), as_row(shift), as_row(bq), as_row(bv)

    def project(owner, index, values):
        standard, unused = standardize(values.astype(FULL))
        low = (standard * gain_row + shift_row).astype(LOW)
        rows = piece(owner, index)
        normed[rows, :] = low
        q_ref[rows, :] = (dot(low, wq[...], NT) + bq_row).astype(LOW)
        k_ref[rows, :] = dot(low, wk[...], NT).astype(LOW)
        v_ref[rows, :] = (dot(low, wv[...], NT) + bv_row).astype(LOW)

    def mine(index, nothing):
        project(team.me, index, x_ref[rows_at(index * part, part, part), :])
        return nothing

    lax.fori_loop(0, count, mine, 0)
    near.wait()

    def next_to(index, nothing):
        project(team.sibling, index, landing[piece(team.sibling, index), :])
        return nothing

    lax.fori_loop(0, count, next_to, 0)

    def across(index, nothing):
        far_copy(index).wait_recv()
        pass_copy(index).start()
        project(team.far, index, landing[piece(team.far, index), :])
        pass_copy(index).wait_recv()
        project(team.diagonal, index, landing[piece(team.diagonal, index), :])
        return nothing

    lax.fori_loop(0, count, across, 0)
    for slot, owner in ((1, team.sibling), (2, team.far), (3, team.diagonal)):
        keep(owner, landing.at[rows_at(owner * own, own, own)], slot).start()
    for slot, owner in ((1, team.sibling), (2, team.far), (3, team.diagonal)):
        keep(owner, landing.at[rows_at(owner * own, own, own)], slot).wait()
    keep(team.me, x_ref, 0).wait()
    for index in range(count):
        far_copy(index).wait_send()
        pass_copy(index).wait_send()


def gather_and_project(x, gain, shift, wq, bq, wk, wv, bv):
    own, width = x.shape
    length, columns, part = 4 * own, wq.shape[0], 128
    count = own // part
    narrow = jax.ShapeDtypeStruct((length, columns), LOW)
    wide = jax.ShapeDtypeStruct((length, width), LOW)
    return pl.pallas_call(
        functools.partial(project_kernel, part),
        out_shape=(wide, wide, narrow, narrow, narrow),
        in_specs=[VMEM] * 8,
        out_specs=(ANY, VMEM, VMEM, VMEM, VMEM),
        scratch_shapes=[
            pltpu.VMEM((length, width), LOW),
            DMA((count,)),
            DMA((count,)),
            DMA,
            DMA,
            DMA((count,)),
            DMA((count,)),
            DMA((4,)),
        ],
        compiler_params=pltpu.CompilerParams(
            collective_id=0, has_side_effects=True, vmem_limit_bytes=48 << 20
        ),
        name="gather_and_project",
    )(x, gain, shift, wq, bq, wk, wv, bv)


class Reduction:
    def __init__(self, team, near_out, near_in, far_out, far_in, sems):
        self.team = team
        self.near_out, self.near_in, self.far_out, self.far_in = near_out, near_in, far_out, far_in
        self.sems = sems

    def near(self, pair):
        return self.team.copy(
            self.near_out.at[pair % 2],
            self.near_in.at[pair],
            self.sems.at[0, pair],
            self.sems.at[1, pair],
            self.team.sibling,
        )

    def across(self, pair):
        return self.team.copy(
            self.far_out.at[pair], self.far_in.at[pair], self.sems.at[2, pair], self.sems.at[3, pair], self.team.far
        )

    def give(self, pair, values):
        @pl.when(pair >= 2)
        def _():
            self.near(pair - 2).wait_send()

        self.near_out[pair % 2] = values.astype(LOW)
        self.near(pair).start()

    def combine(self, pair, values):
        self.near(pair).wait_recv()
        return values + self.near_in[pair].astype(FULL)

    def send(self, pair, values):
        self.far_out[pair] = values.astype(LOW)
        self.across(pair).start()

    def arrived(self, pair):
        self.across(pair).wait_recv()
        return self.far_in[pair].astype(FULL)

    def finish(self, pairs):
        for pair in range(pairs // 2):
            self.across(pair).wait_send()
        for pair in (pairs - 2, pairs - 1):
            self.near(pair).wait_send()


def owner_at(team_me, step):
    half = lax.div(step, 4)
    odd = lax.rem(step, 2)
    one = flip(team_me, 0)
    base = one + odd * (team_me - one)
    return lax.rem(base + 2 * (1 - half), 4)


def part_at(step):
    return lax.rem(lax.div(step, 2), 2)


def ffn_kernel(
    part,
    size,
    mixed_ref,
    pieces,
    x_all,
    cot_ref,
    wo,
    up,
    down,
    up_bias,
    out_bias,
    gain,
    shift,
    down_bias,
    out_far,
    out_own,
    grad_middle,
    grad_mixed,
    up_part,
    down_part,
    grad_wo,
    sums,
    middle_own,
    up_half,
    down_half,
    halves_out,
    halves_in,
    half_sems,
    halving_parts,
    keep_sems,
    cot_all,
    normed_all,
    hidden_all,
    gpre_all,
    out_slots,
    out_near,
    own_sum,
    near_out,
    near_in,
    far_out,
    far_in,
    mixed_out,
    branch_own,
    cot_sems,
    slot_sems,
    red_sems,
    a2a_sems,
):
    team = Team()
    length = mixed_ref.shape[0]
    width = x_all.shape[1]
    columns = mixed_ref.shape[1]
    own = length // 4
    steps = length // part

    def rows_of(owner, index):
        return rows_at(owner * own + index * part, part, part)

    def step_rows(device, step):
        return rows_of(owner_at(device, step), part_at(step))

    spreads = [
        Spread(
            team,
            cot_ref.at[pl.ds(index * part, part)],
            cot_all,
            lambda owner, index=index: rows_of(owner, index),
            cot_sems.at[index],
        )
        for index in range(own // part)
    ]
    reduction = Reduction(team, near_out, near_in, far_out, far_in, red_sems)

    def slot_copy(pair):
        slot = lax.rem(pair, 2)
        return team.copy(
            out_slots.at[slot], out_near.at[pair], slot_sems.at[0, slot], slot_sems.at[1, pair], team.sibling
        )

    plane = Plane(size)
    team.greet((team.sibling, team.far, team.diagonal), *[plane.partner(bit) for bit in range(3)])

    for spread in spreads:
        spread.start()
    sums[...] = jnp.zeros_like(sums)
    gain_row, shift_row, bias_row = as_row(gain), as_row(shift), as_row(out_bias)
    up_row, down_row = as_row(up_bias), as_row(down_bias)

    def forward(step, keep_middle):
        rows = step_rows(team.me, step)

        def weights(owner):
            return wo[rows_at(owner * columns, columns, 64), :]

        branch = dot(mixed_ref[rows, :], weights(team.me), NN)
        branch = branch + dot(pieces[0, rows, :], weights(team.sibling), NN)
        branch = branch + dot(pieces[1, rows, :], weights(team.far), NN)
        branch = branch + dot(pieces[2, rows, :], weights(team.diagonal), NN)
        middle = x_all[rows, :].astype(FULL) + (branch + bias_row)
        if keep_middle:

            @pl.when(step >= steps // 2)
            def _():
                middle_own[rows_at(part_at(step) * part, part, part), :] = middle

        standard, unused = standardize(middle)
        low = (standard * gain_row + shift_row).astype(LOW)
        normed_all[rows, :] = low
        pre = dot(low, up[...], NN) + up_row
        bell = 0.5 * (1.0 + lax.erf(pre * 0.7071067811865476))
        hidden = (pre * bell).astype(LOW)
        hidden_all[rows, :] = hidden
        slope = bell + pre * (jnp.exp(pre * pre * -0.5) * 0.3989422804014327)
        gpre_all[rows, :] = slope.astype(LOW)

        out = dot(hidden, down[...], NN)
        pair = lax.div(step, 2)
        if keep_middle:
            place = rows_at(part_at(step) * part, part, part)

            @pl.when(step < steps // 2)
            def _():
                out_far[place, :] = out.astype(LOW)

            @pl.when(step >= steps // 2)
            def _():
                out_own[place, :] = middle + out + down_row
        else:

            @pl.when(pair >= 2)
            def _():
                slot_copy(pair - 2).wait_send()

            out_slots[lax.rem(pair, 2)] = out.astype(LOW)
            slot_copy(pair).start()
    def backward(step):
        rows = step_rows(team.me, step)
        slope = gpre_all[rows, :].astype(FULL)
        grad_pre = (dot(cot_all[rows, :], down[...], NT) * slope).astype(LOW)
        gpre_all[rows, :] = grad_pre
        sums[4:5, :] += column_sums(grad_pre.astype(FULL))
        return dot(grad_pre, up[...], NT)

    def pair_forward(pair, nothing):
        forward(2 * pair, False)
        forward(2 * pair + 1, True)
        return nothing

    half = width // 2
    down_total = Halving(plane, down_half, None, 0, *halving_parts)
    up_keep = pltpu.make_async_copy(up_half, up_part, keep_sems.at[0])
    down_keep = pltpu.make_async_copy(down_half.at[down_total.inner(2)], down_part, keep_sems.at[1])
    halves = (normed_all, gpre_all, up_half), (hidden_all, cot_all, down_half)
    side_copies = [
        plane.remote(halves_out.at[index], halves_in.at[index], half_sems, index, plane.partner(0))
        for index in range(2)
    ]
    def place_of(pair):
        return rows_at(part_at(2 * pair) * part, part, part)

    def add_out(pair):
        slot_copy(pair).wait_recv()
        place, given = place_of(pair), out_near[pair].astype(FULL)

        @pl.when(pair < steps // 4)
        def _():
            out_far[place, :] = (out_far[place, :].astype(FULL) + given).astype(LOW)

        @pl.when(pair >= steps // 4)
        def _():
            out_own[place, :] += given

    def combine(pair):
        reduction.near(pair).wait_recv()
        given = reduction.near_in[pair].astype(FULL)

        @pl.when(pair < steps // 4)
        def _():
            reduction.send(pair, reduction.far_out[lax.rem(pair, 2)].astype(FULL) + given)

        @pl.when(pair >= steps // 4)
        def _():
            own_sum[place_of(pair), :] += given

    def pair_backward(pair, nothing):
        first, second = 2 * pair, 2 * pair + 1
        for index, spread in enumerate(spreads):

            @pl.when(pair == index)
            def _(spread=spread):
                spread.middle()
                spread.passed().wait_recv()

        @pl.when(pair == len(spreads))
        def _():
            for spread in spreads:
                spread.near().wait_recv()
                spread.kept().wait()
            side_half(1)

        @pl.when(pair == len(spreads) + 1)
        def _():
            own_half(1)

        reduction.give(pair, backward(first))
        add_out(pair)

        @pl.when(pair >= 1)
        def _():
            combine(pair - 1)

        values = backward(second)

        @pl.when(pair < steps // 4)
        def _():
            far_out[lax.rem(pair, 2)] = values.astype(LOW)

        @pl.when(pair >= steps // 4)
        def _():
            own_sum[place_of(pair), :] = values

        return nothing

    def side_half(index):
        left, right, unused = halves[index]
        lanes = rows_at((1 - plane.side) * half, half, half)

        def one(slab, nothing):
            columns_of = rows_at(slab * 256, 256, 256)
            halves_out[index, :, columns_of] = dot(left[:, lanes], right[:, columns_of], TN).astype(LOW)
            return nothing

        lax.fori_loop(0, width // 256, one, 0)
        side_copies[index].start()

    def own_half(index):
        left, right, target = halves[index]
        lanes = rows_at(plane.side * half, half, half)

        def one(slab, nothing):
            columns_of = rows_at(slab * 256, 256, 256)
            target[:, columns_of] = dot(left[:, lanes], right[:, columns_of], TN)
            return nothing

        lax.fori_loop(0, width // 256, one, 0)

    def add_side(index):
        side_copies[index].wait()
        halves[index][2][...] += halves_in[index].astype(FULL)

    lax.fori_loop(0, steps // 2, pair_forward, 0)
    lax.fori_loop(0, steps // 2, pair_backward, 0)
    side_half(0)
    add_side(1)
    down_total.start(0)
    combine(steps // 2 - 1)

    def back(index, nothing):
        @pl.when(index == 1)
        def _():
            down_total.finish(0)
            down_total.start(1)

        rows = rows_at(index * part, part, part)
        own_rows = rows_of(team.me, index)
        grad = own_sum[rows, :] + reduction.arrived(index)
        standard, inverse = standardize(middle_own[rows, :])
        incoming = cot_all[own_rows, :].astype(FULL)
        grad_mid = incoming + norm_back(grad, gain_row, standard, inverse)
        grad_middle[rows, :] = grad_mid
        branch_low = grad_mid.astype(LOW)
        branch_own[rows, :] = branch_low
        for slot, owner in enumerate((team.sibling, team.far, team.diagonal)):
            side = wo[rows_at(owner * columns, columns, 64), :]
            mixed_out[slot, rows, :] = dot(branch_low, side, NT).astype(LOW)
            exchange(index, slot, owner).start()
        side = wo[rows_at(team.me * columns, columns, 64), :]
        grad_mixed[own_rows, :] = dot(branch_low, side, NT).astype(LOW)
        sums[0:1, :] += column_sums(grad * standard)
        sums[1:2, :] += column_sums(grad)
        sums[2:3, :] += column_sums(branch_low.astype(FULL))
        sums[3:4, :] += column_sums(incoming)
        return nothing

    def exchange(index, slot, owner):
        return team.copy(
            mixed_out.at[slot, rows_at(index * part, part, part)],
            grad_mixed.at[rows_of(team.me, index)],
            a2a_sems.at[2 * index, slot],
            a2a_sems.at[2 * index + 1, slot],
            owner,
        )

    lax.fori_loop(0, own // part, back, 0)
    own_half(0)
    own_rows = rows_at(team.me * own, own, own)
    for source, owner in (
        (mixed_ref.at[own_rows], team.me),
        (pieces.at[0, own_rows], team.sibling),
        (pieces.at[1, own_rows], team.far),
        (pieces.at[2, own_rows], team.diagonal),
    ):
        grad_wo[rows_at(owner * columns, columns, 64), :] = dot(source[...], branch_own[...], TN).astype(LOW)
    down_total.finish(1)
    down_keep.start()
    add_side(0)
    up_keep.start()
    for index in range(own // part):
        for slot, owner in enumerate((team.sibling, team.far, team.diagonal)):
            exchange(index, slot, owner).wait()
    down_keep.wait()
    up_keep.wait()
    for spread in spreads:
        spread.sent()
    for pair in (steps // 2 - 2, steps // 2 - 1):
        slot_copy(pair).wait_send()
    reduction.finish(steps // 2)


def ffn(size, mixed, pieces, x_all, cotangent, wo, up, down, up_bias, out_bias, gain, shift, down_bias):
    length, columns = mixed.shape
    width = x_all.shape[1]
    hidden = up.shape[1]
    own, part = length // 4, 320
    steps = length // part
    pairs = steps // 2

    def shape(dims, kind):
        return jax.ShapeDtypeStruct(dims, kind)

    return pl.pallas_call(
        functools.partial(ffn_kernel, part, size),
        out_shape=(
            shape((own, width), LOW),
            shape((own, width), FULL),
            shape((own, width), FULL),
            shape((length, columns), LOW),
            shape((width // 2, hidden), FULL),
            shape((hidden // 8, width), FULL),
            shape((width, width), LOW),
            shape((8, width), FULL),
        ),
        in_specs=[VMEM] * 12,
        out_specs=(VMEM,) * 4 + (ANY, ANY, VMEM, VMEM),
        scratch_shapes=[
            pltpu.VMEM((own, width), FULL),
            pltpu.VMEM((width // 2, hidden), FULL),
            pltpu.VMEM((hidden // 2, width), FULL),
            pltpu.VMEM((2, width // 2, width), LOW),
            pltpu.VMEM((2, width // 2, width), LOW),
            DMA((2, 2)),
            halving_scratch(size, width // 2, width),
            DMA((2,)),
            pltpu.VMEM((length, width), LOW),
            pltpu.VMEM((length, width), LOW),
            pltpu.VMEM((length, hidden), LOW),
            pltpu.VMEM((length, hidden), LOW),
            pltpu.VMEM((2, part, width), LOW),
            pltpu.VMEM((pairs, part, width), LOW),
            pltpu.VMEM((own, width), FULL),
            pltpu.VMEM((2, part, width), LOW),
            pltpu.VMEM((pairs, part, width), LOW),
            pltpu.VMEM((pairs // 2, part, width), LOW),
            pltpu.VMEM((pairs // 2, part, width), LOW),
            pltpu.VMEM((3, own, columns), LOW),
            pltpu.VMEM((own, width), LOW),
            DMA((own // part, 7)),
            DMA((2, pairs)),
            DMA((4, pairs)),
            DMA((4, 3)),
        ],
        compiler_params=pltpu.CompilerParams(
            collective_id=2, has_side_effects=True, vmem_limit_bytes=63 << 20
        ),
        name="ffn",
    )(mixed, pieces, x_all, cotangent, wo, up, down, up_bias, out_bias, gain, shift, down_bias)


def last_kernel(
    part,
    size,
    dq_ref,
    dk_ref,
    dv_ref,
    wq,
    wk,
    wv,
    normed_all,
    x_all,
    grad_middle,
    gain,
    wo_sum,
    wide,
    input_grad,
    grad_sum,
    vectors,
    own_grad,
    near_out,
    near_in,
    far_out,
    far_in,
    red_sems,
    sources,
    wires,
    total_parts,
    packed,
    packed_in,
    vec_sems,
    keep_sems,
):
    team, plane = Team(), Plane(size)
    length, columns = dq_ref.shape
    width = normed_all.shape[1]
    own = length // 4
    pairs = length // part // 2
    grads = Reduction(team, near_out, near_in, far_out, far_in, red_sems)
    slabs = sources.shape[0]
    lanes_of = width // slabs
    totals = [Direct(plane, sources.at[slab], wires.at[slab], *total_parts[slab]) for slab in range(slabs)]
    others = greet_all(team, plane, True)
    events = Events(totals)

    def slab_grads(slab, nothing):
        lanes = rows_at(slab * lanes_of, lanes_of, lanes_of)
        for index, source in enumerate((dq_ref, dk_ref, dv_ref)):
            value = dot(source[...], normed_all[:, lanes], TN)
            sources[slab, index * columns : (index + 1) * columns, :] = value.astype(LOW)
        sources[slab, 3 * columns : 4 * columns, :] = wo_sum[:, lanes]
        for index, total in enumerate(totals):

            @pl.when(slab == index)
            def _(total=total):
                total.start(0)

        return nothing

    lax.fori_loop(0, slabs, slab_grads, 0)
    gain_row = as_row(gain)
    packed[...] = jnp.zeros_like(packed)
    packed[0:4, :] = wide[0:4, :]
    packed[8:9, :] = wide[4:5, :]
    packed[9:10, 0:columns] = column_sums(dq_ref[...].astype(FULL))
    packed[10:11, 0:columns] = column_sums(dv_ref[...].astype(FULL))

    def step_rows(step):
        return rows_at(owner_at(team.me, step) * own + part_at(step) * part, part, part)

    def compute(step):
        rows = step_rows(step)
        total = dot(dq_ref[rows, :], wq[...], NN) + dot(dk_ref[rows, :], wk[...], NN)
        return total + dot(dv_ref[rows, :], wv[...], NN)

    everything = list(events.waiting)

    def events_at(pair, plan):
        for when, (start, stop) in plan.items():

            @pl.when(pair == when)
            def _(start=start, stop=stop):
                events.waiting = everything[start:stop]
                events.take(1 << 20)

    def pair_step(pair, nothing):
        first, second = 2 * pair, 2 * pair + 1
        grads.give(pair, compute(first))
        standard, unused = standardize(x_all[step_rows(second), :].astype(FULL))
        events_at(pair, {1: (0, 1), 2: (1, 2), 3: (3, 4)})
        values = grads.combine(pair, compute(second))
        packed[4:5, :] += column_sums(values * standard)
        packed[5:6, :] += column_sums(values)

        @pl.when(pair < pairs // 2)
        def _():
            grads.send(pair, values)

        @pl.when(pair >= pairs // 2)
        def _():
            own_grad[rows_at(part_at(second) * part, part, part), :] = values

        events_at(pair, {2: (2, 3), 3: (4, 5)})
        return nothing

    lax.fori_loop(0, pairs, pair_step, 0)
    events.waiting = everything[5:]

    def vector_copy(step):
        return pltpu.make_async_remote_copy(
            src_ref=packed.at[pl.ds(16 * step, 16)],
            dst_ref=packed_in.at[step],
            send_sem=vec_sems.at[0, step],
            recv_sem=vec_sems.at[1, step],
            device_id=others[step],
            device_id_type=MESH,
        )

    def finish_rows(index):
        rows = pl.ds(index * part, part)
        grad = own_grad[rows, :] + grads.arrived(index)
        standard, inverse = standardize(x_all[rows_at(team.me * own + index * part, part, part), :].astype(FULL))
        input_grad[rows, :] = grad_middle[rows, :] + norm_back(grad, gain_row, standard, inverse)

    for step in range(len(others)):
        vector_copy(step).start()
        events.next(1)
        vector_copy(step).wait()
        here = packed[16 * step : 16 * (step + 1), :]
        keep = 16 if step < plane.bits else 8
        row = lax.broadcasted_iota(jnp.int32, here.shape, 0)
        added = here + jnp.where(row < keep, packed_in[step], 0.0)
        packed[16 * (step + 1) : 16 * (step + 2), :] = added
    vectors[...] = packed[16 * len(others) : 16 * (len(others) + 1), :]
    events.take(1 << 20)
    for index in range(own // part):
        finish_rows(index)
    events.end()
    keeps = []
    for slab in range(slabs):
        lanes = pl.ds(slab * lanes_of, lanes_of)
        keeps.append(pltpu.make_async_copy(wires.at[slab], grad_sum.at[:, lanes], keep_sems.at[slab]))
    for keep in keeps:
        keep.start()
    for keep in keeps:
        keep.wait()
    grads.finish(pairs)


def last(size, dq, dk, dv, wq, wk, wv, normed_all, x_all, grad_middle, gain, wo_sum, wide):
    length, columns = dq.shape
    own, width = grad_middle.shape
    part, slabs = 320, 3
    pairs = length // part // 2
    bits = size.bit_length() - 1
    slab = (4 * columns, width // slabs)

    def shape(dims, kind):
        return jax.ShapeDtypeStruct(dims, kind)

    return pl.pallas_call(
        functools.partial(last_kernel, part, size),
        out_shape=(
            shape((own, width), FULL),
            shape((4 * columns, width), LOW),
            shape((16, width), FULL),
        ),
        in_specs=[VMEM] * 12,
        out_specs=(VMEM, ANY, VMEM),
        scratch_shapes=[
            pltpu.VMEM((own, width), FULL),
            pltpu.VMEM((2, part, width), LOW),
            pltpu.VMEM((pairs, part, width), LOW),
            pltpu.VMEM((pairs // 2, part, width), LOW),
            pltpu.VMEM((pairs // 2, part, width), LOW),
            DMA((4, pairs)),
            pltpu.VMEM((slabs, *slab), LOW),
            pltpu.VMEM((slabs, *slab), LOW),
            [direct_scratch(size, *slab) for unused in range(slabs)],
            pltpu.VMEM((16 * (bits + 3), width), FULL),
            pltpu.VMEM((bits + 2, 16, width), FULL),
            DMA((2, bits + 2)),
            DMA((slabs,)),
        ],
        compiler_params=pltpu.CompilerParams(
            collective_id=4, has_side_effects=True, vmem_limit_bytes=60 << 20
        ),
        name="last",
    )(dq, dk, dv, wq, wk, wv, normed_all, x_all, grad_middle, gain, wo_sum, wide)


def local(
    size,
    layer_input,
    segment_ids,
    cotangent,
    attn_gain,
    attn_shift,
    query_weight,
    query_bias,
    key_weight,
    value_weight,
    value_bias,
    out_weight,
    out_bias,
    ffn_gain,
    ffn_shift,
    up_weight,
    up_bias,
    down_weight,
    down_bias,
):
    query_side, key_side, value_side = query_weight.T, key_weight.T, value_weight.T
    x_all, normed_rows, queries, key_rows, value_rows = gather_and_project(
        layer_input,
        attn_gain,
        attn_shift,
        query_side,
        query_bias,
        key_side,
        value_side,
        value_bias,
    )
    mixed, mixed_rot, log_totals, pieces, out_all, q_rot, k_rot, v_rot = attend_forward(
        segment_ids, queries, key_rows, value_rows, out_weight
    )
    out_far, out_own, grad_middle, grad_mixed, up_part, down_part, out_part, sums = ffn(
        size,
        mixed,
        pieces,
        x_all,
        cotangent,
        out_all,
        up_weight,
        down_weight,
        up_bias,
        out_bias,
        ffn_gain,
        ffn_shift,
        down_bias,
    )
    dq, dk, dv, grad_up, grad_down, wo_sum, out_in = attend_backward(
        size, segment_ids, q_rot, k_rot, v_rot, grad_mixed, mixed_rot, log_totals, up_part, down_part, out_part, out_far
    )
    layer_output = (out_own + out_in.astype(FULL)).astype(LOW)
    input_grad, grads, vectors = last(
        size,
        dq,
        dk,
        dv,
        query_side,
        key_side,
        value_side,
        normed_rows,
        x_all,
        grad_middle,
        attn_gain,
        wo_sum,
        sums,
    )
    columns = query_side.shape[0]
    grads = grads.astype(FULL)
    return (
        layer_output,
        input_grad,
        vectors[4],
        vectors[5],
        grads[0:columns].T,
        vectors[9, 0:columns],
        grads[columns : 2 * columns].T,
        grads[2 * columns : 3 * columns].T,
        vectors[10, 0:columns],
        grads[3 * columns :],
        vectors[2],
        vectors[0],
        vectors[1],
        grad_up.astype(FULL),
        vectors[8],
        grad_down.astype(FULL),
        vectors[3],
    )


def solution(mesh):
    return jax.shard_map(
        functools.partial(local, mesh.shape["dp"]),
        mesh=mesh,
        in_specs=(
            P(("dp", "seq"), None),
            P("dp", None),
            P(("dp", "seq"), None),
            P(),
            P(),
            P(None, "seq"),
            P("seq"),
            P(None, "seq"),
            P(None, "seq"),
            P("seq"),
            P("seq", None),
            P(),
            P(),
            P(),
            P(None, "seq"),
            P("seq"),
            P("seq", None),
            P(),
        ),
        out_specs=(
            P(("dp", "seq"), None),
            P(("dp", "seq"), None),
            P(),
            P(),
            P(None, "seq"),
            P("seq"),
            P(None, "seq"),
            P(None, "seq"),
            P("seq"),
            P("seq", None),
            P(),
            P(),
            P(),
            P(None, "seq"),
            P("seq"),
            P("seq", None),
            P(),
        ),
        check_vma=False,
    )
```

```python
import functools

import jax
import jax.numpy as jnp
from jax import lax
from jax.experimental import pallas as pl
from jax.experimental.pallas import tpu as pltpu
from jax.sharding import PartitionSpec as P

HEAD = 64
SCALE = HEAD ** (-0.5)
LOG_SCALE = SCALE * 1.4426950408889634
LONGEST = 2048
EPSILON = 1e-06
NN = (((1,), (0,)), ((), ()))
NT = (((1,), (1,)), ((), ()))
TN = (((0,), (0,)), ((), ()))
MESH = pl.DeviceIdType.MESH
LOW = jnp.bfloat16
FULL = jnp.float32
VMEM = pl.BlockSpec(memory_space=pltpu.VMEM)
SMEM = pl.BlockSpec(memory_space=pltpu.SMEM)
ANY = pl.BlockSpec(memory_space=pl.ANY)
DMA = pltpu.SemaphoreType.DMA


def flip(index, bit):
    size = 1 << bit
    return index + size - 2 * size * lax.rem(lax.div(index, size), 2)


class Team:
    def __init__(self):
        self.row = lax.axis_index("dp")
        self.me = lax.axis_index("seq")
        self.sibling = flip(self.me, 0)
        self.far = flip(self.me, 1)
        self.diagonal = flip(self.sibling, 1)

    def device(self, index):
        return (self.row, index)

    def greet(self, others, *more):
        barrier = pltpu.get_barrier_semaphore()
        devices = [self.device(other) for other in others] + list(more)
        for device in devices:
            pl.semaphore_signal(barrier, inc=1, device_id=device, device_id_type=MESH)
        pl.semaphore_wait(barrier, len(devices))

    def copy(self, source, target, send, receive, other):
        return pltpu.make_async_remote_copy(
            src_ref=source,
            dst_ref=target,
            send_sem=send,
            recv_sem=receive,
            device_id=self.device(other),
            device_id_type=MESH,
        )


def loads_of(pairs, sems):
    return [pltpu.make_async_copy(source, target, sems.at[index]) for index, (source, target) in enumerate(pairs)]


def rows_at(start, count, multiple):
    return pl.ds(pl.multiple_of(start, multiple), count)


def standardize(values):
    average = jnp.mean(values, axis=-1, keepdims=True)
    centered = values - average
    variance = jnp.mean(centered * centered, axis=-1, keepdims=True)
    inverse = lax.rsqrt(variance + EPSILON)
    return centered * inverse, inverse


def norm_back(grad, gain_row, standard, inverse):
    scaled = grad * gain_row
    mean_one = jnp.mean(scaled, axis=-1, keepdims=True)
    mean_two = jnp.mean(scaled * standard, axis=-1, keepdims=True)
    return inverse * (scaled - mean_one - standard * mean_two)


def column_sums(values):
    return jnp.sum(values, axis=0, keepdims=True)


def first_at_least(segments, value):
    length = segments.shape[1]

    def halve(unused, ends):
        low, high = ends
        middle = jnp.minimum(lax.div(low + high, 2), length - 1)
        below = segments[0, middle] < value
        open_yet = low < high
        return (
            jnp.where(open_yet & below, middle + 1, low),
            jnp.where(open_yet & jnp.logical_not(below), middle, high),
        )

    return lax.fori_loop(0, length.bit_length(), halve, (jnp.int32(0), jnp.int32(length)))[0]


def rotation(segments):
    length = segments.shape[1]
    one, two = first_at_least(segments, 1), first_at_least(segments, 2)
    offset = jnp.where(one == LONGEST, 0, jnp.where(two - one == LONGEST, one, two))
    border = jnp.where(one == LONGEST, two - one, jnp.where(two - one == LONGEST, length - two, one))
    return offset, border


def as_row(ref):
    return ref[...].astype(FULL).reshape(1, -1)


def dot(left_side, right_side, dims):
    return lax.dot_general(left_side, right_side, dims, preferred_element_type=jnp.float32)


def keep_head(head, values):
    lane = lax.broadcasted_iota(jnp.int32, values.shape, 1)
    inside = (lane >= head * HEAD) & (lane < (head + 1) * HEAD)
    return jnp.where(inside, values, jnp.zeros_like(values))


class Spread:
    def __init__(self, team, source, target, rows_of, sems):
        self.team, self.source, self.target, self.rows_of, self.sems = team, source, target, rows_of, sems

    def place(self, owner):
        return self.target.at[self.rows_of(owner)]

    def across(self):
        here = self.place(self.team.me)
        return self.team.copy(self.source, here, self.sems.at[0], self.sems.at[1], self.team.far)

    def near(self):
        here = self.place(self.team.me)
        return self.team.copy(self.source, here, self.sems.at[2], self.sems.at[3], self.team.sibling)

    def passed(self):
        there = self.place(self.team.far)
        return self.team.copy(there, there, self.sems.at[4], self.sems.at[5], self.team.sibling)

    def kept(self):
        return pltpu.make_async_copy(self.source, self.place(self.team.me), self.sems.at[6])

    def start(self):
        self.across().start()
        self.near().start()
        self.kept().start()

    def middle(self):
        self.across().wait_recv()
        self.passed().start()

    def sent(self):
        self.across().wait_send()
        self.near().wait_send()
        self.passed().wait_send()


EXTRA = 72


def rotated_block(ref, shift, length, index):
    width = ref.shape[2]
    sub = lax.broadcasted_iota(jnp.int32, (32, 8, width), 1)
    start = lax.rem(shift + index * 256, length)
    group = lax.div(start, 8)
    skip = start - group * 8
    turned = pltpu.roll(ref[pl.ds(group, 33)], lax.rem(8 - skip, 8), 1)
    return jnp.where(sub < 8 - skip, turned[:32], turned[1:]).reshape(256, width)


def rotate(ref, shift, length, put):
    def one(index, nothing):
        put(index, rotated_block(ref, shift, length, index))
        return nothing

    lax.fori_loop(0, length // 256, one, 0)


def wrap(ref, length):
    ref[length // 8 : length // 8 + EXTRA] = ref[0:EXTRA]


def rotate_into(source, target, buffer, shift):
    length, width = source.shape
    buffer[0 : length // 8] = source[...].astype(FULL).reshape(length // 8, 8, width)
    wrap(buffer, length)

    def put(index, block):
        target[rows_at(index * 256, 256, 256), :] = block.astype(LOW)

    rotate(buffer, shift, length, put)


def forward_kernel(
    rows_of,
    keys_of,
    head_count,
    spans,
    q_ref,
    k_ref,
    v_ref,
    wo_ref,
    mixed_ref,
    mixed_rot_ref,
    log_ref,
    pieces,
    wo_all,
    q_rot,
    k_rot,
    v_rot,
    v_heads,
    buffer,
    wo_sems,
    far_sems,
    near_sems,
    pass_sems,
):
    length, width = q_ref.shape
    team = Team()
    spread = Spread(team, wo_ref, wo_all, lambda owner: rows_at(owner * width, width, 64), wo_sems)

    def far_copy(index):
        rows = rows_at(index * 256, 256, 256)
        return team.copy(
            mixed_ref.at[rows], pieces.at[1, rows], far_sems.at[0, index], far_sems.at[1, index], team.far
        )

    def near_copy(index):
        rows = rows_at(index * 256, 256, 256)
        return team.copy(
            mixed_ref.at[rows], pieces.at[0, rows], near_sems.at[0, index], near_sems.at[1, index], team.sibling
        )

    def pass_copy(index):
        rows = rows_at(index * 256, 256, 256)
        return team.copy(
            pieces.at[1, rows], pieces.at[2, rows], pass_sems.at[0, index], pass_sems.at[1, index], team.sibling
        )

    team.greet((team.sibling, team.far))
    spread.start()
    small = length - LONGEST
    offset, border = rotation(spans)

    rotate_into(q_ref, q_rot, buffer, offset)
    rotate_into(k_ref, k_rot, buffer, offset)
    rotate_into(v_ref, v_rot, buffer, offset)
    v_all = v_rot[...]
    for head in range(head_count):
        v_heads[head] = jnp.concatenate(
            [keep_head(head, v_all), jnp.full((length, 256 - width), 1, jnp.bfloat16)], axis=1
        )

    def block(row, key_base, key_count, masked):
        rows = pl.ds(row, rows_of)
        total = jnp.zeros((rows_of, width), jnp.float32)
        logs = []
        for head in range(head_count):
            q_head = keep_head(head, q_rot[rows, :])
            top, parts = None, []
            for chunk in range(key_count // keys_of):
                keys = pl.ds(key_base + chunk * keys_of, keys_of)
                scores = dot(q_head, k_rot[keys, :], NT)
                if masked:
                    shape = (rows_of, keys_of)
                    row_id = lax.broadcasted_iota(jnp.int32, shape, 0) + (row - LONGEST)
                    key_id = lax.broadcasted_iota(jnp.int32, shape, 1) + chunk * keys_of
                    scores = jnp.where((row_id < border) == (key_id < border), scores, -1e30)
                high = jnp.max(scores, axis=1, keepdims=True)
                top = high if top is None else jnp.maximum(top, high)
                parts.append(scores)
            summed = jnp.zeros((rows_of, 256), jnp.float32)
            for chunk, scores in enumerate(parts):
                keys = pl.ds(key_base + chunk * keys_of, keys_of)
                weights = jnp.exp2((scores - top) * LOG_SCALE).astype(jnp.bfloat16)
                summed = summed + dot(weights, v_heads[head, keys, :], NN)
            norm = summed[:, 255:256]
            total = total + summed[:, :width] * (1.0 / norm)
            logs.append(top * LOG_SCALE + jnp.log2(norm))
        mixed_rot_ref[pl.ds(lax.div(row, 8), rows_of // 8)] = total.reshape(rows_of // 8, 8, width)
        logs.append(jnp.zeros((rows_of, 128 - head_count), jnp.float32))
        log_ref[rows, :] = jnp.concatenate(logs, axis=1)

    def send(index):
        rows = rows_at(index * 256, 256, 256)
        mixed_ref[rows, :] = rotated_block(mixed_rot_ref, length - offset, length, index).astype(LOW)
        far_copy(index).start()
        near_copy(index).start()

    def pass_on(index):
        far_copy(index).wait_recv()
        pass_copy(index).start()

    def little(index, nothing):
        block(pl.multiple_of(LONGEST + index * rows_of, rows_of), LONGEST, small, True)
        return nothing

    lax.fori_loop(0, small // rows_of, little, 0)
    lag, trips = 2, LONGEST // rows_of

    def large(index, nothing):
        block(pl.multiple_of(index * rows_of, rows_of), 0, LONGEST, False)

        @pl.when(index == 0)
        def _():
            mixed_rot_ref[length // 8 : length // 8 + 32] = mixed_rot_ref[0:32]

        send(index)

        @pl.when(index == trips // 2)
        def _():
            spread.middle()

        @pl.when(index >= lag)
        def _():
            pass_on(index - lag)

        return nothing

    lax.fori_loop(0, trips, large, 0)
    blocks = length // 256
    for index in range(trips, blocks):
        send(index)
    for index in range(trips - lag, blocks):
        pass_on(index)
    for index in range(blocks):
        near_copy(index).wait()
        far_copy(index).wait_send()
        pass_copy(index).wait()
    spread.sent()
    spread.near().wait_recv()
    spread.passed().wait_recv()
    spread.kept().wait()


def attend_forward(spans, queries, key_rows, value_rows, out_weight):
    length, width = queries.shape
    head_count = width // HEAD
    return pl.pallas_call(
        functools.partial(forward_kernel, 256, 512, head_count),
        out_shape=(
            jax.ShapeDtypeStruct((length, width), jnp.bfloat16),
            jax.ShapeDtypeStruct((length // 8 + EXTRA, 8, width), jnp.float32),
            jax.ShapeDtypeStruct((length, 128), jnp.float32),
            jax.ShapeDtypeStruct((3, length, width), LOW),
            jax.ShapeDtypeStruct((4 * out_weight.shape[0], out_weight.shape[1]), LOW),
            jax.ShapeDtypeStruct((length, width), LOW),
            jax.ShapeDtypeStruct((length, width), LOW),
            jax.ShapeDtypeStruct((length, width), LOW),
        ),
        in_specs=[SMEM, VMEM, VMEM, VMEM, VMEM],
        out_specs=(VMEM, VMEM, VMEM, ANY, ANY, VMEM, VMEM, VMEM),
        scratch_shapes=[
            pltpu.VMEM((head_count, length, 256), jnp.bfloat16),
            pltpu.VMEM((length // 8 + EXTRA, 8, width), FULL),
            DMA((7,)),
            DMA((2, length // 256)),
            DMA((2, length // 256)),
            DMA((2, length // 256)),
        ],
        compiler_params=pltpu.CompilerParams(
            collective_id=1, has_side_effects=True, vmem_limit_bytes=60 << 20
        ),
        name="attend_forward",
    )(spans, queries, key_rows, value_rows, out_weight)


class Plane:
    def __init__(self, size):
        self.me, self.lane = lax.axis_index("dp"), lax.axis_index("seq")
        self.size, self.bits = size, size.bit_length() - 1
        self.ranks = min(4, size // 2)
        self.side, self.rank = lax.rem(self.me, 2), lax.rem(lax.div(self.me, 2), self.ranks)
        self.extra = (size // 2 // self.ranks).bit_length() - 1

    def device(self, index):
        return (index, self.lane)

    def partner(self, bit):
        return self.device(flip(self.me, bit))

    def digit(self, bit):
        return lax.rem(lax.div(self.me, 1 << bit), 2)

    def other_rank(self, offset):
        return lax.rem(self.rank + offset, self.ranks)

    def ranked(self, offset):
        return self.device(self.me + 2 * (self.other_rank(offset) - self.rank))

    def remote(self, source, target, sems, index, device):
        return pltpu.make_async_remote_copy(
            src_ref=source,
            dst_ref=target,
            send_sem=sems.at[0, index],
            recv_sem=sems.at[1, index],
            device_id=device,
            device_id_type=MESH,
        )


class Halving:
    def __init__(self, plane, part, wire, first, sends, receives, sems):
        self.plane, self.part, self.wire, self.first = plane, part, wire, first
        self.sends, self.receives, self.sems = sends, receives, sems
        self.halvings, self.whole = halvings_of(plane.bits)
        self.stages = 2 * self.halvings + self.whole + 1
        half = part.shape[0]
        self.bases, self.sizes = [0], [half]
        for level in range(self.halvings):
            size = self.sizes[-1] // 2
            self.bases.append(self.bases[-1] + plane.digit(level + 1) * size)
            self.sizes.append(size)
        self.step = self.sizes[-1]
        self.shift = plane.side * half

    def inner(self, level):
        return rows_at(self.bases[level], self.sizes[level], self.step)

    def place(self, level):
        return rows_at(self.shift + self.bases[level], self.sizes[level], self.step)

    def copies(self, stage):
        plane = self.plane
        if stage < self.halvings + self.whole:
            return [
                plane.remote(self.sends[stage], self.receives[stage], self.sems, stage, plane.partner(stage + 1))
            ]
        level = 2 * self.halvings + self.whole - stage
        here = self.wire.at[self.place(level)]
        return [plane.remote(here, here, self.sems, stage, plane.partner(level))]

    def start(self, stage):
        if stage < self.halvings:
            size = self.sizes[stage + 1]
            first = self.bases[stage] + (1 - self.plane.digit(stage + 1)) * size
            self.sends[stage][...] = self.part[rows_at(first, size, self.step), :].astype(LOW)
        elif stage < self.halvings + self.whole:
            self.sends[stage][...] = self.part[self.inner(self.halvings), :].astype(LOW)
        elif stage == self.halvings + self.whole:
            self.wire[self.place(self.halvings), :] = self.part[self.inner(self.halvings), :].astype(LOW)
        for copy in self.copies(stage):
            copy.start()

    def finish(self, stage):
        for copy in self.copies(stage):
            copy.wait()
        if stage < self.halvings:
            self.part[self.inner(stage + 1), :] += self.receives[stage][...].astype(FULL)
        elif stage < self.halvings + self.whole:
            value = self.sends[stage][...].astype(FULL) + self.receives[stage][...].astype(FULL)
            self.part[self.inner(self.halvings), :] = value


def halvings_of(bits):
    halvings = min(bits - 1, 2)
    return halvings, bits - 1 - halvings


def halving_scratch(size, half, width):
    bits = size.bit_length() - 1
    halvings, whole = halvings_of(bits)
    shapes = [(half >> (stage + 1), width) for stage in range(halvings)] + [(half >> halvings, width)] * whole
    kinds = [pltpu.VMEM(dims, LOW) for dims in shapes]
    return [kinds, list(kinds), DMA((2, 2 * halvings + whole + 1))]


class Direct:
    first = 0

    def __init__(self, plane, source, wire, part, received, sends, receives, sems):
        self.plane, self.source, self.wire, self.part = plane, source, wire, part
        self.received, self.sends, self.receives, self.sems = received, sends, receives, sems
        self.half = source.shape[0] // 2
        self.piece = self.half // plane.ranks
        self.stages = 4 + plane.extra

    def side_rows(self, side):
        return rows_at(side * self.half, self.half, self.half)

    def rank_rows(self, rank):
        return rows_at(rank * self.piece, self.piece, self.piece)

    def own_rows(self):
        start = self.plane.side * self.half + self.plane.rank * self.piece
        return rows_at(start, self.piece, self.piece)

    def copies(self, stage):
        plane = self.plane
        if stage == 0:
            source = self.source.at[self.side_rows(1 - plane.side)]
            return [plane.remote(source, self.received, self.sems, 0, plane.partner(0))]
        if stage == self.stages - 1:
            here = self.wire.at[self.side_rows(plane.side)]
            return [plane.remote(here, here, self.sems, 1, plane.partner(0))]
        if 1 < stage < self.stages - 2:
            slot = plane.ranks + stage - 3
            index = 2 * plane.ranks + stage - 2
            device = plane.partner(plane.bits - plane.extra + stage - 2)
            return [plane.remote(self.sends.at[slot], self.receives.at[slot], self.sems, index, device)]
        copies = []
        for offset in range(1, plane.ranks):
            device = plane.ranked(offset)
            if stage == 1:
                slot = offset - 1
                copies.append(
                    plane.remote(self.sends.at[slot], self.receives.at[slot], self.sems, 1 + offset, device)
                )
            else:
                here = self.wire.at[self.own_rows()]
                copies.append(plane.remote(here, here, self.sems, plane.ranks + offset, device))
        return copies

    def start(self, stage):
        plane = self.plane
        if stage == 1:
            for offset in range(1, plane.ranks):
                rows = self.rank_rows(plane.other_rank(offset))
                self.sends[offset - 1] = self.part[rows, :].astype(LOW)
        elif 1 < stage < self.stages - 2:
            self.sends[plane.ranks + stage - 3] = self.part[self.rank_rows(plane.rank), :].astype(LOW)
        elif stage == self.stages - 2:
            self.wire[self.own_rows(), :] = self.part[self.rank_rows(plane.rank), :].astype(LOW)
        for copy in self.copies(stage):
            copy.start()

    def finish(self, stage):
        plane = self.plane
        for copy in self.copies(stage):
            copy.wait()
        if stage == 0:
            received = self.received[...].astype(FULL)
            self.part[...] = self.source[self.side_rows(plane.side), :].astype(FULL) + received
        elif stage == 1:
            value = self.part[self.rank_rows(plane.rank), :]
            for slot in range(plane.ranks - 1):
                value = value + self.receives[slot].astype(FULL)
            self.part[self.rank_rows(plane.rank), :] = value
        elif stage < self.stages - 2:
            slot = plane.ranks + stage - 3
            value = self.sends[slot].astype(FULL) + self.receives[slot].astype(FULL)
            self.part[self.rank_rows(plane.rank), :] = value


def direct_scratch(size, rows, width):
    ranks = min(4, size // 2)
    extra = (size // 2 // ranks).bit_length() - 1
    half = rows // 2
    pieces = pltpu.VMEM((ranks - 1 + extra, half // ranks, width), LOW)
    return [
        pltpu.VMEM((half, width), FULL),
        pltpu.VMEM((half, width), LOW),
        pieces,
        pieces,
        DMA((2, 2 * ranks + extra)),
    ]


class Events:
    def __init__(self, totals):
        self.totals = totals
        last = totals[0].stages - 1
        self.waiting = sorted(
            (2 * (stage - total.first) + index, index, stage)
            for index, total in enumerate(totals)
            for stage in range(total.first, last)
        )

    def start(self):
        for total in self.totals:
            total.start(total.first)

    def take(self, limit):
        ready = [event for event in self.waiting if event[0] < limit]
        self.waiting = [event for event in self.waiting if event[0] >= limit]
        for unused, index, stage in ready:
            self.totals[index].finish(stage)
            self.totals[index].start(stage + 1)

    def next(self, count):
        if self.waiting[:count]:
            self.take(self.waiting[min(count, len(self.waiting)) - 1][0] + 1)

    def end(self):
        self.take(1 << 20)
        for total in self.totals:
            total.finish(total.stages - 1)


def greet_all(team, plane, direct):
    barrier = pltpu.get_barrier_semaphore()
    others = [plane.partner(bit) for bit in range(plane.bits)]
    others += [team.device(team.sibling), team.device(team.far)]
    greeted = list(others)
    if direct:
        greeted = [plane.partner(0), team.device(team.sibling), team.device(team.far)]
        greeted += [plane.partner(plane.bits - plane.extra + index) for index in range(plane.extra)]
        greeted += [plane.ranked(offset) for offset in range(1, plane.ranks)]
    for other in greeted:
        pl.semaphore_signal(barrier, inc=1, device_id=other, device_id_type=MESH)
    pl.semaphore_wait(barrier, len(greeted))
    return others


def backward_kernel(
    keys_of,
    rows_of,
    head_count,
    size,
    spans,
    q_hbm,
    k_hbm,
    v_hbm,
    d_hbm,
    mixed_hbm,
    log_hbm,
    up_part,
    down_part,
    wo_part,
    out_far,
    dq_ref,
    dk_ref,
    dv_ref,
    up_sum,
    down_sum,
    wo_sum,
    out_in,
    d_rot,
    q_turned,
    d_turned,
    k_turned,
    q_heads,
    d_heads,
    dq_turned,
    dk_rot,
    dv_rot,
    log_rows,
    deltas,
    parts,
    wires,
    total_parts,
    wo_near,
    wo_far,
    wo_sems,
    out_sems,
    keep_sems,
    dq_side,
    q_rot,
    k_rot,
    v_rot,
    d_ref,
    mixed_rot_ref,
    log_ref,
    load_sems,
):
    length, width = q_rot.shape
    small = length - LONGEST
    offset, border = rotation(spans)
    low, full = jnp.bfloat16, jnp.float32
    team, plane = Team(), Plane(size)
    columns = wo_sum.shape[0]
    lanes_of = up_part.shape[1] // 2
    totals, loads = [], []
    for index, source in enumerate((up_part, up_part, down_part, down_part)):
        lanes = pl.ds((index % 2) * lanes_of, lanes_of)
        total = Halving(plane, parts.at[index], wires.at[index], index // 2 * 2, *total_parts[index])
        place = parts.at[index, total.inner(index // 2 * 2)]
        loads.append(pltpu.make_async_copy(source.at[:, lanes], place, keep_sems.at[index]))
        totals.append(total)
    for load in loads:
        load.start()
    events = Events(totals)
    greet_all(team, plane, False)
    for load in loads:
        load.wait()
    events.start()
    arrays = (
        (q_hbm, q_rot),
        (k_hbm, k_rot),
        (v_hbm, v_rot),
        (d_hbm, d_ref),
        (mixed_hbm, mixed_rot_ref),
        (log_hbm, log_ref),
    )
    fetches = loads_of(arrays, load_sems)
    for fetch in fetches:
        fetch.start()
    out_copy = team.copy(out_far, out_in, out_sems.at[0], out_sems.at[1], team.far)
    out_copy.start()

    def wo_rows(owner):
        return rows_at(owner * columns, columns, 64)

    wo_copies = [
        team.copy(wo_part.at[wo_rows(owner)], wo_near.at[slot], wo_sems.at[0, slot], wo_sems.at[1, slot], team.sibling)
        for slot, owner in enumerate((team.sibling, team.diagonal))
    ]
    for copy in wo_copies:
        copy.start()
    wo_across = team.copy(wo_far.at[0], wo_far.at[1], wo_sems.at[0, 2], wo_sems.at[1, 2], team.far)

    for fetch in fetches:
        fetch.wait()
    rotate_into(d_ref, d_rot, dq_turned, offset)
    q_all, k_all, d_all = q_rot[...], k_rot[...], d_rot[...]
    q_turned[...] = jnp.transpose(q_all)
    k_turned[...] = jnp.transpose(k_all)
    d_turned[...] = jnp.transpose(d_all)
    for head in range(head_count):
        q_heads[head] = keep_head(head, q_all)
        d_heads[head] = keep_head(head, d_all)
    products = jnp.transpose(d_all.astype(full) * mixed_rot_ref[0 : length // 8].reshape(length, width))
    for head in range(head_count):
        deltas[head : head + 1, :] = jnp.sum(products[head * HEAD : (head + 1) * HEAD, :], axis=0, keepdims=True)
    log_rows[...] = jnp.transpose(log_ref[...])[0:8, :]
    dq_side[...] = jnp.zeros_like(dq_side)

    def block(key_row, row_base, row_count, masked, before):
        keys = pl.ds(key_row, keys_of)
        dk_sum = jnp.zeros((keys_of, width), full)
        dv_sum = jnp.zeros((keys_of, width), full)
        for head in range(head_count):
            before(head)
            k_head = keep_head(head, k_rot[keys, :])
            v_head = keep_head(head, v_rot[keys, :])
            lanes = slice(head * HEAD, (head + 1) * HEAD)
            k_side = k_turned[lanes, keys]
            for chunk in range(row_count // rows_of):
                start = row_base + chunk * rows_of
                rows = slice(start, start + rows_of)
                scores = dot(k_head, q_turned[:, rows], NN)
                dprobs = dot(v_head, d_turned[:, rows], NN)
                probs = jnp.exp2(scores * LOG_SCALE - log_rows[head : head + 1, rows])
                if masked:
                    shape = (keys_of, rows_of)
                    key_id = lax.broadcasted_iota(jnp.int32, shape, 0) + (key_row - LONGEST)
                    row_id = lax.broadcasted_iota(jnp.int32, shape, 1) + chunk * rows_of
                    probs = jnp.where((row_id < border) == (key_id < border), probs, 0.0)
                dv_sum = dv_sum + dot(probs.astype(low), d_heads[head, rows, :], NN)
                draw = (probs * (dprobs - deltas[head : head + 1, rows])).astype(low)
                dk_sum = dk_sum + dot(draw, q_heads[head, rows, :], NN)
                dq_side[lanes, rows] += dot(k_side, draw, NN)
        groups = pl.ds(lax.div(key_row, 8), keys_of // 8)
        dk_rot[groups] = (dk_sum * SCALE).reshape(keys_of // 8, 8, width)
        dv_rot[groups] = dv_sum.reshape(keys_of // 8, 8, width)

    trips = LONGEST // keys_of

    def gather_wo():
        for copy in wo_copies:
            copy.wait()
        wo_far[0] = (wo_part[wo_rows(team.far), :].astype(full) + wo_near[1].astype(full)).astype(low)
        wo_across.start()

    def large(index, nothing):
        def before(head):
            for trip in range(trips):
                slot = trip * head_count + head
                limit = (slot + 1) // 2
                earlier = slot // 2
                if limit > earlier:

                    @pl.when(index == trip)
                    def _(limit=limit, slot=slot):
                        events.waiting = [event for event in everything if event[0] >= earlier]
                        events.take(limit)
                        if slot == 1:
                            gather_wo()

        block(pl.multiple_of(index * keys_of, keys_of), 0, LONGEST, False, before)
        return nothing

    def little(index, nothing):
        block(
            pl.multiple_of(LONGEST + index * keys_of, keys_of), LONGEST, small, True, lambda head: None
        )
        return nothing

    everything = list(events.waiting)
    lax.fori_loop(0, trips, large, 0)
    slots = trips * head_count
    events.waiting = [event for event in everything if event[0] >= slots // 2]
    lax.fori_loop(0, small // keys_of, little, 0)

    def unrotate(buffer, target):
        wrap(buffer, length)

        def put(index, block_rows):
            target[rows_at(index * 256, 256, 256), :] = block_rows.astype(low)

        rotate(buffer, length - offset, length, put)

    unrotate(dk_rot, dk_ref)
    unrotate(dv_rot, dv_ref)
    dq_turned[0 : length // 8] = jnp.transpose(dq_side[...] * SCALE).reshape(length // 8, 8, width)
    unrotate(dq_turned, dq_ref)
    events.end()
    keeps = []
    for index, target in enumerate((up_sum, up_sum, down_sum, down_sum)):
        lanes = pl.ds((index % 2) * lanes_of, lanes_of)
        keeps.append(pltpu.make_async_copy(wires.at[index], target.at[:, lanes], keep_sems.at[index]))
    for keep in keeps:
        keep.start()
    wo_across.wait()
    mine = wo_part[wo_rows(team.me), :].astype(full) + wo_near[0].astype(full)
    wo_sum[...] = (mine + wo_far[1].astype(full)).astype(low)
    out_copy.wait()
    for keep in keeps:
        keep.wait()


def attend_backward(
    size, spans, q_rot, k_rot, v_rot, grad_mixed, mixed_rot, log_totals, up_part, down_part, wo_part, out_far
):
    length, width = q_rot.shape
    head_count = width // HEAD
    low, full = jnp.bfloat16, jnp.float32
    half = (up_part.shape[0], up_part.shape[1] // 2)
    whole = (2 * up_part.shape[0], up_part.shape[1])
    wo_shape = (wo_part.shape[0] // 4, wo_part.shape[1])

    def shape(dims):
        return jax.ShapeDtypeStruct(dims, low)

    grouped = (length // 8 + EXTRA, 8, width)
    return pl.pallas_call(
        functools.partial(backward_kernel, 256, 512, head_count, size),
        out_shape=(shape((length, width)),) * 3
        + (shape(whole), shape(whole), shape(wo_shape), shape(out_far.shape)),
        in_specs=[SMEM] + [ANY] * 8 + [VMEM, ANY],
        out_specs=(VMEM,) * 3 + (ANY, ANY, VMEM, ANY),
        scratch_shapes=[
            pltpu.VMEM((length, width), low),
            pltpu.VMEM((width, length), low),
            pltpu.VMEM((width, length), low),
            pltpu.VMEM((width, length), low),
            pltpu.VMEM((head_count, length, width), low),
            pltpu.VMEM((head_count, length, width), low),
            pltpu.VMEM(grouped, full),
            pltpu.VMEM(grouped, full),
            pltpu.VMEM(grouped, full),
            pltpu.VMEM((8, length), full),
            pltpu.VMEM((8, length), full),
            pltpu.VMEM((4, *half), full),
            pltpu.VMEM((4, 2 * half[0], half[1]), low),
            [halving_scratch(size, *half) for unused in range(4)],
            pltpu.VMEM((2, *wo_shape), low),
            pltpu.VMEM((2, *wo_shape), low),
            DMA((2, 3)),
            DMA((2,)),
            DMA((4,)),
            pltpu.VMEM((width, length), full),
            pltpu.VMEM((length, width), low),
            pltpu.VMEM((length, width), low),
            pltpu.VMEM((length, width), low),
            pltpu.VMEM((length, width), low),
            pltpu.VMEM(mixed_rot.shape, full),
            pltpu.VMEM(log_totals.shape, full),
            DMA((6,)),
        ],
        compiler_params=pltpu.CompilerParams(
            collective_id=3, has_side_effects=True, vmem_limit_bytes=63 << 20
        ),
        name="attend_backward",
    )(spans, q_rot, k_rot, v_rot, grad_mixed, mixed_rot, log_totals, up_part, down_part, wo_part, out_far)


def project_kernel(
    part,
    x_ref,
    gain,
    shift,
    wq,
    bq,
    wk,
    wv,
    bv,
    x_all,
    normed,
    q_ref,
    k_ref,
    v_ref,
    landing,
    far_send,
    far_recv,
    near_send,
    near_recv,
    pass_send,
    pass_recv,
    keep_sem,
):
    team = Team()
    own = x_ref.shape[0]
    count = own // part

    def piece(owner, index):
        return rows_at(owner * own + index * part, part, part)

    def far_copy(index):
        source = x_ref.at[rows_at(index * part, part, part)]
        return team.copy(
            source, landing.at[piece(team.me, index)], far_send.at[index], far_recv.at[index], team.far
        )

    def pass_copy(index):
        place = landing.at[piece(team.far, index)]
        return team.copy(place, place, pass_send.at[index], pass_recv.at[index], team.sibling)

    near = team.copy(
        x_ref, landing.at[rows_at(team.me * own, own, own)], near_send, near_recv, team.sibling
    )

    def keep(owner, source, slot):
        return pltpu.make_async_copy(source, x_all.at[rows_at(owner * own, own, own)], keep_sem.at[slot])

    team.greet((team.sibling, team.far))
    for index in range(count):
        far_copy(index).start()
    near.start()
    keep(team.me, x_ref, 0).start()

    gain_row, shift_row, bq_row, bv_row = as_row(gain), as_row(shift), as_row(bq), as_row(bv)

    def project(owner, index, values):
        standard, unused = standardize(values.astype(FULL))
        low = (standard * gain_row + shift_row).astype(LOW)
        rows = piece(owner, index)
        normed[rows, :] = low
        q_ref[rows, :] = (dot(low, wq[...], NT) + bq_row).astype(LOW)
        k_ref[rows, :] = dot(low, wk[...], NT).astype(LOW)
        v_ref[rows, :] = (dot(low, wv[...], NT) + bv_row).astype(LOW)

    def mine(index, nothing):
        project(team.me, index, x_ref[rows_at(index * part, part, part), :])
        return nothing

    lax.fori_loop(0, count, mine, 0)
    near.wait()

    def next_to(index, nothing):
        project(team.sibling, index, landing[piece(team.sibling, index), :])
        return nothing

    lax.fori_loop(0, count, next_to, 0)

    def across(index, nothing):
        far_copy(index).wait_recv()
        pass_copy(index).start()
        project(team.far, index, landing[piece(team.far, index), :])
        pass_copy(index).wait_recv()
        project(team.diagonal, index, landing[piece(team.diagonal, index), :])
        return nothing

    lax.fori_loop(0, count, across, 0)
    for slot, owner in ((1, team.sibling), (2, team.far), (3, team.diagonal)):
        keep(owner, landing.at[rows_at(owner * own, own, own)], slot).start()
    for slot, owner in ((1, team.sibling), (2, team.far), (3, team.diagonal)):
        keep(owner, landing.at[rows_at(owner * own, own, own)], slot).wait()
    keep(team.me, x_ref, 0).wait()
    for index in range(count):
        far_copy(index).wait_send()
        pass_copy(index).wait_send()


def gather_and_project(x, gain, shift, wq, bq, wk, wv, bv):
    own, width = x.shape
    length, columns, part = 4 * own, wq.shape[0], 128
    count = own // part
    narrow = jax.ShapeDtypeStruct((length, columns), LOW)
    wide = jax.ShapeDtypeStruct((length, width), LOW)
    return pl.pallas_call(
        functools.partial(project_kernel, part),
        out_shape=(wide, wide, narrow, narrow, narrow),
        in_specs=[VMEM] * 8,
        out_specs=(ANY, VMEM, VMEM, VMEM, VMEM),
        scratch_shapes=[
            pltpu.VMEM((length, width), LOW),
            DMA((count,)),
            DMA((count,)),
            DMA,
            DMA,
            DMA((count,)),
            DMA((count,)),
            DMA((4,)),
        ],
        compiler_params=pltpu.CompilerParams(
            collective_id=0, has_side_effects=True, vmem_limit_bytes=63 << 20
        ),
        name="gather_and_project",
    )(x, gain, shift, wq, bq, wk, wv, bv)


class Reduction:
    def __init__(self, team, near_out, near_in, far_out, far_in, sems):
        self.team = team
        self.near_out, self.near_in, self.far_out, self.far_in = near_out, near_in, far_out, far_in
        self.sems = sems

    def near(self, pair):
        return self.team.copy(
            self.near_out.at[pair % 2],
            self.near_in.at[pair],
            self.sems.at[0, pair],
            self.sems.at[1, pair],
            self.team.sibling,
        )

    def across(self, pair):
        return self.team.copy(
            self.far_out.at[pair], self.far_in.at[pair], self.sems.at[2, pair], self.sems.at[3, pair], self.team.far
        )

    def give(self, pair, values):
        @pl.when(pair >= 2)
        def _():
            self.near(pair - 2).wait_send()

        self.near_out[pair % 2] = values.astype(LOW)
        self.near(pair).start()

    def combine(self, pair, values):
        self.near(pair).wait_recv()
        return values + self.near_in[pair].astype(FULL)

    def send(self, pair, values):
        self.far_out[pair] = values.astype(LOW)
        self.across(pair).start()

    def arrived(self, pair):
        self.across(pair).wait_recv()
        return self.far_in[pair].astype(FULL)

    def finish(self, pairs):
        for pair in range(pairs // 2):
            self.across(pair).wait_send()
        for pair in (pairs - 2, pairs - 1):
            self.near(pair).wait_send()


def owner_at(team_me, step):
    half = lax.div(step, 4)
    odd = lax.rem(step, 2)
    one = flip(team_me, 0)
    base = one + odd * (team_me - one)
    return lax.rem(base + 2 * (1 - half), 4)


def part_at(step):
    return lax.rem(lax.div(step, 2), 2)


def ffn_kernel(
    part,
    size,
    mixed_hbm,
    pieces_hbm,
    x_hbm,
    cot_ref,
    wo_hbm,
    up_hbm,
    down_hbm,
    up_bias,
    out_bias,
    gain,
    shift,
    down_bias,
    out_far,
    out_own,
    grad_middle,
    grad_mixed,
    up_part,
    down_part,
    grad_wo,
    sums,
    middle_own,
    up_half,
    down_half,
    halves_out,
    halves_in,
    half_sems,
    halving_parts,
    keep_sems,
    cot_all,
    normed_all,
    hidden_all,
    gpre_all,
    out_slots,
    out_near,
    own_sum,
    near_out,
    near_in,
    far_out,
    far_in,
    mixed_out,
    branch_own,
    cot_sems,
    slot_sems,
    red_sems,
    a2a_sems,
    mixed_ref,
    pieces,
    x_all,
    wo,
    up,
    down,
    load_sems,
):
    team = Team()
    length = mixed_ref.shape[0]
    width = x_all.shape[1]
    columns = mixed_ref.shape[1]
    own = length // 4
    steps = length // part

    def rows_of(owner, index):
        return rows_at(owner * own + index * part, part, part)

    def step_rows(device, step):
        return rows_of(owner_at(device, step), part_at(step))

    spreads = [
        Spread(
            team,
            cot_ref.at[pl.ds(index * part, part)],
            cot_all,
            lambda owner, index=index: rows_of(owner, index),
            cot_sems.at[index],
        )
        for index in range(own // part)
    ]
    reduction = Reduction(team, near_out, near_in, far_out, far_in, red_sems)

    def slot_copy(pair):
        slot = lax.rem(pair, 2)
        return team.copy(
            out_slots.at[slot], out_near.at[pair], slot_sems.at[0, slot], slot_sems.at[1, pair], team.sibling
        )

    plane = Plane(size)
    team.greet((team.sibling, team.far, team.diagonal), *[plane.partner(bit) for bit in range(3)])

    for spread in spreads:
        spread.start()
    arrays = (mixed_hbm, mixed_ref), (pieces_hbm, pieces), (x_hbm, x_all), (wo_hbm, wo), (up_hbm, up), (down_hbm, down)
    loads = loads_of(arrays, load_sems)
    for load in loads:
        load.start()
    for load in loads:
        load.wait()
    sums[...] = jnp.zeros_like(sums)
    gain_row, shift_row, bias_row = as_row(gain), as_row(shift), as_row(out_bias)
    up_row, down_row = as_row(up_bias), as_row(down_bias)

    def forward(step, keep_middle):
        rows = step_rows(team.me, step)

        def weights(owner):
            return wo[rows_at(owner * columns, columns, 64), :]

        branch = dot(mixed_ref[rows, :], weights(team.me), NN)
        branch = branch + dot(pieces[0, rows, :], weights(team.sibling), NN)
        branch = branch + dot(pieces[1, rows, :], weights(team.far), NN)
        branch = branch + dot(pieces[2, rows, :], weights(team.diagonal), NN)
        middle = x_all[rows, :].astype(FULL) + (branch + bias_row)
        if keep_middle:

            @pl.when(step >= steps // 2)
            def _():
                middle_own[rows_at(part_at(step) * part, part, part), :] = middle

        standard, unused = standardize(middle)
        low = (standard * gain_row + shift_row).astype(LOW)
        normed_all[rows, :] = low
        pre = dot(low, up[...], NN) + up_row
        bell = 0.5 * (1.0 + lax.erf(pre * 0.7071067811865476))
        hidden = (pre * bell).astype(LOW)
        hidden_all[rows, :] = hidden
        slope = bell + pre * (jnp.exp(pre * pre * -0.5) * 0.3989422804014327)
        gpre_all[rows, :] = slope.astype(LOW)

        out = dot(hidden, down[...], NN)
        pair = lax.div(step, 2)
        if keep_middle:
            place = rows_at(part_at(step) * part, part, part)

            @pl.when(step < steps // 2)
            def _():
                out_far[place, :] = out.astype(LOW)

            @pl.when(step >= steps // 2)
            def _():
                out_own[place, :] = middle + out + down_row
        else:

            @pl.when(pair >= 2)
            def _():
                slot_copy(pair - 2).wait_send()

            out_slots[lax.rem(pair, 2)] = out.astype(LOW)
            slot_copy(pair).start()
    def backward(step):
        rows = step_rows(team.me, step)
        slope = gpre_all[rows, :].astype(FULL)
        grad_pre = (dot(cot_all[rows, :], down[...], NT) * slope).astype(LOW)
        gpre_all[rows, :] = grad_pre
        sums[4:5, :] += column_sums(grad_pre.astype(FULL))
        return dot(grad_pre, up[...], NT)

    def pair_forward(pair, nothing):
        forward(2 * pair, False)
        forward(2 * pair + 1, True)
        return nothing

    half = width // 2
    down_total = Halving(plane, down_half, None, 0, *halving_parts)
    up_keep = pltpu.make_async_copy(up_half, up_part, keep_sems.at[0])
    down_keep = pltpu.make_async_copy(down_half.at[down_total.inner(2)], down_part, keep_sems.at[1])
    halves = (normed_all, gpre_all, up_half), (hidden_all, cot_all, down_half)
    side_copies = [
        plane.remote(halves_out.at[index], halves_in.at[index], half_sems, index, plane.partner(0))
        for index in range(2)
    ]
    def place_of(pair):
        return rows_at(part_at(2 * pair) * part, part, part)

    def add_out(pair):
        slot_copy(pair).wait_recv()
        place, given = place_of(pair), out_near[pair].astype(FULL)

        @pl.when(pair < steps // 4)
        def _():
            out_far[place, :] = (out_far[place, :].astype(FULL) + given).astype(LOW)

        @pl.when(pair >= steps // 4)
        def _():
            out_own[place, :] += given

    def combine(pair):
        reduction.near(pair).wait_recv()
        given = reduction.near_in[pair].astype(FULL)

        @pl.when(pair < steps // 4)
        def _():
            reduction.send(pair, reduction.far_out[lax.rem(pair, 2)].astype(FULL) + given)

        @pl.when(pair >= steps // 4)
        def _():
            own_sum[place_of(pair), :] += given

    def pair_backward(pair, nothing):
        first, second = 2 * pair, 2 * pair + 1
        for index, spread in enumerate(spreads):

            @pl.when(pair == index)
            def _(spread=spread):
                spread.middle()
                spread.passed().wait_recv()

        @pl.when(pair == len(spreads))
        def _():
            for spread in spreads:
                spread.near().wait_recv()
                spread.kept().wait()
            side_half(1)

        @pl.when(pair == len(spreads) + 1)
        def _():
            own_half(1)

        reduction.give(pair, backward(first))
        add_out(pair)

        @pl.when(pair >= 1)
        def _():
            combine(pair - 1)

        values = backward(second)

        @pl.when(pair < steps // 4)
        def _():
            far_out[lax.rem(pair, 2)] = values.astype(LOW)

        @pl.when(pair >= steps // 4)
        def _():
            own_sum[place_of(pair), :] = values

        return nothing

    def side_half(index):
        left, right, unused = halves[index]
        lanes = rows_at((1 - plane.side) * half, half, half)

        def one(slab, nothing):
            columns_of = rows_at(slab * 256, 256, 256)
            halves_out[index, :, columns_of] = dot(left[:, lanes], right[:, columns_of], TN).astype(LOW)
            return nothing

        lax.fori_loop(0, width // 256, one, 0)
        side_copies[index].start()

    def own_half(index):
        left, right, target = halves[index]
        lanes = rows_at(plane.side * half, half, half)

        def one(slab, nothing):
            columns_of = rows_at(slab * 256, 256, 256)
            target[:, columns_of] = dot(left[:, lanes], right[:, columns_of], TN)
            return nothing

        lax.fori_loop(0, width // 256, one, 0)

    def add_side(index):
        side_copies[index].wait()
        halves[index][2][...] += halves_in[index].astype(FULL)

    lax.fori_loop(0, steps // 2, pair_forward, 0)
    lax.fori_loop(0, steps // 2, pair_backward, 0)
    side_half(0)
    add_side(1)
    down_total.start(0)
    combine(steps // 2 - 1)

    def back(index, nothing):
        @pl.when(index == 1)
        def _():
            down_total.finish(0)
            down_total.start(1)

        rows = rows_at(index * part, part, part)
        own_rows = rows_of(team.me, index)
        grad = own_sum[rows, :] + reduction.arrived(index)
        standard, inverse = standardize(middle_own[rows, :])
        incoming = cot_all[own_rows, :].astype(FULL)
        grad_mid = incoming + norm_back(grad, gain_row, standard, inverse)
        grad_middle[rows, :] = grad_mid
        branch_low = grad_mid.astype(LOW)
        branch_own[rows, :] = branch_low
        for slot, owner in enumerate((team.sibling, team.far, team.diagonal)):
            side = wo[rows_at(owner * columns, columns, 64), :]
            mixed_out[slot, rows, :] = dot(branch_low, side, NT).astype(LOW)
            exchange(index, slot, owner).start()
        side = wo[rows_at(team.me * columns, columns, 64), :]
        grad_mixed[own_rows, :] = dot(branch_low, side, NT).astype(LOW)
        sums[0:1, :] += column_sums(grad * standard)
        sums[1:2, :] += column_sums(grad)
        sums[2:3, :] += column_sums(branch_low.astype(FULL))
        sums[3:4, :] += column_sums(incoming)
        return nothing

    def exchange(index, slot, owner):
        return team.copy(
            mixed_out.at[slot, rows_at(index * part, part, part)],
            grad_mixed.at[rows_of(team.me, index)],
            a2a_sems.at[2 * index, slot],
            a2a_sems.at[2 * index + 1, slot],
            owner,
        )

    lax.fori_loop(0, own // part, back, 0)
    own_half(0)
    own_rows = rows_at(team.me * own, own, own)
    for source, owner in (
        (mixed_ref.at[own_rows], team.me),
        (pieces.at[0, own_rows], team.sibling),
        (pieces.at[1, own_rows], team.far),
        (pieces.at[2, own_rows], team.diagonal),
    ):
        grad_wo[rows_at(owner * columns, columns, 64), :] = dot(source[...], branch_own[...], TN).astype(LOW)
    down_total.finish(1)
    down_keep.start()
    add_side(0)
    up_keep.start()
    for index in range(own // part):
        for slot, owner in enumerate((team.sibling, team.far, team.diagonal)):
            exchange(index, slot, owner).wait()
    down_keep.wait()
    up_keep.wait()
    for spread in spreads:
        spread.sent()
    for pair in (steps // 2 - 2, steps // 2 - 1):
        slot_copy(pair).wait_send()
    reduction.finish(steps // 2)


def ffn(size, mixed, pieces, x_all, cotangent, wo, up, down, up_bias, out_bias, gain, shift, down_bias):
    length, columns = mixed.shape
    width = x_all.shape[1]
    hidden = up.shape[1]
    own, part = length // 4, 320
    steps = length // part
    pairs = steps // 2

    def shape(dims, kind):
        return jax.ShapeDtypeStruct(dims, kind)

    return pl.pallas_call(
        functools.partial(ffn_kernel, part, size),
        out_shape=(
            shape((own, width), LOW),
            shape((own, width), FULL),
            shape((own, width), FULL),
            shape((length, columns), LOW),
            shape((width // 2, hidden), FULL),
            shape((hidden // 8, width), FULL),
            shape((width, width), LOW),
            shape((8, width), FULL),
        ),
        in_specs=[ANY] * 7 + [VMEM] * 5,
        out_specs=(VMEM,) * 4 + (ANY, ANY, VMEM, VMEM),
        scratch_shapes=[
            pltpu.VMEM((own, width), FULL),
            pltpu.VMEM((width // 2, hidden), FULL),
            pltpu.VMEM((hidden // 2, width), FULL),
            pltpu.VMEM((2, width // 2, width), LOW),
            pltpu.VMEM((2, width // 2, width), LOW),
            DMA((2, 2)),
            halving_scratch(size, width // 2, width),
            DMA((2,)),
            pltpu.VMEM((length, width), LOW),
            pltpu.VMEM((length, width), LOW),
            pltpu.VMEM((length, hidden), LOW),
            pltpu.VMEM((length, hidden), LOW),
            pltpu.VMEM((2, part, width), LOW),
            pltpu.VMEM((pairs, part, width), LOW),
            pltpu.VMEM((own, width), FULL),
            pltpu.VMEM((2, part, width), LOW),
            pltpu.VMEM((pairs, part, width), LOW),
            pltpu.VMEM((pairs // 2, part, width), LOW),
            pltpu.VMEM((pairs // 2, part, width), LOW),
            pltpu.VMEM((3, own, columns), LOW),
            pltpu.VMEM((own, width), LOW),
            DMA((own // part, 7)),
            DMA((2, pairs)),
            DMA((4, pairs)),
            DMA((4, 3)),
            pltpu.VMEM(mixed.shape, LOW),
            pltpu.VMEM(pieces.shape, LOW),
            pltpu.VMEM(x_all.shape, LOW),
            pltpu.VMEM(wo.shape, LOW),
            pltpu.VMEM(up.shape, LOW),
            pltpu.VMEM(down.shape, LOW),
            DMA((6,)),
        ],
        compiler_params=pltpu.CompilerParams(
            collective_id=2, has_side_effects=True, vmem_limit_bytes=63 << 20
        ),
        name="ffn",
    )(mixed, pieces, x_all, cotangent, wo, up, down, up_bias, out_bias, gain, shift, down_bias)


def last_kernel(
    part,
    size,
    dq_hbm,
    dk_hbm,
    dv_hbm,
    wq,
    wk,
    wv,
    normed_hbm,
    x_hbm,
    grad_hbm,
    gain,
    wo_sum,
    wide,
    input_grad,
    grad_sum,
    vectors,
    own_grad,
    near_out,
    near_in,
    far_out,
    far_in,
    red_sems,
    sources,
    wires,
    total_parts,
    packed,
    packed_in,
    vec_sems,
    keep_sems,
    dq_ref,
    dk_ref,
    dv_ref,
    normed_all,
    x_all,
    grad_middle,
    load_sems,
):
    team, plane = Team(), Plane(size)
    arrays = (
        (dq_hbm, dq_ref),
        (dk_hbm, dk_ref),
        (dv_hbm, dv_ref),
        (normed_hbm, normed_all),
        (x_hbm, x_all),
        (grad_hbm, grad_middle),
    )
    loads = loads_of(arrays, load_sems)
    for load in loads:
        load.start()
    length, columns = dq_ref.shape
    width = normed_all.shape[1]
    own = length // 4
    pairs = length // part // 2
    grads = Reduction(team, near_out, near_in, far_out, far_in, red_sems)
    slabs = sources.shape[0]
    lanes_of = width // slabs
    totals = [Direct(plane, sources.at[slab], wires.at[slab], *total_parts[slab]) for slab in range(slabs)]
    others = greet_all(team, plane, True)
    events = Events(totals)

    def slab_grads(slab, nothing):
        lanes = rows_at(slab * lanes_of, lanes_of, lanes_of)
        for index, source in enumerate((dq_ref, dk_ref, dv_ref)):
            value = dot(source[...], normed_all[:, lanes], TN)
            sources[slab, index * columns : (index + 1) * columns, :] = value.astype(LOW)
        sources[slab, 3 * columns : 4 * columns, :] = wo_sum[:, lanes]
        for index, total in enumerate(totals):

            @pl.when(slab == index)
            def _(total=total):
                total.start(0)

        return nothing

    for load in loads[:4]:
        load.wait()
    lax.fori_loop(0, slabs, slab_grads, 0)
    for load in loads[4:]:
        load.wait()
    gain_row = as_row(gain)
    packed[...] = jnp.zeros_like(packed)
    packed[0:4, :] = wide[0:4, :]
    packed[8:9, :] = wide[4:5, :]
    packed[9:10, 0:columns] = column_sums(dq_ref[...].astype(FULL))
    packed[10:11, 0:columns] = column_sums(dv_ref[...].astype(FULL))

    def step_rows(step):
        return rows_at(owner_at(team.me, step) * own + part_at(step) * part, part, part)

    def compute(step):
        rows = step_rows(step)
        total = dot(dq_ref[rows, :], wq[...], NN) + dot(dk_ref[rows, :], wk[...], NN)
        return total + dot(dv_ref[rows, :], wv[...], NN)

    everything = list(events.waiting)

    def events_at(pair, plan):
        for when, (start, stop) in plan.items():

            @pl.when(pair == when)
            def _(start=start, stop=stop):
                events.waiting = everything[start:stop]
                events.take(1 << 20)

    def pair_step(pair, nothing):
        first, second = 2 * pair, 2 * pair + 1
        grads.give(pair, compute(first))
        standard, unused = standardize(x_all[step_rows(second), :].astype(FULL))
        events_at(pair, {1: (0, 1), 2: (1, 2), 3: (3, 4)})
        values = grads.combine(pair, compute(second))
        packed[4:5, :] += column_sums(values * standard)
        packed[5:6, :] += column_sums(values)

        @pl.when(pair < pairs // 2)
        def _():
            grads.send(pair, values)

        @pl.when(pair >= pairs // 2)
        def _():
            own_grad[rows_at(part_at(second) * part, part, part), :] = values

        events_at(pair, {2: (2, 3), 3: (4, 5)})
        return nothing

    lax.fori_loop(0, pairs, pair_step, 0)
    events.waiting = everything[5:]

    def vector_copy(step):
        return pltpu.make_async_remote_copy(
            src_ref=packed.at[pl.ds(16 * step, 16)],
            dst_ref=packed_in.at[step],
            send_sem=vec_sems.at[0, step],
            recv_sem=vec_sems.at[1, step],
            device_id=others[step],
            device_id_type=MESH,
        )

    def finish_rows(index):
        rows = pl.ds(index * part, part)
        grad = own_grad[rows, :] + grads.arrived(index)
        standard, inverse = standardize(x_all[rows_at(team.me * own + index * part, part, part), :].astype(FULL))
        input_grad[rows, :] = grad_middle[rows, :] + norm_back(grad, gain_row, standard, inverse)

    for step in range(len(others)):
        vector_copy(step).start()
        events.next(1)
        vector_copy(step).wait()
        here = packed[16 * step : 16 * (step + 1), :]
        keep = 16 if step < plane.bits else 8
        row = lax.broadcasted_iota(jnp.int32, here.shape, 0)
        added = here + jnp.where(row < keep, packed_in[step], 0.0)
        packed[16 * (step + 1) : 16 * (step + 2), :] = added
    vectors[...] = packed[16 * len(others) : 16 * (len(others) + 1), :]
    events.take(1 << 20)
    for index in range(own // part):
        finish_rows(index)
    events.end()
    keeps = []
    for slab in range(slabs):
        lanes = pl.ds(slab * lanes_of, lanes_of)
        keeps.append(pltpu.make_async_copy(wires.at[slab], grad_sum.at[:, lanes], keep_sems.at[slab]))
    for keep in keeps:
        keep.start()
    for keep in keeps:
        keep.wait()
    grads.finish(pairs)


def last(size, dq, dk, dv, wq, wk, wv, normed_all, x_all, grad_middle, gain, wo_sum, wide):
    length, columns = dq.shape
    own, width = grad_middle.shape
    part, slabs = 320, 3
    pairs = length // part // 2
    bits = size.bit_length() - 1
    slab = (4 * columns, width // slabs)

    def shape(dims, kind):
        return jax.ShapeDtypeStruct(dims, kind)

    return pl.pallas_call(
        functools.partial(last_kernel, part, size),
        out_shape=(
            shape((own, width), FULL),
            shape((4 * columns, width), LOW),
            shape((16, width), FULL),
        ),
        in_specs=[ANY] * 3 + [VMEM] * 3 + [ANY] * 3 + [VMEM] * 3,
        out_specs=(VMEM, ANY, VMEM),
        scratch_shapes=[
            pltpu.VMEM((own, width), FULL),
            pltpu.VMEM((2, part, width), LOW),
            pltpu.VMEM((pairs, part, width), LOW),
            pltpu.VMEM((pairs // 2, part, width), LOW),
            pltpu.VMEM((pairs // 2, part, width), LOW),
            DMA((4, pairs)),
            pltpu.VMEM((slabs, *slab), LOW),
            pltpu.VMEM((slabs, *slab), LOW),
            [direct_scratch(size, *slab) for unused in range(slabs)],
            pltpu.VMEM((16 * (bits + 3), width), FULL),
            pltpu.VMEM((bits + 2, 16, width), FULL),
            DMA((2, bits + 2)),
            DMA((slabs,)),
            pltpu.VMEM(dq.shape, LOW),
            pltpu.VMEM(dk.shape, LOW),
            pltpu.VMEM(dv.shape, LOW),
            pltpu.VMEM(normed_all.shape, LOW),
            pltpu.VMEM(x_all.shape, LOW),
            pltpu.VMEM(grad_middle.shape, FULL),
            DMA((6,)),
        ],
        compiler_params=pltpu.CompilerParams(
            collective_id=4, has_side_effects=True, vmem_limit_bytes=60 << 20
        ),
        name="last",
    )(dq, dk, dv, wq, wk, wv, normed_all, x_all, grad_middle, gain, wo_sum, wide)


def local(
    size,
    layer_input,
    segment_ids,
    cotangent,
    attn_gain,
    attn_shift,
    query_weight,
    query_bias,
    key_weight,
    value_weight,
    value_bias,
    out_weight,
    out_bias,
    ffn_gain,
    ffn_shift,
    up_weight,
    up_bias,
    down_weight,
    down_bias,
):
    query_side, key_side, value_side = query_weight.T, key_weight.T, value_weight.T
    x_all, normed_rows, queries, key_rows, value_rows = gather_and_project(
        layer_input,
        attn_gain,
        attn_shift,
        query_side,
        query_bias,
        key_side,
        value_side,
        value_bias,
    )
    mixed, mixed_rot, log_totals, pieces, out_all, q_rot, k_rot, v_rot = attend_forward(
        segment_ids, queries, key_rows, value_rows, out_weight
    )
    out_far, out_own, grad_middle, grad_mixed, up_part, down_part, out_part, sums = ffn(
        size,
        mixed,
        pieces,
        x_all,
        cotangent,
        out_all,
        up_weight,
        down_weight,
        up_bias,
        out_bias,
        ffn_gain,
        ffn_shift,
        down_bias,
    )
    dq, dk, dv, grad_up, grad_down, wo_sum, out_in = attend_backward(
        size, segment_ids, q_rot, k_rot, v_rot, grad_mixed, mixed_rot, log_totals, up_part, down_part, out_part, out_far
    )
    layer_output = (out_own + out_in.astype(FULL)).astype(LOW)
    input_grad, grads, vectors = last(
        size,
        dq,
        dk,
        dv,
        query_side,
        key_side,
        value_side,
        normed_rows,
        x_all,
        grad_middle,
        attn_gain,
        wo_sum,
        sums,
    )
    columns = query_side.shape[0]
    grads = grads.astype(FULL)
    return (
        layer_output,
        input_grad,
        vectors[4],
        vectors[5],
        grads[0:columns].T,
        vectors[9, 0:columns],
        grads[columns : 2 * columns].T,
        grads[2 * columns : 3 * columns].T,
        vectors[10, 0:columns],
        grads[3 * columns :],
        vectors[2],
        vectors[0],
        vectors[1],
        grad_up.astype(FULL),
        vectors[8],
        grad_down.astype(FULL),
        vectors[3],
    )


def solution(mesh):
    return jax.shard_map(
        functools.partial(local, mesh.shape["dp"]),
        mesh=mesh,
        in_specs=(
            P(("dp", "seq"), None),
            P("dp", None),
            P(("dp", "seq"), None),
            P(),
            P(),
            P(None, "seq"),
            P("seq"),
            P(None, "seq"),
            P(None, "seq"),
            P("seq"),
            P("seq", None),
            P(),
            P(),
            P(),
            P(None, "seq"),
            P("seq"),
            P("seq", None),
            P(),
        ),
        out_specs=(
            P(("dp", "seq"), None),
            P(("dp", "seq"), None),
            P(),
            P(),
            P(None, "seq"),
            P("seq"),
            P(None, "seq"),
            P(None, "seq"),
            P("seq"),
            P("seq", None),
            P(),
            P(),
            P(),
            P(None, "seq"),
            P("seq"),
            P("seq", None),
            P(),
        ),
        check_vma=False,
    )
```

```python
import functools

import jax
import jax.numpy as jnp
from jax import lax
from jax.experimental import pallas as pl
from jax.experimental.pallas import tpu as pltpu
from jax.sharding import PartitionSpec as P

HEAD = 64
SCALE = HEAD ** (-0.5)
LOG_SCALE = SCALE * 1.4426950408889634
LONGEST = 2048
EPSILON = 1e-06
NN = (((1,), (0,)), ((), ()))
NT = (((1,), (1,)), ((), ()))
TN = (((0,), (0,)), ((), ()))
MESH = pl.DeviceIdType.MESH
LOW = jnp.bfloat16
FULL = jnp.float32
VMEM = pl.BlockSpec(memory_space=pltpu.VMEM)
SMEM = pl.BlockSpec(memory_space=pltpu.SMEM)
ANY = pl.BlockSpec(memory_space=pl.ANY)
DMA = pltpu.SemaphoreType.DMA


def flip(index, bit):
    size = 1 << bit
    return index + size - 2 * size * lax.rem(lax.div(index, size), 2)


class Team:
    def __init__(self):
        self.row = lax.axis_index("dp")
        self.me = lax.axis_index("seq")
        self.sibling = flip(self.me, 0)
        self.far = flip(self.me, 1)
        self.diagonal = flip(self.sibling, 1)

    def device(self, index):
        return (self.row, index)

    def greet(self, others, *more):
        barrier = pltpu.get_barrier_semaphore()
        devices = [self.device(other) for other in others] + list(more)
        for device in devices:
            pl.semaphore_signal(barrier, inc=1, device_id=device, device_id_type=MESH)
        pl.semaphore_wait(barrier, len(devices))

    def copy(self, source, target, send, receive, other):
        return pltpu.make_async_remote_copy(
            src_ref=source,
            dst_ref=target,
            send_sem=send,
            recv_sem=receive,
            device_id=self.device(other),
            device_id_type=MESH,
        )


def loads_of(pairs, sems):
    return [pltpu.make_async_copy(source, target, sems.at[index]) for index, (source, target) in enumerate(pairs)]


def rows_at(start, count, multiple):
    return pl.ds(pl.multiple_of(start, multiple), count)


def standardize(values):
    average = jnp.mean(values, axis=-1, keepdims=True)
    centered = values - average
    variance = jnp.mean(centered * centered, axis=-1, keepdims=True)
    inverse = lax.rsqrt(variance + EPSILON)
    return centered * inverse, inverse


def norm_back(grad, gain_row, standard, inverse):
    scaled = grad * gain_row
    mean_one = jnp.mean(scaled, axis=-1, keepdims=True)
    mean_two = jnp.mean(scaled * standard, axis=-1, keepdims=True)
    return inverse * (scaled - mean_one - standard * mean_two)


def column_sums(values):
    return jnp.sum(values, axis=0, keepdims=True)


def first_at_least(segments, value):
    length = segments.shape[1]

    def halve(unused, ends):
        low, high = ends
        middle = jnp.minimum(lax.div(low + high, 2), length - 1)
        below = segments[0, middle] < value
        open_yet = low < high
        return (
            jnp.where(open_yet & below, middle + 1, low),
            jnp.where(open_yet & jnp.logical_not(below), middle, high),
        )

    return lax.fori_loop(0, length.bit_length(), halve, (jnp.int32(0), jnp.int32(length)))[0]


def rotation(segments):
    length = segments.shape[1]
    one, two = first_at_least(segments, 1), first_at_least(segments, 2)
    offset = jnp.where(one == LONGEST, 0, jnp.where(two - one == LONGEST, one, two))
    border = jnp.where(one == LONGEST, two - one, jnp.where(two - one == LONGEST, length - two, one))
    return offset, border


def as_row(ref):
    return ref[...].astype(FULL).reshape(1, -1)


def dot(left_side, right_side, dims):
    return lax.dot_general(left_side, right_side, dims, preferred_element_type=jnp.float32)


def keep_head(head, values):
    lane = lax.broadcasted_iota(jnp.int32, values.shape, 1)
    inside = (lane >= head * HEAD) & (lane < (head + 1) * HEAD)
    return jnp.where(inside, values, jnp.zeros_like(values))


class Spread:
    def __init__(self, team, source, target, rows_of, sems):
        self.team, self.source, self.target, self.rows_of, self.sems = team, source, target, rows_of, sems

    def place(self, owner):
        return self.target.at[self.rows_of(owner)]

    def across(self):
        here = self.place(self.team.me)
        return self.team.copy(self.source, here, self.sems.at[0], self.sems.at[1], self.team.far)

    def near(self):
        here = self.place(self.team.me)
        return self.team.copy(self.source, here, self.sems.at[2], self.sems.at[3], self.team.sibling)

    def passed(self):
        there = self.place(self.team.far)
        return self.team.copy(there, there, self.sems.at[4], self.sems.at[5], self.team.sibling)

    def kept(self):
        return pltpu.make_async_copy(self.source, self.place(self.team.me), self.sems.at[6])

    def start(self):
        self.across().start()
        self.near().start()
        self.kept().start()

    def middle(self):
        self.across().wait_recv()
        self.passed().start()

    def sent(self):
        self.across().wait_send()
        self.near().wait_send()
        self.passed().wait_send()


EXTRA = 72


def rotated_block(ref, shift, length, index):
    width = ref.shape[2]
    sub = lax.broadcasted_iota(jnp.int32, (32, 8, width), 1)
    start = lax.rem(shift + index * 256, length)
    group = lax.div(start, 8)
    skip = start - group * 8
    turned = pltpu.roll(ref[pl.ds(group, 33)], lax.rem(8 - skip, 8), 1)
    return jnp.where(sub < 8 - skip, turned[:32], turned[1:]).reshape(256, width)


def rotate(ref, shift, length, put):
    def one(index, nothing):
        put(index, rotated_block(ref, shift, length, index))
        return nothing

    lax.fori_loop(0, length // 256, one, 0)


def wrap(ref, length):
    ref[length // 8 : length // 8 + EXTRA] = ref[0:EXTRA]


def rotate_into(source, target, buffer, shift):
    length, width = source.shape
    buffer[0 : length // 8] = source[...].astype(FULL).reshape(length // 8, 8, width)
    wrap(buffer, length)

    def put(index, block):
        target[rows_at(index * 256, 256, 256), :] = block.astype(LOW)

    rotate(buffer, shift, length, put)


def forward_kernel(
    rows_of,
    keys_of,
    head_count,
    spans,
    q_ref,
    k_ref,
    v_ref,
    wo_ref,
    mixed_ref,
    mixed_rot_ref,
    log_ref,
    pieces,
    wo_all,
    q_hbm,
    k_hbm,
    v_hbm,
    v_heads,
    buffer,
    wo_sems,
    far_sems,
    near_sems,
    pass_sems,
    q_rot,
    k_rot,
    v_rot,
    store_sems,
):
    length, width = q_ref.shape
    team = Team()
    spread = Spread(team, wo_ref, wo_all, lambda owner: rows_at(owner * width, width, 64), wo_sems)

    def far_copy(index):
        rows = rows_at(index * 256, 256, 256)
        return team.copy(
            mixed_ref.at[rows], pieces.at[1, rows], far_sems.at[0, index], far_sems.at[1, index], team.far
        )

    def near_copy(index):
        rows = rows_at(index * 256, 256, 256)
        return team.copy(
            mixed_ref.at[rows], pieces.at[0, rows], near_sems.at[0, index], near_sems.at[1, index], team.sibling
        )

    def pass_copy(index):
        rows = rows_at(index * 256, 256, 256)
        return team.copy(
            pieces.at[1, rows], pieces.at[2, rows], pass_sems.at[0, index], pass_sems.at[1, index], team.sibling
        )

    team.greet((team.sibling, team.far))
    spread.start()
    small = length - LONGEST
    offset, border = rotation(spans)

    rotate_into(q_ref, q_rot, buffer, offset)
    rotate_into(k_ref, k_rot, buffer, offset)
    rotate_into(v_ref, v_rot, buffer, offset)
    stores = loads_of(((q_rot, q_hbm), (k_rot, k_hbm), (v_rot, v_hbm)), store_sems)
    v_all = v_rot[...]
    for head in range(head_count):
        v_heads[head] = jnp.concatenate(
            [keep_head(head, v_all), jnp.full((length, 256 - width), 1, jnp.bfloat16)], axis=1
        )

    def block(row, key_base, key_count, masked):
        rows = pl.ds(row, rows_of)
        total = jnp.zeros((rows_of, width), jnp.float32)
        logs = []
        for head in range(head_count):
            q_head = keep_head(head, q_rot[rows, :])
            top, parts = None, []
            for chunk in range(key_count // keys_of):
                keys = pl.ds(key_base + chunk * keys_of, keys_of)
                scores = dot(q_head, k_rot[keys, :], NT)
                if masked:
                    shape = (rows_of, keys_of)
                    row_id = lax.broadcasted_iota(jnp.int32, shape, 0) + (row - LONGEST)
                    key_id = lax.broadcasted_iota(jnp.int32, shape, 1) + chunk * keys_of
                    scores = jnp.where((row_id < border) == (key_id < border), scores, -1e30)
                high = jnp.max(scores, axis=1, keepdims=True)
                top = high if top is None else jnp.maximum(top, high)
                parts.append(scores)
            summed = jnp.zeros((rows_of, 256), jnp.float32)
            for chunk, scores in enumerate(parts):
                keys = pl.ds(key_base + chunk * keys_of, keys_of)
                weights = jnp.exp2((scores - top) * LOG_SCALE).astype(jnp.bfloat16)
                summed = summed + dot(weights, v_heads[head, keys, :], NN)
            norm = summed[:, 255:256]
            total = total + summed[:, :width] * (1.0 / norm)
            logs.append(top * LOG_SCALE + jnp.log2(norm))
        mixed_rot_ref[pl.ds(lax.div(row, 8), rows_of // 8)] = total.reshape(rows_of // 8, 8, width)
        logs.append(jnp.zeros((rows_of, 128 - head_count), jnp.float32))
        log_ref[rows, :] = jnp.concatenate(logs, axis=1)

    def send(index):
        rows = rows_at(index * 256, 256, 256)
        mixed_ref[rows, :] = rotated_block(mixed_rot_ref, length - offset, length, index).astype(LOW)
        far_copy(index).start()
        near_copy(index).start()

    def pass_on(index):
        far_copy(index).wait_recv()
        pass_copy(index).start()

    def little(index, nothing):
        block(pl.multiple_of(LONGEST + index * rows_of, rows_of), LONGEST, small, True)
        return nothing

    lax.fori_loop(0, small // rows_of, little, 0)
    for store in stores:
        store.start()
    lag, trips = 2, LONGEST // rows_of

    def large(index, nothing):
        block(pl.multiple_of(index * rows_of, rows_of), 0, LONGEST, False)

        @pl.when(index == 0)
        def _():
            mixed_rot_ref[length // 8 : length // 8 + 32] = mixed_rot_ref[0:32]

        send(index)

        @pl.when(index == trips // 2)
        def _():
            spread.middle()

        @pl.when(index >= lag)
        def _():
            pass_on(index - lag)

        return nothing

    lax.fori_loop(0, trips, large, 0)
    blocks = length // 256
    for index in range(trips, blocks):
        send(index)
    for index in range(trips - lag, blocks):
        pass_on(index)
    for index in range(blocks):
        near_copy(index).wait()
        far_copy(index).wait_send()
        pass_copy(index).wait()
    spread.sent()
    spread.near().wait_recv()
    spread.passed().wait_recv()
    spread.kept().wait()
    for store in stores:
        store.wait()


def attend_forward(spans, queries, key_rows, value_rows, out_weight):
    length, width = queries.shape
    head_count = width // HEAD
    return pl.pallas_call(
        functools.partial(forward_kernel, 256, 512, head_count),
        out_shape=(
            jax.ShapeDtypeStruct((length, width), jnp.bfloat16),
            jax.ShapeDtypeStruct((length // 8 + EXTRA, 8, width), jnp.float32),
            jax.ShapeDtypeStruct((length, 128), jnp.float32),
            jax.ShapeDtypeStruct((3, length, width), LOW),
            jax.ShapeDtypeStruct((4 * out_weight.shape[0], out_weight.shape[1]), LOW),
            jax.ShapeDtypeStruct((length, width), LOW),
            jax.ShapeDtypeStruct((length, width), LOW),
            jax.ShapeDtypeStruct((length, width), LOW),
        ),
        in_specs=[SMEM, VMEM, VMEM, VMEM, VMEM],
        out_specs=(VMEM, VMEM, VMEM, ANY, ANY, ANY, ANY, ANY),
        scratch_shapes=[
            pltpu.VMEM((head_count, length, 256), jnp.bfloat16),
            pltpu.VMEM((length // 8 + EXTRA, 8, width), FULL),
            DMA((7,)),
            DMA((2, length // 256)),
            DMA((2, length // 256)),
            DMA((2, length // 256)),
            pltpu.VMEM((length, width), LOW),
            pltpu.VMEM((length, width), LOW),
            pltpu.VMEM((length, width), LOW),
            DMA((3,)),
        ],
        compiler_params=pltpu.CompilerParams(
            collective_id=1, has_side_effects=True, vmem_limit_bytes=60 << 20
        ),
        name="attend_forward",
    )(spans, queries, key_rows, value_rows, out_weight)


class Plane:
    def __init__(self, size):
        self.me, self.lane = lax.axis_index("dp"), lax.axis_index("seq")
        self.size, self.bits = size, size.bit_length() - 1
        self.ranks = min(4, size // 2)
        self.side, self.rank = lax.rem(self.me, 2), lax.rem(lax.div(self.me, 2), self.ranks)
        self.extra = (size // 2 // self.ranks).bit_length() - 1

    def device(self, index):
        return (index, self.lane)

    def partner(self, bit):
        return self.device(flip(self.me, bit))

    def digit(self, bit):
        return lax.rem(lax.div(self.me, 1 << bit), 2)

    def other_rank(self, offset):
        return lax.rem(self.rank + offset, self.ranks)

    def ranked(self, offset):
        return self.device(self.me + 2 * (self.other_rank(offset) - self.rank))

    def remote(self, source, target, sems, index, device):
        return pltpu.make_async_remote_copy(
            src_ref=source,
            dst_ref=target,
            send_sem=sems.at[0, index],
            recv_sem=sems.at[1, index],
            device_id=device,
            device_id_type=MESH,
        )


class Halving:
    def __init__(self, plane, part, wire, first, sends, receives, sems):
        self.plane, self.part, self.wire, self.first = plane, part, wire, first
        self.sends, self.receives, self.sems = sends, receives, sems
        self.halvings, self.whole = halvings_of(plane.bits)
        self.stages = 2 * self.halvings + self.whole + 1
        half = part.shape[0]
        self.bases, self.sizes = [0], [half]
        for level in range(self.halvings):
            size = self.sizes[-1] // 2
            self.bases.append(self.bases[-1] + plane.digit(level + 1) * size)
            self.sizes.append(size)
        self.step = self.sizes[-1]
        self.shift = plane.side * half

    def inner(self, level):
        return rows_at(self.bases[level], self.sizes[level], self.step)

    def place(self, level):
        return rows_at(self.shift + self.bases[level], self.sizes[level], self.step)

    def copies(self, stage):
        plane = self.plane
        if stage < self.halvings + self.whole:
            return [
                plane.remote(self.sends[stage], self.receives[stage], self.sems, stage, plane.partner(stage + 1))
            ]
        level = 2 * self.halvings + self.whole - stage
        here = self.wire.at[self.place(level)]
        return [plane.remote(here, here, self.sems, stage, plane.partner(level))]

    def start(self, stage):
        if stage < self.halvings:
            size = self.sizes[stage + 1]
            first = self.bases[stage] + (1 - self.plane.digit(stage + 1)) * size
            self.sends[stage][...] = self.part[rows_at(first, size, self.step), :].astype(LOW)
        elif stage < self.halvings + self.whole:
            self.sends[stage][...] = self.part[self.inner(self.halvings), :].astype(LOW)
        elif stage == self.halvings + self.whole:
            self.wire[self.place(self.halvings), :] = self.part[self.inner(self.halvings), :].astype(LOW)
        for copy in self.copies(stage):
            copy.start()

    def finish(self, stage):
        for copy in self.copies(stage):
            copy.wait()
        if stage < self.halvings:
            self.part[self.inner(stage + 1), :] += self.receives[stage][...].astype(FULL)
        elif stage < self.halvings + self.whole:
            value = self.sends[stage][...].astype(FULL) + self.receives[stage][...].astype(FULL)
            self.part[self.inner(self.halvings), :] = value


def halvings_of(bits):
    halvings = min(bits - 1, 2)
    return halvings, bits - 1 - halvings


def halving_scratch(size, half, width):
    bits = size.bit_length() - 1
    halvings, whole = halvings_of(bits)
    shapes = [(half >> (stage + 1), width) for stage in range(halvings)] + [(half >> halvings, width)] * whole
    kinds = [pltpu.VMEM(dims, LOW) for dims in shapes]
    return [kinds, list(kinds), DMA((2, 2 * halvings + whole + 1))]


class Direct:
    first = 0

    def __init__(self, plane, source, wire, part, received, sends, receives, sems):
        self.plane, self.source, self.wire, self.part = plane, source, wire, part
        self.received, self.sends, self.receives, self.sems = received, sends, receives, sems
        self.half = source.shape[0] // 2
        self.piece = self.half // plane.ranks
        self.stages = 4 + plane.extra

    def side_rows(self, side):
        return rows_at(side * self.half, self.half, self.half)

    def rank_rows(self, rank):
        return rows_at(rank * self.piece, self.piece, self.piece)

    def own_rows(self):
        start = self.plane.side * self.half + self.plane.rank * self.piece
        return rows_at(start, self.piece, self.piece)

    def copies(self, stage):
        plane = self.plane
        if stage == 0:
            source = self.source.at[self.side_rows(1 - plane.side)]
            return [plane.remote(source, self.received, self.sems, 0, plane.partner(0))]
        if stage == self.stages - 1:
            here = self.wire.at[self.side_rows(plane.side)]
            return [plane.remote(here, here, self.sems, 1, plane.partner(0))]
        if 1 < stage < self.stages - 2:
            slot = plane.ranks + stage - 3
            index = 2 * plane.ranks + stage - 2
            device = plane.partner(plane.bits - plane.extra + stage - 2)
            return [plane.remote(self.sends.at[slot], self.receives.at[slot], self.sems, index, device)]
        copies = []
        for offset in range(1, plane.ranks):
            device = plane.ranked(offset)
            if stage == 1:
                slot = offset - 1
                copies.append(
                    plane.remote(self.sends.at[slot], self.receives.at[slot], self.sems, 1 + offset, device)
                )
            else:
                here = self.wire.at[self.own_rows()]
                copies.append(plane.remote(here, here, self.sems, plane.ranks + offset, device))
        return copies

    def start(self, stage):
        plane = self.plane
        if stage == 1:
            for offset in range(1, plane.ranks):
                rows = self.rank_rows(plane.other_rank(offset))
                self.sends[offset - 1] = self.part[rows, :].astype(LOW)
        elif 1 < stage < self.stages - 2:
            self.sends[plane.ranks + stage - 3] = self.part[self.rank_rows(plane.rank), :].astype(LOW)
        elif stage == self.stages - 2:
            self.wire[self.own_rows(), :] = self.part[self.rank_rows(plane.rank), :].astype(LOW)
        for copy in self.copies(stage):
            copy.start()

    def finish(self, stage):
        plane = self.plane
        for copy in self.copies(stage):
            copy.wait()
        if stage == 0:
            received = self.received[...].astype(FULL)
            self.part[...] = self.source[self.side_rows(plane.side), :].astype(FULL) + received
        elif stage == 1:
            value = self.part[self.rank_rows(plane.rank), :]
            for slot in range(plane.ranks - 1):
                value = value + self.receives[slot].astype(FULL)
            self.part[self.rank_rows(plane.rank), :] = value
        elif stage < self.stages - 2:
            slot = plane.ranks + stage - 3
            value = self.sends[slot].astype(FULL) + self.receives[slot].astype(FULL)
            self.part[self.rank_rows(plane.rank), :] = value


def direct_scratch(size, rows, width):
    ranks = min(4, size // 2)
    extra = (size // 2 // ranks).bit_length() - 1
    half = rows // 2
    pieces = pltpu.VMEM((ranks - 1 + extra, half // ranks, width), LOW)
    return [
        pltpu.VMEM((half, width), FULL),
        pltpu.VMEM((half, width), LOW),
        pieces,
        pieces,
        DMA((2, 2 * ranks + extra)),
    ]


class Events:
    def __init__(self, totals):
        self.totals = totals
        last = totals[0].stages - 1
        self.waiting = sorted(
            (2 * (stage - total.first) + index, index, stage)
            for index, total in enumerate(totals)
            for stage in range(total.first, last)
        )

    def start(self):
        for total in self.totals:
            total.start(total.first)

    def take(self, limit):
        ready = [event for event in self.waiting if event[0] < limit]
        self.waiting = [event for event in self.waiting if event[0] >= limit]
        for unused, index, stage in ready:
            self.totals[index].finish(stage)
            self.totals[index].start(stage + 1)

    def next(self, count):
        if self.waiting[:count]:
            self.take(self.waiting[min(count, len(self.waiting)) - 1][0] + 1)

    def end(self):
        self.take(1 << 20)
        for total in self.totals:
            total.finish(total.stages - 1)


def greet_all(team, plane, direct):
    barrier = pltpu.get_barrier_semaphore()
    others = [plane.partner(bit) for bit in range(plane.bits)]
    others += [team.device(team.sibling), team.device(team.far)]
    greeted = list(others)
    if direct:
        greeted = [plane.partner(0), team.device(team.sibling), team.device(team.far)]
        greeted += [plane.partner(plane.bits - plane.extra + index) for index in range(plane.extra)]
        greeted += [plane.ranked(offset) for offset in range(1, plane.ranks)]
    for other in greeted:
        pl.semaphore_signal(barrier, inc=1, device_id=other, device_id_type=MESH)
    pl.semaphore_wait(barrier, len(greeted))
    return others


def backward_kernel(
    keys_of,
    rows_of,
    head_count,
    size,
    spans,
    q_hbm,
    k_hbm,
    v_hbm,
    d_hbm,
    mixed_hbm,
    log_hbm,
    up_part,
    down_part,
    wo_part,
    out_far,
    dq_ref,
    dk_ref,
    dv_ref,
    up_sum,
    down_sum,
    wo_sum,
    out_in,
    d_rot,
    q_turned,
    d_turned,
    k_turned,
    q_heads,
    d_heads,
    dq_turned,
    dk_rot,
    dv_rot,
    log_rows,
    deltas,
    parts,
    wires,
    total_parts,
    wo_near,
    wo_far,
    wo_sems,
    out_sems,
    keep_sems,
    dq_side,
    q_rot,
    k_rot,
    v_rot,
    d_ref,
    mixed_rot_ref,
    log_ref,
    load_sems,
):
    length, width = q_rot.shape
    small = length - LONGEST
    offset, border = rotation(spans)
    low, full = jnp.bfloat16, jnp.float32
    team, plane = Team(), Plane(size)
    columns = wo_sum.shape[0]
    lanes_of = up_part.shape[1] // 2
    totals, loads = [], []
    for index, source in enumerate((up_part, up_part, down_part, down_part)):
        lanes = pl.ds((index % 2) * lanes_of, lanes_of)
        total = Halving(plane, parts.at[index], wires.at[index], index // 2 * 2, *total_parts[index])
        place = parts.at[index, total.inner(index // 2 * 2)]
        loads.append(pltpu.make_async_copy(source.at[:, lanes], place, keep_sems.at[index]))
        totals.append(total)
    for load in loads:
        load.start()
    events = Events(totals)
    greet_all(team, plane, False)
    for load in loads:
        load.wait()
    events.start()
    arrays = (
        (q_hbm, q_rot),
        (k_hbm, k_rot),
        (v_hbm, v_rot),
        (d_hbm, d_ref),
        (mixed_hbm, mixed_rot_ref),
        (log_hbm, log_ref),
    )
    fetches = loads_of(arrays, load_sems)
    for fetch in fetches:
        fetch.start()
    out_copy = team.copy(out_far, out_in, out_sems.at[0], out_sems.at[1], team.far)
    out_copy.start()

    def wo_rows(owner):
        return rows_at(owner * columns, columns, 64)

    wo_copies = [
        team.copy(wo_part.at[wo_rows(owner)], wo_near.at[slot], wo_sems.at[0, slot], wo_sems.at[1, slot], team.sibling)
        for slot, owner in enumerate((team.sibling, team.diagonal))
    ]
    for copy in wo_copies:
        copy.start()
    wo_across = team.copy(wo_far.at[0], wo_far.at[1], wo_sems.at[0, 2], wo_sems.at[1, 2], team.far)

    for fetch in fetches:
        fetch.wait()
    rotate_into(d_ref, d_rot, dq_turned, offset)
    q_all, k_all, d_all = q_rot[...], k_rot[...], d_rot[...]
    q_turned[...] = jnp.transpose(q_all)
    k_turned[...] = jnp.transpose(k_all)
    d_turned[...] = jnp.transpose(d_all)
    for head in range(head_count):
        q_heads[head] = keep_head(head, q_all)
        d_heads[head] = keep_head(head, d_all)
    products = jnp.transpose(d_all.astype(full) * mixed_rot_ref[0 : length // 8].reshape(length, width))
    for head in range(head_count):
        deltas[head : head + 1, :] = jnp.sum(products[head * HEAD : (head + 1) * HEAD, :], axis=0, keepdims=True)
    log_rows[...] = jnp.transpose(log_ref[...])[0:8, :]
    dq_side[...] = jnp.zeros_like(dq_side)

    def block(key_row, row_base, row_count, masked, before):
        keys = pl.ds(key_row, keys_of)
        dk_sum = jnp.zeros((keys_of, width), full)
        dv_sum = jnp.zeros((keys_of, width), full)
        for head in range(head_count):
            before(head)
            k_head = keep_head(head, k_rot[keys, :])
            v_head = keep_head(head, v_rot[keys, :])
            lanes = slice(head * HEAD, (head + 1) * HEAD)
            k_side = k_turned[lanes, keys]
            for chunk in range(row_count // rows_of):
                start = row_base + chunk * rows_of
                rows = slice(start, start + rows_of)
                scores = dot(k_head, q_turned[:, rows], NN)
                dprobs = dot(v_head, d_turned[:, rows], NN)
                probs = jnp.exp2(scores * LOG_SCALE - log_rows[head : head + 1, rows])
                if masked:
                    shape = (keys_of, rows_of)
                    key_id = lax.broadcasted_iota(jnp.int32, shape, 0) + (key_row - LONGEST)
                    row_id = lax.broadcasted_iota(jnp.int32, shape, 1) + chunk * rows_of
                    probs = jnp.where((row_id < border) == (key_id < border), probs, 0.0)
                dv_sum = dv_sum + dot(probs.astype(low), d_heads[head, rows, :], NN)
                draw = (probs * (dprobs - deltas[head : head + 1, rows])).astype(low)
                dk_sum = dk_sum + dot(draw, q_heads[head, rows, :], NN)
                dq_side[lanes, rows] += dot(k_side, draw, NN)
        groups = pl.ds(lax.div(key_row, 8), keys_of // 8)
        dk_rot[groups] = (dk_sum * SCALE).reshape(keys_of // 8, 8, width)
        dv_rot[groups] = dv_sum.reshape(keys_of // 8, 8, width)

    trips = LONGEST // keys_of

    def gather_wo():
        for copy in wo_copies:
            copy.wait()
        wo_far[0] = (wo_part[wo_rows(team.far), :].astype(full) + wo_near[1].astype(full)).astype(low)
        wo_across.start()

    def large(index, nothing):
        def before(head):
            for trip in range(trips):
                slot = trip * head_count + head
                limit = (slot * 2 + 3) // 5
                earlier = (slot * 2 + 1) // 5
                if limit > earlier:

                    @pl.when(index == trip)
                    def _(limit=limit, slot=slot):
                        events.waiting = [event for event in everything if event[0] >= earlier]
                        events.take(limit)
                        if slot == 1:
                            gather_wo()

        block(pl.multiple_of(index * keys_of, keys_of), 0, LONGEST, False, before)
        return nothing

    def little(index, nothing):
        block(
            pl.multiple_of(LONGEST + index * keys_of, keys_of), LONGEST, small, True, lambda head: None
        )
        return nothing

    everything = list(events.waiting)
    lax.fori_loop(0, trips, large, 0)
    slots = trips * head_count
    events.waiting = [event for event in everything if event[0] >= slots // 2]
    lax.fori_loop(0, small // keys_of, little, 0)

    def unrotate(buffer, target):
        wrap(buffer, length)

        def put(index, block_rows):
            target[rows_at(index * 256, 256, 256), :] = block_rows.astype(low)

        rotate(buffer, length - offset, length, put)

    unrotate(dk_rot, dk_ref)
    unrotate(dv_rot, dv_ref)
    dq_turned[0 : length // 8] = jnp.transpose(dq_side[...] * SCALE).reshape(length // 8, 8, width)
    unrotate(dq_turned, dq_ref)
    events.end()
    keeps = []
    for index, target in enumerate((up_sum, up_sum, down_sum, down_sum)):
        lanes = pl.ds((index % 2) * lanes_of, lanes_of)
        keeps.append(pltpu.make_async_copy(wires.at[index], target.at[:, lanes], keep_sems.at[index]))
    for keep in keeps:
        keep.start()
    wo_across.wait()
    mine = wo_part[wo_rows(team.me), :].astype(full) + wo_near[0].astype(full)
    wo_sum[...] = (mine + wo_far[1].astype(full)).astype(low)
    out_copy.wait()
    for keep in keeps:
        keep.wait()


def attend_backward(
    size, spans, q_rot, k_rot, v_rot, grad_mixed, mixed_rot, log_totals, up_part, down_part, wo_part, out_far
):
    length, width = q_rot.shape
    head_count = width // HEAD
    low, full = jnp.bfloat16, jnp.float32
    half = (up_part.shape[0], up_part.shape[1] // 2)
    whole = (2 * up_part.shape[0], up_part.shape[1])
    wo_shape = (wo_part.shape[0] // 4, wo_part.shape[1])

    def shape(dims):
        return jax.ShapeDtypeStruct(dims, low)

    grouped = (length // 8 + EXTRA, 8, width)
    return pl.pallas_call(
        functools.partial(backward_kernel, 256, 512, head_count, size),
        out_shape=(shape((length, width)),) * 3
        + (shape(whole), shape(whole), shape(wo_shape), shape(out_far.shape)),
        in_specs=[SMEM] + [ANY] * 8 + [VMEM, ANY],
        out_specs=(VMEM,) * 3 + (ANY, ANY, VMEM, ANY),
        scratch_shapes=[
            pltpu.VMEM((length, width), low),
            pltpu.VMEM((width, length), low),
            pltpu.VMEM((width, length), low),
            pltpu.VMEM((width, length), low),
            pltpu.VMEM((head_count, length, width), low),
            pltpu.VMEM((head_count, length, width), low),
            pltpu.VMEM(grouped, full),
            pltpu.VMEM(grouped, full),
            pltpu.VMEM(grouped, full),
            pltpu.VMEM((8, length), full),
            pltpu.VMEM((8, length), full),
            pltpu.VMEM((4, *half), full),
            pltpu.VMEM((4, 2 * half[0], half[1]), low),
            [halving_scratch(size, *half) for unused in range(4)],
            pltpu.VMEM((2, *wo_shape), low),
            pltpu.VMEM((2, *wo_shape), low),
            DMA((2, 3)),
            DMA((2,)),
            DMA((4,)),
            pltpu.VMEM((width, length), full),
            pltpu.VMEM((length, width), low),
            pltpu.VMEM((length, width), low),
            pltpu.VMEM((length, width), low),
            pltpu.VMEM((length, width), low),
            pltpu.VMEM(mixed_rot.shape, full),
            pltpu.VMEM(log_totals.shape, full),
            DMA((6,)),
        ],
        compiler_params=pltpu.CompilerParams(
            collective_id=3, has_side_effects=True, vmem_limit_bytes=63 << 20
        ),
        name="attend_backward",
    )(spans, q_rot, k_rot, v_rot, grad_mixed, mixed_rot, log_totals, up_part, down_part, wo_part, out_far)


def project_kernel(
    part,
    x_ref,
    gain,
    shift,
    wq,
    bq,
    wk,
    wv,
    bv,
    x_all,
    normed,
    q_ref,
    k_ref,
    v_ref,
    landing,
    far_send,
    far_recv,
    near_send,
    near_recv,
    pass_send,
    pass_recv,
    keep_sem,
):
    team = Team()
    own = x_ref.shape[0]
    count = own // part

    def piece(owner, index):
        return rows_at(owner * own + index * part, part, part)

    def far_copy(index):
        source = x_ref.at[rows_at(index * part, part, part)]
        return team.copy(
            source, landing.at[piece(team.me, index)], far_send.at[index], far_recv.at[index], team.far
        )

    def pass_copy(index):
        place = landing.at[piece(team.far, index)]
        return team.copy(place, place, pass_send.at[index], pass_recv.at[index], team.sibling)

    near = team.copy(
        x_ref, landing.at[rows_at(team.me * own, own, own)], near_send, near_recv, team.sibling
    )

    def keep(owner, source, slot):
        return pltpu.make_async_copy(source, x_all.at[rows_at(owner * own, own, own)], keep_sem.at[slot])

    team.greet((team.sibling, team.far))
    for index in range(count):
        far_copy(index).start()
    near.start()
    keep(team.me, x_ref, 0).start()

    gain_row, shift_row, bq_row, bv_row = as_row(gain), as_row(shift), as_row(bq), as_row(bv)

    def project(owner, index, values):
        standard, unused = standardize(values.astype(FULL))
        low = (standard * gain_row + shift_row).astype(LOW)
        rows = piece(owner, index)
        normed[rows, :] = low
        q_ref[rows, :] = (dot(low, wq[...], NT) + bq_row).astype(LOW)
        k_ref[rows, :] = dot(low, wk[...], NT).astype(LOW)
        v_ref[rows, :] = (dot(low, wv[...], NT) + bv_row).astype(LOW)

    def mine(index, nothing):
        project(team.me, index, x_ref[rows_at(index * part, part, part), :])
        return nothing

    lax.fori_loop(0, count, mine, 0)
    near.wait()

    def next_to(index, nothing):
        project(team.sibling, index, landing[piece(team.sibling, index), :])
        return nothing

    lax.fori_loop(0, count, next_to, 0)

    def across(index, nothing):
        far_copy(index).wait_recv()
        pass_copy(index).start()
        project(team.far, index, landing[piece(team.far, index), :])
        pass_copy(index).wait_recv()
        project(team.diagonal, index, landing[piece(team.diagonal, index), :])
        return nothing

    lax.fori_loop(0, count, across, 0)
    for slot, owner in ((1, team.sibling), (2, team.far), (3, team.diagonal)):
        keep(owner, landing.at[rows_at(owner * own, own, own)], slot).start()
    for slot, owner in ((1, team.sibling), (2, team.far), (3, team.diagonal)):
        keep(owner, landing.at[rows_at(owner * own, own, own)], slot).wait()
    keep(team.me, x_ref, 0).wait()
    for index in range(count):
        far_copy(index).wait_send()
        pass_copy(index).wait_send()


def gather_and_project(x, gain, shift, wq, bq, wk, wv, bv):
    own, width = x.shape
    length, columns, part = 4 * own, wq.shape[0], 128
    count = own // part
    narrow = jax.ShapeDtypeStruct((length, columns), LOW)
    wide = jax.ShapeDtypeStruct((length, width), LOW)
    return pl.pallas_call(
        functools.partial(project_kernel, part),
        out_shape=(wide, wide, narrow, narrow, narrow),
        in_specs=[VMEM] * 8,
        out_specs=(ANY, VMEM, VMEM, VMEM, VMEM),
        scratch_shapes=[
            pltpu.VMEM((length, width), LOW),
            DMA((count,)),
            DMA((count,)),
            DMA,
            DMA,
            DMA((count,)),
            DMA((count,)),
            DMA((4,)),
        ],
        compiler_params=pltpu.CompilerParams(
            collective_id=0, has_side_effects=True, vmem_limit_bytes=63 << 20
        ),
        name="gather_and_project",
    )(x, gain, shift, wq, bq, wk, wv, bv)


class Reduction:
    def __init__(self, team, near_out, near_in, far_out, far_in, sems):
        self.team = team
        self.near_out, self.near_in, self.far_out, self.far_in = near_out, near_in, far_out, far_in
        self.sems = sems

    def near(self, pair):
        return self.team.copy(
            self.near_out.at[pair % 2],
            self.near_in.at[pair],
            self.sems.at[0, pair],
            self.sems.at[1, pair],
            self.team.sibling,
        )

    def across(self, pair):
        return self.team.copy(
            self.far_out.at[pair], self.far_in.at[pair], self.sems.at[2, pair], self.sems.at[3, pair], self.team.far
        )

    def give(self, pair, values):
        @pl.when(pair >= 2)
        def _():
            self.near(pair - 2).wait_send()

        self.near_out[pair % 2] = values.astype(LOW)
        self.near(pair).start()

    def combine(self, pair, values):
        self.near(pair).wait_recv()
        return values + self.near_in[pair].astype(FULL)

    def send(self, pair, values):
        self.far_out[pair] = values.astype(LOW)
        self.across(pair).start()

    def arrived(self, pair):
        self.across(pair).wait_recv()
        return self.far_in[pair].astype(FULL)

    def finish(self, pairs):
        for pair in range(pairs // 2):
            self.across(pair).wait_send()
        for pair in (pairs - 2, pairs - 1):
            self.near(pair).wait_send()


def owner_at(team_me, step):
    half = lax.div(step, 4)
    odd = lax.rem(step, 2)
    one = flip(team_me, 0)
    base = one + odd * (team_me - one)
    return lax.rem(base + 2 * (1 - half), 4)


def part_at(step):
    return lax.rem(lax.div(step, 2), 2)


def ffn_kernel(
    part,
    size,
    mixed_hbm,
    pieces_hbm,
    x_hbm,
    cot_ref,
    wo_hbm,
    up_hbm,
    down_hbm,
    up_bias,
    out_bias,
    gain,
    shift,
    down_bias,
    out_far,
    out_own,
    grad_middle,
    grad_mixed,
    up_part,
    down_part,
    grad_wo,
    sums,
    middle_own,
    up_half,
    down_half,
    halves_out,
    halves_in,
    half_sems,
    halving_parts,
    keep_sems,
    cot_all,
    normed_all,
    hidden_all,
    gpre_all,
    out_slots,
    out_near,
    own_sum,
    near_out,
    near_in,
    far_out,
    far_in,
    mixed_out,
    branch_own,
    cot_sems,
    slot_sems,
    red_sems,
    a2a_sems,
    mixed_ref,
    pieces,
    x_all,
    wo,
    up,
    down,
    load_sems,
):
    team = Team()
    length = mixed_ref.shape[0]
    width = x_all.shape[1]
    columns = mixed_ref.shape[1]
    own = length // 4
    steps = length // part

    def rows_of(owner, index):
        return rows_at(owner * own + index * part, part, part)

    def step_rows(device, step):
        return rows_of(owner_at(device, step), part_at(step))

    spreads = [
        Spread(
            team,
            cot_ref.at[pl.ds(index * part, part)],
            cot_all,
            lambda owner, index=index: rows_of(owner, index),
            cot_sems.at[index],
        )
        for index in range(own // part)
    ]
    reduction = Reduction(team, near_out, near_in, far_out, far_in, red_sems)

    def slot_copy(pair):
        slot = lax.rem(pair, 2)
        return team.copy(
            out_slots.at[slot], out_near.at[pair], slot_sems.at[0, slot], slot_sems.at[1, pair], team.sibling
        )

    plane = Plane(size)
    team.greet((team.sibling, team.far, team.diagonal), *[plane.partner(bit) for bit in range(3)])

    for spread in spreads:
        spread.start()
    arrays = (mixed_hbm, mixed_ref), (pieces_hbm, pieces), (x_hbm, x_all), (wo_hbm, wo), (up_hbm, up), (down_hbm, down)
    loads = loads_of(arrays, load_sems)
    for load in loads:
        load.start()
    for load in loads:
        load.wait()
    sums[...] = jnp.zeros_like(sums)
    gain_row, shift_row, bias_row = as_row(gain), as_row(shift), as_row(out_bias)
    up_row, down_row = as_row(up_bias), as_row(down_bias)

    def forward(step, keep_middle):
        rows = step_rows(team.me, step)

        def weights(owner):
            return wo[rows_at(owner * columns, columns, 64), :]

        branch = dot(mixed_ref[rows, :], weights(team.me), NN)
        branch = branch + dot(pieces[0, rows, :], weights(team.sibling), NN)
        branch = branch + dot(pieces[1, rows, :], weights(team.far), NN)
        branch = branch + dot(pieces[2, rows, :], weights(team.diagonal), NN)
        middle = x_all[rows, :].astype(FULL) + (branch + bias_row)
        if keep_middle:

            @pl.when(step >= steps // 2)
            def _():
                middle_own[rows_at(part_at(step) * part, part, part), :] = middle

        standard, unused = standardize(middle)
        low = (standard * gain_row + shift_row).astype(LOW)
        normed_all[rows, :] = low
        pre = dot(low, up[...], NN) + up_row
        bell = 0.5 * (1.0 + lax.erf(pre * 0.7071067811865476))
        hidden = (pre * bell).astype(LOW)
        hidden_all[rows, :] = hidden
        slope = bell + pre * (jnp.exp(pre * pre * -0.5) * 0.3989422804014327)
        gpre_all[rows, :] = slope.astype(LOW)

        out = dot(hidden, down[...], NN)
        pair = lax.div(step, 2)
        if keep_middle:
            place = rows_at(part_at(step) * part, part, part)

            @pl.when(step < steps // 2)
            def _():
                out_far[place, :] = out.astype(LOW)

            @pl.when(step >= steps // 2)
            def _():
                out_own[place, :] = middle + out + down_row
        else:

            @pl.when(pair >= 2)
            def _():
                slot_copy(pair - 2).wait_send()

            out_slots[lax.rem(pair, 2)] = out.astype(LOW)
            slot_copy(pair).start()
    def backward(step):
        rows = step_rows(team.me, step)
        slope = gpre_all[rows, :].astype(FULL)
        grad_pre = (dot(cot_all[rows, :], down[...], NT) * slope).astype(LOW)
        gpre_all[rows, :] = grad_pre
        sums[4:5, :] += column_sums(grad_pre.astype(FULL))
        return dot(grad_pre, up[...], NT)

    def pair_forward(pair, nothing):
        forward(2 * pair, False)
        forward(2 * pair + 1, True)
        return nothing

    half = width // 2
    down_total = Halving(plane, down_half, None, 0, *halving_parts)
    up_keep = pltpu.make_async_copy(up_half, up_part, keep_sems.at[0])
    down_keep = pltpu.make_async_copy(down_half.at[down_total.inner(2)], down_part, keep_sems.at[1])
    halves = (normed_all, gpre_all, up_half), (hidden_all, cot_all, down_half)
    side_copies = [
        plane.remote(halves_out.at[index], halves_in.at[index], half_sems, index, plane.partner(0))
        for index in range(2)
    ]
    def place_of(pair):
        return rows_at(part_at(2 * pair) * part, part, part)

    def add_out(pair):
        slot_copy(pair).wait_recv()
        place, given = place_of(pair), out_near[pair].astype(FULL)

        @pl.when(pair < steps // 4)
        def _():
            out_far[place, :] = (out_far[place, :].astype(FULL) + given).astype(LOW)

        @pl.when(pair >= steps // 4)
        def _():
            out_own[place, :] += given

    def combine(pair):
        reduction.near(pair).wait_recv()
        given = reduction.near_in[pair].astype(FULL)

        @pl.when(pair < steps // 4)
        def _():
            reduction.send(pair, reduction.far_out[lax.rem(pair, 2)].astype(FULL) + given)

        @pl.when(pair >= steps // 4)
        def _():
            own_sum[place_of(pair), :] += given

    def pair_backward(pair, nothing):
        first, second = 2 * pair, 2 * pair + 1
        for index, spread in enumerate(spreads):

            @pl.when(pair == index)
            def _(spread=spread):
                spread.middle()
                spread.passed().wait_recv()

        @pl.when(pair == len(spreads))
        def _():
            for spread in spreads:
                spread.near().wait_recv()
                spread.kept().wait()
            side_half(1)

        @pl.when(pair == len(spreads) + 1)
        def _():
            own_half(1)

        reduction.give(pair, backward(first))
        add_out(pair)

        @pl.when(pair >= 1)
        def _():
            combine(pair - 1)

        values = backward(second)

        @pl.when(pair < steps // 4)
        def _():
            far_out[lax.rem(pair, 2)] = values.astype(LOW)

        @pl.when(pair >= steps // 4)
        def _():
            own_sum[place_of(pair), :] = values

        return nothing

    def side_half(index):
        left, right, unused = halves[index]
        lanes = rows_at((1 - plane.side) * half, half, half)

        def one(slab, nothing):
            columns_of = rows_at(slab * 256, 256, 256)
            halves_out[index, :, columns_of] = dot(left[:, lanes], right[:, columns_of], TN).astype(LOW)
            return nothing

        lax.fori_loop(0, width // 256, one, 0)
        side_copies[index].start()

    def own_half(index):
        left, right, target = halves[index]
        lanes = rows_at(plane.side * half, half, half)

        def one(slab, nothing):
            columns_of = rows_at(slab * 256, 256, 256)
            target[:, columns_of] = dot(left[:, lanes], right[:, columns_of], TN)
            return nothing

        lax.fori_loop(0, width // 256, one, 0)

    def add_side(index):
        side_copies[index].wait()
        halves[index][2][...] += halves_in[index].astype(FULL)

    lax.fori_loop(0, steps // 2, pair_forward, 0)
    lax.fori_loop(0, steps // 2, pair_backward, 0)
    side_half(0)
    add_side(1)
    down_total.start(0)
    combine(steps // 2 - 1)

    def back(index, nothing):
        @pl.when(index == 1)
        def _():
            down_total.finish(0)
            down_total.start(1)

        rows = rows_at(index * part, part, part)
        own_rows = rows_of(team.me, index)
        grad = own_sum[rows, :] + reduction.arrived(index)
        standard, inverse = standardize(middle_own[rows, :])
        incoming = cot_all[own_rows, :].astype(FULL)
        grad_mid = incoming + norm_back(grad, gain_row, standard, inverse)
        grad_middle[rows, :] = grad_mid
        branch_low = grad_mid.astype(LOW)
        branch_own[rows, :] = branch_low
        for slot, owner in enumerate((team.sibling, team.far, team.diagonal)):
            side = wo[rows_at(owner * columns, columns, 64), :]
            mixed_out[slot, rows, :] = dot(branch_low, side, NT).astype(LOW)
            exchange(index, slot, owner).start()
        side = wo[rows_at(team.me * columns, columns, 64), :]
        grad_mixed[own_rows, :] = dot(branch_low, side, NT).astype(LOW)
        sums[0:1, :] += column_sums(grad * standard)
        sums[1:2, :] += column_sums(grad)
        sums[2:3, :] += column_sums(branch_low.astype(FULL))
        sums[3:4, :] += column_sums(incoming)
        return nothing

    def exchange(index, slot, owner):
        return team.copy(
            mixed_out.at[slot, rows_at(index * part, part, part)],
            grad_mixed.at[rows_of(team.me, index)],
            a2a_sems.at[2 * index, slot],
            a2a_sems.at[2 * index + 1, slot],
            owner,
        )

    lax.fori_loop(0, own // part, back, 0)
    own_half(0)
    own_rows = rows_at(team.me * own, own, own)
    for source, owner in (
        (mixed_ref.at[own_rows], team.me),
        (pieces.at[0, own_rows], team.sibling),
        (pieces.at[1, own_rows], team.far),
        (pieces.at[2, own_rows], team.diagonal),
    ):
        grad_wo[rows_at(owner * columns, columns, 64), :] = dot(source[...], branch_own[...], TN).astype(LOW)
    down_total.finish(1)
    down_keep.start()
    add_side(0)
    up_keep.start()
    for index in range(own // part):
        for slot, owner in enumerate((team.sibling, team.far, team.diagonal)):
            exchange(index, slot, owner).wait()
    down_keep.wait()
    up_keep.wait()
    for spread in spreads:
        spread.sent()
    for pair in (steps // 2 - 2, steps // 2 - 1):
        slot_copy(pair).wait_send()
    reduction.finish(steps // 2)


def ffn(size, mixed, pieces, x_all, cotangent, wo, up, down, up_bias, out_bias, gain, shift, down_bias):
    length, columns = mixed.shape
    width = x_all.shape[1]
    hidden = up.shape[1]
    own, part = length // 4, 320
    steps = length // part
    pairs = steps // 2

    def shape(dims, kind):
        return jax.ShapeDtypeStruct(dims, kind)

    return pl.pallas_call(
        functools.partial(ffn_kernel, part, size),
        out_shape=(
            shape((own, width), LOW),
            shape((own, width), FULL),
            shape((own, width), FULL),
            shape((length, columns), LOW),
            shape((width // 2, hidden), FULL),
            shape((hidden // 8, width), FULL),
            shape((width, width), LOW),
            shape((8, width), FULL),
        ),
        in_specs=[ANY] * 7 + [VMEM] * 5,
        out_specs=(VMEM,) * 4 + (ANY, ANY, VMEM, VMEM),
        scratch_shapes=[
            pltpu.VMEM((own, width), FULL),
            pltpu.VMEM((width // 2, hidden), FULL),
            pltpu.VMEM((hidden // 2, width), FULL),
            pltpu.VMEM((2, width // 2, width), LOW),
            pltpu.VMEM((2, width // 2, width), LOW),
            DMA((2, 2)),
            halving_scratch(size, width // 2, width),
            DMA((2,)),
            pltpu.VMEM((length, width), LOW),
            pltpu.VMEM((length, width), LOW),
            pltpu.VMEM((length, hidden), LOW),
            pltpu.VMEM((length, hidden), LOW),
            pltpu.VMEM((2, part, width), LOW),
            pltpu.VMEM((pairs, part, width), LOW),
            pltpu.VMEM((own, width), FULL),
            pltpu.VMEM((2, part, width), LOW),
            pltpu.VMEM((pairs, part, width), LOW),
            pltpu.VMEM((pairs // 2, part, width), LOW),
            pltpu.VMEM((pairs // 2, part, width), LOW),
            pltpu.VMEM((3, own, columns), LOW),
            pltpu.VMEM((own, width), LOW),
            DMA((own // part, 7)),
            DMA((2, pairs)),
            DMA((4, pairs)),
            DMA((4, 3)),
            pltpu.VMEM(mixed.shape, LOW),
            pltpu.VMEM(pieces.shape, LOW),
            pltpu.VMEM(x_all.shape, LOW),
            pltpu.VMEM(wo.shape, LOW),
            pltpu.VMEM(up.shape, LOW),
            pltpu.VMEM(down.shape, LOW),
            DMA((6,)),
        ],
        compiler_params=pltpu.CompilerParams(
            collective_id=2, has_side_effects=True, vmem_limit_bytes=63 << 20
        ),
        name="ffn",
    )(mixed, pieces, x_all, cotangent, wo, up, down, up_bias, out_bias, gain, shift, down_bias)


def last_kernel(
    part,
    size,
    dq_hbm,
    dk_hbm,
    dv_hbm,
    wq,
    wk,
    wv,
    normed_hbm,
    x_hbm,
    grad_hbm,
    gain,
    wo_sum,
    wide,
    input_grad,
    grad_sum,
    vectors,
    own_grad,
    near_out,
    near_in,
    far_out,
    far_in,
    red_sems,
    sources,
    wires,
    total_parts,
    packed,
    packed_in,
    vec_sems,
    keep_sems,
    dq_ref,
    dk_ref,
    dv_ref,
    normed_all,
    x_all,
    grad_middle,
    load_sems,
):
    team, plane = Team(), Plane(size)
    arrays = (
        (dq_hbm, dq_ref),
        (dk_hbm, dk_ref),
        (dv_hbm, dv_ref),
        (normed_hbm, normed_all),
        (x_hbm, x_all),
        (grad_hbm, grad_middle),
    )
    loads = loads_of(arrays, load_sems)
    for load in loads:
        load.start()
    length, columns = dq_ref.shape
    width = normed_all.shape[1]
    own = length // 4
    pairs = length // part // 2
    grads = Reduction(team, near_out, near_in, far_out, far_in, red_sems)
    slabs = sources.shape[0]
    lanes_of = width // slabs
    totals = [Direct(plane, sources.at[slab], wires.at[slab], *total_parts[slab]) for slab in range(slabs)]
    others = greet_all(team, plane, True)
    events = Events(totals)

    def slab_grads(slab, nothing):
        lanes = rows_at(slab * lanes_of, lanes_of, lanes_of)
        for index, source in enumerate((dq_ref, dk_ref, dv_ref)):
            value = dot(source[...], normed_all[:, lanes], TN)
            sources[slab, index * columns : (index + 1) * columns, :] = value.astype(LOW)
        sources[slab, 3 * columns : 4 * columns, :] = wo_sum[:, lanes]
        for index, total in enumerate(totals):

            @pl.when(slab == index)
            def _(total=total):
                total.start(0)

        return nothing

    for load in loads[:4]:
        load.wait()
    lax.fori_loop(0, slabs, slab_grads, 0)
    for load in loads[4:]:
        load.wait()
    gain_row = as_row(gain)
    packed[...] = jnp.zeros_like(packed)
    packed[0:4, :] = wide[0:4, :]
    packed[8:9, :] = wide[4:5, :]
    packed[9:10, 0:columns] = column_sums(dq_ref[...].astype(FULL))
    packed[10:11, 0:columns] = column_sums(dv_ref[...].astype(FULL))

    def step_rows(step):
        return rows_at(owner_at(team.me, step) * own + part_at(step) * part, part, part)

    def compute(step):
        rows = step_rows(step)
        total = dot(dq_ref[rows, :], wq[...], NN) + dot(dk_ref[rows, :], wk[...], NN)
        return total + dot(dv_ref[rows, :], wv[...], NN)

    everything = list(events.waiting)

    def events_at(pair, plan):
        for when, (start, stop) in plan.items():

            @pl.when(pair == when)
            def _(start=start, stop=stop):
                events.waiting = everything[start:stop]
                events.take(1 << 20)

    def pair_step(pair, nothing):
        first, second = 2 * pair, 2 * pair + 1
        grads.give(pair, compute(first))
        standard, unused = standardize(x_all[step_rows(second), :].astype(FULL))
        events_at(pair, {1: (0, 1), 2: (1, 2), 3: (2, 4)})
        values = grads.combine(pair, compute(second))
        packed[4:5, :] += column_sums(values * standard)
        packed[5:6, :] += column_sums(values)

        @pl.when(pair < pairs // 2)
        def _():
            grads.send(pair, values)

        @pl.when(pair >= pairs // 2)
        def _():
            own_grad[rows_at(part_at(second) * part, part, part), :] = values

        events_at(pair, {3: (4, 5)})
        return nothing

    lax.fori_loop(0, pairs, pair_step, 0)
    events.waiting = everything[5:]

    def vector_copy(step):
        return pltpu.make_async_remote_copy(
            src_ref=packed.at[pl.ds(16 * step, 16)],
            dst_ref=packed_in.at[step],
            send_sem=vec_sems.at[0, step],
            recv_sem=vec_sems.at[1, step],
            device_id=others[step],
            device_id_type=MESH,
        )

    def finish_rows(index):
        rows = pl.ds(index * part, part)
        grad = own_grad[rows, :] + grads.arrived(index)
        standard, inverse = standardize(x_all[rows_at(team.me * own + index * part, part, part), :].astype(FULL))
        input_grad[rows, :] = grad_middle[rows, :] + norm_back(grad, gain_row, standard, inverse)

    for step in range(len(others)):
        vector_copy(step).start()
        events.next(1)
        vector_copy(step).wait()
        here = packed[16 * step : 16 * (step + 1), :]
        keep = 16 if step < plane.bits else 8
        row = lax.broadcasted_iota(jnp.int32, here.shape, 0)
        added = here + jnp.where(row < keep, packed_in[step], 0.0)
        packed[16 * (step + 1) : 16 * (step + 2), :] = added
    vectors[...] = packed[16 * len(others) : 16 * (len(others) + 1), :]
    events.take(1 << 20)
    for index in range(own // part):
        finish_rows(index)
    events.end()
    keeps = []
    for slab in range(slabs):
        lanes = pl.ds(slab * lanes_of, lanes_of)
        keeps.append(pltpu.make_async_copy(wires.at[slab], grad_sum.at[:, lanes], keep_sems.at[slab]))
    for keep in keeps:
        keep.start()
    for keep in keeps:
        keep.wait()
    grads.finish(pairs)


def last(size, dq, dk, dv, wq, wk, wv, normed_all, x_all, grad_middle, gain, wo_sum, wide):
    length, columns = dq.shape
    own, width = grad_middle.shape
    part, slabs = 320, 3
    pairs = length // part // 2
    bits = size.bit_length() - 1
    slab = (4 * columns, width // slabs)

    def shape(dims, kind):
        return jax.ShapeDtypeStruct(dims, kind)

    return pl.pallas_call(
        functools.partial(last_kernel, part, size),
        out_shape=(
            shape((own, width), FULL),
            shape((4 * columns, width), LOW),
            shape((16, width), FULL),
        ),
        in_specs=[ANY] * 3 + [VMEM] * 3 + [ANY] * 3 + [VMEM] * 3,
        out_specs=(VMEM, ANY, VMEM),
        scratch_shapes=[
            pltpu.VMEM((own, width), FULL),
            pltpu.VMEM((2, part, width), LOW),
            pltpu.VMEM((pairs, part, width), LOW),
            pltpu.VMEM((pairs // 2, part, width), LOW),
            pltpu.VMEM((pairs // 2, part, width), LOW),
            DMA((4, pairs)),
            pltpu.VMEM((slabs, *slab), LOW),
            pltpu.VMEM((slabs, *slab), LOW),
            [direct_scratch(size, *slab) for unused in range(slabs)],
            pltpu.VMEM((16 * (bits + 3), width), FULL),
            pltpu.VMEM((bits + 2, 16, width), FULL),
            DMA((2, bits + 2)),
            DMA((slabs,)),
            pltpu.VMEM(dq.shape, LOW),
            pltpu.VMEM(dk.shape, LOW),
            pltpu.VMEM(dv.shape, LOW),
            pltpu.VMEM(normed_all.shape, LOW),
            pltpu.VMEM(x_all.shape, LOW),
            pltpu.VMEM(grad_middle.shape, FULL),
            DMA((6,)),
        ],
        compiler_params=pltpu.CompilerParams(
            collective_id=4, has_side_effects=True, vmem_limit_bytes=60 << 20
        ),
        name="last",
    )(dq, dk, dv, wq, wk, wv, normed_all, x_all, grad_middle, gain, wo_sum, wide)


def local(
    size,
    layer_input,
    segment_ids,
    cotangent,
    attn_gain,
    attn_shift,
    query_weight,
    query_bias,
    key_weight,
    value_weight,
    value_bias,
    out_weight,
    out_bias,
    ffn_gain,
    ffn_shift,
    up_weight,
    up_bias,
    down_weight,
    down_bias,
):
    query_side, key_side, value_side = query_weight.T, key_weight.T, value_weight.T
    x_all, normed_rows, queries, key_rows, value_rows = gather_and_project(
        layer_input,
        attn_gain,
        attn_shift,
        query_side,
        query_bias,
        key_side,
        value_side,
        value_bias,
    )
    mixed, mixed_rot, log_totals, pieces, out_all, q_rot, k_rot, v_rot = attend_forward(
        segment_ids, queries, key_rows, value_rows, out_weight
    )
    out_far, out_own, grad_middle, grad_mixed, up_part, down_part, out_part, sums = ffn(
        size,
        mixed,
        pieces,
        x_all,
        cotangent,
        out_all,
        up_weight,
        down_weight,
        up_bias,
        out_bias,
        ffn_gain,
        ffn_shift,
        down_bias,
    )
    dq, dk, dv, grad_up, grad_down, wo_sum, out_in = attend_backward(
        size, segment_ids, q_rot, k_rot, v_rot, grad_mixed, mixed_rot, log_totals, up_part, down_part, out_part, out_far
    )
    layer_output = (out_own + out_in.astype(FULL)).astype(LOW)
    input_grad, grads, vectors = last(
        size,
        dq,
        dk,
        dv,
        query_side,
        key_side,
        value_side,
        normed_rows,
        x_all,
        grad_middle,
        attn_gain,
        wo_sum,
        sums,
    )
    columns = query_side.shape[0]
    grads = grads.astype(FULL)
    return (
        layer_output,
        input_grad,
        vectors[4],
        vectors[5],
        grads[0:columns].T,
        vectors[9, 0:columns],
        grads[columns : 2 * columns].T,
        grads[2 * columns : 3 * columns].T,
        vectors[10, 0:columns],
        grads[3 * columns :],
        vectors[2],
        vectors[0],
        vectors[1],
        grad_up.astype(FULL),
        vectors[8],
        grad_down.astype(FULL),
        vectors[3],
    )


def solution(mesh):
    return jax.shard_map(
        functools.partial(local, mesh.shape["dp"]),
        mesh=mesh,
        in_specs=(
            P(("dp", "seq"), None),
            P("dp", None),
            P(("dp", "seq"), None),
            P(),
            P(),
            P(None, "seq"),
            P("seq"),
            P(None, "seq"),
            P(None, "seq"),
            P("seq"),
            P("seq", None),
            P(),
            P(),
            P(),
            P(None, "seq"),
            P("seq"),
            P("seq", None),
            P(),
        ),
        out_specs=(
            P(("dp", "seq"), None),
            P(("dp", "seq"), None),
            P(),
            P(),
            P(None, "seq"),
            P("seq"),
            P(None, "seq"),
            P(None, "seq"),
            P("seq"),
            P("seq", None),
            P(),
            P(),
            P(),
            P(None, "seq"),
            P("seq"),
            P("seq", None),
            P(),
        ),
        check_vma=False,
    )
```

```python
import functools

import jax
import jax.numpy as jnp
from jax import lax
from jax.experimental import pallas as pl
from jax.experimental.pallas import tpu as pltpu
from jax.sharding import PartitionSpec as P

HEAD = 64
SCALE = HEAD ** (-0.5)
LOG_SCALE = SCALE * 1.4426950408889634
LONGEST = 2048
EPSILON = 1e-06
NN = (((1,), (0,)), ((), ()))
NT = (((1,), (1,)), ((), ()))
TN = (((0,), (0,)), ((), ()))
MESH = pl.DeviceIdType.MESH
LOW = jnp.bfloat16
FULL = jnp.float32
VMEM = pl.BlockSpec(memory_space=pltpu.VMEM)
SMEM = pl.BlockSpec(memory_space=pltpu.SMEM)
ANY = pl.BlockSpec(memory_space=pl.ANY)
DMA = pltpu.SemaphoreType.DMA


def flip(index, bit):
    size = 1 << bit
    return index + size - 2 * size * lax.rem(lax.div(index, size), 2)


class Team:
    def __init__(self):
        self.row = lax.axis_index("dp")
        self.me = lax.axis_index("seq")
        self.sibling = flip(self.me, 0)
        self.far = flip(self.me, 1)
        self.diagonal = flip(self.sibling, 1)

    def device(self, index):
        return (self.row, index)

    def greet(self, others, *more):
        barrier = pltpu.get_barrier_semaphore()
        devices = [self.device(other) for other in others] + list(more)
        for device in devices:
            pl.semaphore_signal(barrier, inc=1, device_id=device, device_id_type=MESH)
        pl.semaphore_wait(barrier, len(devices))

    def copy(self, source, target, send, receive, other):
        return pltpu.make_async_remote_copy(
            src_ref=source,
            dst_ref=target,
            send_sem=send,
            recv_sem=receive,
            device_id=self.device(other),
            device_id_type=MESH,
        )


def loads_of(pairs, sems):
    return [pltpu.make_async_copy(source, target, sems.at[index]) for index, (source, target) in enumerate(pairs)]


def rows_at(start, count, multiple):
    return pl.ds(pl.multiple_of(start, multiple), count)


def standardize(values):
    average = jnp.mean(values, axis=-1, keepdims=True)
    centered = values - average
    variance = jnp.mean(centered * centered, axis=-1, keepdims=True)
    inverse = lax.rsqrt(variance + EPSILON)
    return centered * inverse, inverse


def norm_back(grad, gain_row, standard, inverse):
    scaled = grad * gain_row
    mean_one = jnp.mean(scaled, axis=-1, keepdims=True)
    mean_two = jnp.mean(scaled * standard, axis=-1, keepdims=True)
    return inverse * (scaled - mean_one - standard * mean_two)


def column_sums(values):
    return jnp.sum(values, axis=0, keepdims=True)


def first_at_least(segments, value):
    length = segments.shape[1]

    def halve(unused, ends):
        low, high = ends
        middle = jnp.minimum(lax.div(low + high, 2), length - 1)
        below = segments[0, middle] < value
        open_yet = low < high
        return (
            jnp.where(open_yet & below, middle + 1, low),
            jnp.where(open_yet & jnp.logical_not(below), middle, high),
        )

    return lax.fori_loop(0, length.bit_length(), halve, (jnp.int32(0), jnp.int32(length)))[0]


def rotation(segments):
    length = segments.shape[1]
    one, two = first_at_least(segments, 1), first_at_least(segments, 2)
    offset = jnp.where(one == LONGEST, 0, jnp.where(two - one == LONGEST, one, two))
    border = jnp.where(one == LONGEST, two - one, jnp.where(two - one == LONGEST, length - two, one))
    return offset, border


def as_row(ref):
    return ref[...].astype(FULL).reshape(1, -1)


def dot(left_side, right_side, dims):
    return lax.dot_general(left_side, right_side, dims, preferred_element_type=jnp.float32)


def keep_head(head, values):
    lane = lax.broadcasted_iota(jnp.int32, values.shape, 1)
    inside = (lane >= head * HEAD) & (lane < (head + 1) * HEAD)
    return jnp.where(inside, values, jnp.zeros_like(values))


class Spread:
    def __init__(self, team, source, target, rows_of, sems):
        self.team, self.source, self.target, self.rows_of, self.sems = team, source, target, rows_of, sems

    def place(self, owner):
        return self.target.at[self.rows_of(owner)]

    def across(self):
        here = self.place(self.team.me)
        return self.team.copy(self.source, here, self.sems.at[0], self.sems.at[1], self.team.far)

    def near(self):
        here = self.place(self.team.me)
        return self.team.copy(self.source, here, self.sems.at[2], self.sems.at[3], self.team.sibling)

    def passed(self):
        there = self.place(self.team.far)
        return self.team.copy(there, there, self.sems.at[4], self.sems.at[5], self.team.sibling)

    def kept(self):
        return pltpu.make_async_copy(self.source, self.place(self.team.me), self.sems.at[6])

    def start(self):
        self.across().start()
        self.near().start()
        self.kept().start()

    def middle(self):
        self.across().wait_recv()
        self.passed().start()

    def sent(self):
        self.across().wait_send()
        self.near().wait_send()
        self.passed().wait_send()


EXTRA = 72


def rotated_block(ref, shift, length, index):
    width = ref.shape[2]
    sub = lax.broadcasted_iota(jnp.int32, (32, 8, width), 1)
    start = lax.rem(shift + index * 256, length)
    group = lax.div(start, 8)
    skip = start - group * 8
    turned = pltpu.roll(ref[pl.ds(group, 33)], lax.rem(8 - skip, 8), 1)
    return jnp.where(sub < 8 - skip, turned[:32], turned[1:]).reshape(256, width)


def rotate(ref, shift, length, put):
    def one(index, nothing):
        put(index, rotated_block(ref, shift, length, index))
        return nothing

    lax.fori_loop(0, length // 256, one, 0)


def wrap(ref, length):
    ref[length // 8 : length // 8 + EXTRA] = ref[0:EXTRA]


def rotate_into(source, target, buffer, shift):
    length, width = source.shape
    buffer[0 : length // 8] = source[...].astype(FULL).reshape(length // 8, 8, width)
    wrap(buffer, length)

    def put(index, block):
        target[rows_at(index * 256, 256, 256), :] = block.astype(LOW)

    rotate(buffer, shift, length, put)


def forward_kernel(
    rows_of,
    keys_of,
    head_count,
    spans,
    q_ref,
    k_ref,
    v_ref,
    wo_ref,
    mixed_ref,
    mixed_rot_ref,
    log_ref,
    pieces,
    wo_all,
    q_hbm,
    k_hbm,
    v_hbm,
    v_heads,
    buffer,
    wo_sems,
    far_sems,
    near_sems,
    pass_sems,
    q_rot,
    k_rot,
    v_rot,
    store_sems,
):
    length, width = q_ref.shape
    team = Team()
    spread = Spread(team, wo_ref, wo_all, lambda owner: rows_at(owner * width, width, 64), wo_sems)

    def far_copy(index):
        rows = rows_at(index * 256, 256, 256)
        return team.copy(
            mixed_ref.at[rows], pieces.at[1, rows], far_sems.at[0, index], far_sems.at[1, index], team.far
        )

    def near_copy(index):
        rows = rows_at(index * 256, 256, 256)
        return team.copy(
            mixed_ref.at[rows], pieces.at[0, rows], near_sems.at[0, index], near_sems.at[1, index], team.sibling
        )

    def pass_copy(index):
        rows = rows_at(index * 256, 256, 256)
        return team.copy(
            pieces.at[1, rows], pieces.at[2, rows], pass_sems.at[0, index], pass_sems.at[1, index], team.sibling
        )

    team.greet((team.sibling, team.far))
    spread.start()
    small = length - LONGEST
    offset, border = rotation(spans)

    rotate_into(q_ref, q_rot, buffer, offset)
    rotate_into(k_ref, k_rot, buffer, offset)
    rotate_into(v_ref, v_rot, buffer, offset)
    stores = loads_of(((q_rot, q_hbm), (k_rot, k_hbm), (v_rot, v_hbm)), store_sems)
    v_all = v_rot[...]
    for head in range(head_count):
        v_heads[head] = jnp.concatenate(
            [keep_head(head, v_all), jnp.full((length, 256 - width), 1, jnp.bfloat16)], axis=1
        )

    def block(row, key_base, key_count, masked):
        rows = pl.ds(row, rows_of)
        total = jnp.zeros((rows_of, width), jnp.float32)
        logs = []
        for head in range(head_count):
            q_head = keep_head(head, q_rot[rows, :])
            top, parts = None, []
            for chunk in range(key_count // keys_of):
                keys = pl.ds(key_base + chunk * keys_of, keys_of)
                scores = dot(q_head, k_rot[keys, :], NT)
                if masked:
                    shape = (rows_of, keys_of)
                    row_id = lax.broadcasted_iota(jnp.int32, shape, 0) + (row - LONGEST)
                    key_id = lax.broadcasted_iota(jnp.int32, shape, 1) + chunk * keys_of
                    scores = jnp.where((row_id < border) == (key_id < border), scores, -1e30)
                high = jnp.max(scores, axis=1, keepdims=True)
                top = high if top is None else jnp.maximum(top, high)
                parts.append(scores)
            summed = jnp.zeros((rows_of, 256), jnp.float32)
            for chunk, scores in enumerate(parts):
                keys = pl.ds(key_base + chunk * keys_of, keys_of)
                weights = jnp.exp2((scores - top) * LOG_SCALE).astype(jnp.bfloat16)
                summed = summed + dot(weights, v_heads[head, keys, :], NN)
            norm = summed[:, 255:256]
            total = total + summed[:, :width] * (1.0 / norm)
            logs.append(top * LOG_SCALE + jnp.log2(norm))
        mixed_rot_ref[pl.ds(lax.div(row, 8), rows_of // 8)] = total.reshape(rows_of // 8, 8, width)
        logs.append(jnp.zeros((rows_of, 128 - head_count), jnp.float32))
        log_ref[rows, :] = jnp.concatenate(logs, axis=1)

    def send(index):
        rows = rows_at(index * 256, 256, 256)
        mixed_ref[rows, :] = rotated_block(mixed_rot_ref, length - offset, length, index).astype(LOW)
        far_copy(index).start()
        near_copy(index).start()

    def pass_on(index):
        far_copy(index).wait_recv()
        pass_copy(index).start()

    def little(index, nothing):
        block(pl.multiple_of(LONGEST + index * rows_of, rows_of), LONGEST, small, True)
        return nothing

    lax.fori_loop(0, small // rows_of, little, 0)
    for store in stores:
        store.start()
    lag, trips = 2, LONGEST // rows_of

    def large(index, nothing):
        block(pl.multiple_of(index * rows_of, rows_of), 0, LONGEST, False)

        @pl.when(index == 0)
        def _():
            mixed_rot_ref[length // 8 : length // 8 + 32] = mixed_rot_ref[0:32]

        send(index)

        @pl.when(index == trips // 2)
        def _():
            spread.middle()

        @pl.when(index >= lag)
        def _():
            pass_on(index - lag)

        return nothing

    lax.fori_loop(0, trips, large, 0)
    blocks = length // 256
    for index in range(trips, blocks):
        send(index)
    for index in range(trips - lag, blocks):
        pass_on(index)
    for index in range(blocks):
        near_copy(index).wait()
        far_copy(index).wait_send()
        pass_copy(index).wait()
    spread.sent()
    spread.near().wait_recv()
    spread.passed().wait_recv()
    spread.kept().wait()
    for store in stores:
        store.wait()


def attend_forward(spans, queries, key_rows, value_rows, out_weight):
    length, width = queries.shape
    head_count = width // HEAD
    return pl.pallas_call(
        functools.partial(forward_kernel, 256, 512, head_count),
        out_shape=(
            jax.ShapeDtypeStruct((length, width), jnp.bfloat16),
            jax.ShapeDtypeStruct((length // 8 + EXTRA, 8, width), jnp.float32),
            jax.ShapeDtypeStruct((length, 128), jnp.float32),
            jax.ShapeDtypeStruct((3, length, width), LOW),
            jax.ShapeDtypeStruct((4 * out_weight.shape[0], out_weight.shape[1]), LOW),
            jax.ShapeDtypeStruct((length, width), LOW),
            jax.ShapeDtypeStruct((length, width), LOW),
            jax.ShapeDtypeStruct((length, width), LOW),
        ),
        in_specs=[SMEM, VMEM, VMEM, VMEM, VMEM],
        out_specs=(VMEM, VMEM, VMEM, ANY, ANY, ANY, ANY, ANY),
        scratch_shapes=[
            pltpu.VMEM((head_count, length, 256), jnp.bfloat16),
            pltpu.VMEM((length // 8 + EXTRA, 8, width), FULL),
            DMA((7,)),
            DMA((2, length // 256)),
            DMA((2, length // 256)),
            DMA((2, length // 256)),
            pltpu.VMEM((length, width), LOW),
            pltpu.VMEM((length, width), LOW),
            pltpu.VMEM((length, width), LOW),
            DMA((3,)),
        ],
        compiler_params=pltpu.CompilerParams(
            collective_id=1, has_side_effects=True, vmem_limit_bytes=60 << 20
        ),
        name="attend_forward",
    )(spans, queries, key_rows, value_rows, out_weight)


class Plane:
    def __init__(self, size):
        self.me, self.lane = lax.axis_index("dp"), lax.axis_index("seq")
        self.size, self.bits = size, size.bit_length() - 1
        self.ranks = min(4, size // 2)
        self.side, self.rank = lax.rem(self.me, 2), lax.rem(lax.div(self.me, 2), self.ranks)
        self.extra = (size // 2 // self.ranks).bit_length() - 1

    def device(self, index):
        return (index, self.lane)

    def partner(self, bit):
        return self.device(flip(self.me, bit))

    def digit(self, bit):
        return lax.rem(lax.div(self.me, 1 << bit), 2)

    def other_rank(self, offset):
        return lax.rem(self.rank + offset, self.ranks)

    def ranked(self, offset):
        return self.device(self.me + 2 * (self.other_rank(offset) - self.rank))

    def remote(self, source, target, sems, index, device):
        return pltpu.make_async_remote_copy(
            src_ref=source,
            dst_ref=target,
            send_sem=sems.at[0, index],
            recv_sem=sems.at[1, index],
            device_id=device,
            device_id_type=MESH,
        )


class Halving:
    def __init__(self, plane, part, wire, first, sends, receives, sems):
        self.plane, self.part, self.wire, self.first = plane, part, wire, first
        self.sends, self.receives, self.sems = sends, receives, sems
        self.halvings, self.whole = halvings_of(plane.bits)
        self.stages = 2 * self.halvings + self.whole + 1
        half = part.shape[0]
        self.bases, self.sizes = [0], [half]
        for level in range(self.halvings):
            size = self.sizes[-1] // 2
            self.bases.append(self.bases[-1] + plane.digit(level + 1) * size)
            self.sizes.append(size)
        self.step = self.sizes[-1]
        self.shift = plane.side * half

    def inner(self, level):
        return rows_at(self.bases[level], self.sizes[level], self.step)

    def place(self, level):
        return rows_at(self.shift + self.bases[level], self.sizes[level], self.step)

    def copies(self, stage):
        plane = self.plane
        if stage < self.halvings + self.whole:
            return [
                plane.remote(self.sends[stage], self.receives[stage], self.sems, stage, plane.partner(stage + 1))
            ]
        level = 2 * self.halvings + self.whole - stage
        here = self.wire.at[self.place(level)]
        return [plane.remote(here, here, self.sems, stage, plane.partner(level))]

    def start(self, stage):
        if stage < self.halvings:
            size = self.sizes[stage + 1]
            first = self.bases[stage] + (1 - self.plane.digit(stage + 1)) * size
            self.sends[stage][...] = self.part[rows_at(first, size, self.step), :].astype(LOW)
        elif stage < self.halvings + self.whole:
            self.sends[stage][...] = self.part[self.inner(self.halvings), :].astype(LOW)
        elif stage == self.halvings + self.whole:
            self.wire[self.place(self.halvings), :] = self.part[self.inner(self.halvings), :].astype(LOW)
        for copy in self.copies(stage):
            copy.start()

    def finish(self, stage):
        for copy in self.copies(stage):
            copy.wait()
        if stage < self.halvings:
            self.part[self.inner(stage + 1), :] += self.receives[stage][...].astype(FULL)
        elif stage < self.halvings + self.whole:
            value = self.sends[stage][...].astype(FULL) + self.receives[stage][...].astype(FULL)
            self.part[self.inner(self.halvings), :] = value


def halvings_of(bits):
    halvings = min(bits - 1, 2)
    return halvings, bits - 1 - halvings


def halving_scratch(size, half, width):
    bits = size.bit_length() - 1
    halvings, whole = halvings_of(bits)
    shapes = [(half >> (stage + 1), width) for stage in range(halvings)] + [(half >> halvings, width)] * whole
    kinds = [pltpu.VMEM(dims, LOW) for dims in shapes]
    return [kinds, list(kinds), DMA((2, 2 * halvings + whole + 1))]


class Direct:
    first = 0

    def __init__(self, plane, source, wire, part, received, sends, receives, sems):
        self.plane, self.source, self.wire, self.part = plane, source, wire, part
        self.received, self.sends, self.receives, self.sems = received, sends, receives, sems
        self.half = source.shape[0] // 2
        self.piece = self.half // plane.ranks
        self.stages = 4 + plane.extra

    def side_rows(self, side):
        return rows_at(side * self.half, self.half, self.half)

    def rank_rows(self, rank):
        return rows_at(rank * self.piece, self.piece, self.piece)

    def own_rows(self):
        start = self.plane.side * self.half + self.plane.rank * self.piece
        return rows_at(start, self.piece, self.piece)

    def copies(self, stage):
        plane = self.plane
        if stage == 0:
            source = self.source.at[self.side_rows(1 - plane.side)]
            return [plane.remote(source, self.received, self.sems, 0, plane.partner(0))]
        if stage == self.stages - 1:
            here = self.wire.at[self.side_rows(plane.side)]
            return [plane.remote(here, here, self.sems, 1, plane.partner(0))]
        if 1 < stage < self.stages - 2:
            slot = plane.ranks + stage - 3
            index = 2 * plane.ranks + stage - 2
            device = plane.partner(plane.bits - plane.extra + stage - 2)
            return [plane.remote(self.sends.at[slot], self.receives.at[slot], self.sems, index, device)]
        copies = []
        for offset in range(1, plane.ranks):
            device = plane.ranked(offset)
            if stage == 1:
                slot = offset - 1
                copies.append(
                    plane.remote(self.sends.at[slot], self.receives.at[slot], self.sems, 1 + offset, device)
                )
            else:
                here = self.wire.at[self.own_rows()]
                copies.append(plane.remote(here, here, self.sems, plane.ranks + offset, device))
        return copies

    def start(self, stage):
        plane = self.plane
        if stage == 1:
            for offset in range(1, plane.ranks):
                rows = self.rank_rows(plane.other_rank(offset))
                self.sends[offset - 1] = self.part[rows, :].astype(LOW)
        elif 1 < stage < self.stages - 2:
            self.sends[plane.ranks + stage - 3] = self.part[self.rank_rows(plane.rank), :].astype(LOW)
        elif stage == self.stages - 2:
            self.wire[self.own_rows(), :] = self.part[self.rank_rows(plane.rank), :].astype(LOW)
        for copy in self.copies(stage):
            copy.start()

    def finish(self, stage):
        plane = self.plane
        for copy in self.copies(stage):
            copy.wait()
        if stage == 0:
            received = self.received[...].astype(FULL)
            self.part[...] = self.source[self.side_rows(plane.side), :].astype(FULL) + received
        elif stage == 1:
            value = self.part[self.rank_rows(plane.rank), :]
            for slot in range(plane.ranks - 1):
                value = value + self.receives[slot].astype(FULL)
            self.part[self.rank_rows(plane.rank), :] = value
        elif stage < self.stages - 2:
            slot = plane.ranks + stage - 3
            value = self.sends[slot].astype(FULL) + self.receives[slot].astype(FULL)
            self.part[self.rank_rows(plane.rank), :] = value


def direct_scratch(size, rows, width):
    ranks = min(4, size // 2)
    extra = (size // 2 // ranks).bit_length() - 1
    half = rows // 2
    pieces = pltpu.VMEM((ranks - 1 + extra, half // ranks, width), LOW)
    return [
        pltpu.VMEM((half, width), FULL),
        pltpu.VMEM((half, width), LOW),
        pieces,
        pieces,
        DMA((2, 2 * ranks + extra)),
    ]


class Events:
    def __init__(self, totals):
        self.totals = totals
        last = totals[0].stages - 1
        self.waiting = sorted(
            (2 * (stage - total.first) + index, index, stage)
            for index, total in enumerate(totals)
            for stage in range(total.first, last)
        )

    def start(self):
        for total in self.totals:
            total.start(total.first)

    def take(self, limit):
        ready = [event for event in self.waiting if event[0] < limit]
        self.waiting = [event for event in self.waiting if event[0] >= limit]
        for unused, index, stage in ready:
            self.totals[index].finish(stage)
            self.totals[index].start(stage + 1)

    def next(self, count):
        if self.waiting[:count]:
            self.take(self.waiting[min(count, len(self.waiting)) - 1][0] + 1)

    def end(self):
        self.take(1 << 20)
        for total in self.totals:
            total.finish(total.stages - 1)


def greet_all(team, plane, direct):
    barrier = pltpu.get_barrier_semaphore()
    others = [plane.partner(bit) for bit in range(plane.bits)]
    others += [team.device(team.sibling), team.device(team.far)]
    greeted = list(others)
    if direct:
        greeted = [plane.partner(0), team.device(team.sibling), team.device(team.far)]
        greeted += [plane.partner(plane.bits - plane.extra + index) for index in range(plane.extra)]
        greeted += [plane.ranked(offset) for offset in range(1, plane.ranks)]
    for other in greeted:
        pl.semaphore_signal(barrier, inc=1, device_id=other, device_id_type=MESH)
    pl.semaphore_wait(barrier, len(greeted))
    return others


def backward_kernel(
    keys_of,
    rows_of,
    head_count,
    size,
    spans,
    q_hbm,
    k_hbm,
    v_hbm,
    d_hbm,
    mixed_hbm,
    log_hbm,
    up_part,
    down_part,
    wo_part,
    out_far,
    dq_ref,
    dk_ref,
    dv_ref,
    up_sum,
    down_sum,
    wo_sum,
    out_in,
    d_rot,
    q_turned,
    d_turned,
    k_turned,
    q_heads,
    d_heads,
    dq_turned,
    dk_rot,
    dv_rot,
    log_rows,
    deltas,
    parts,
    wires,
    total_parts,
    wo_near,
    wo_far,
    wo_sems,
    out_sems,
    keep_sems,
    dq_side,
    q_rot,
    k_rot,
    v_rot,
    d_ref,
    mixed_rot_ref,
    log_ref,
    load_sems,
):
    length, width = q_rot.shape
    small = length - LONGEST
    offset, border = rotation(spans)
    low, full = jnp.bfloat16, jnp.float32
    team, plane = Team(), Plane(size)
    columns = wo_sum.shape[0]
    lanes_of = up_part.shape[1] // 2
    totals, loads = [], []
    for index, source in enumerate((up_part, up_part, down_part, down_part)):
        lanes = pl.ds((index % 2) * lanes_of, lanes_of)
        total = Halving(plane, parts.at[index], wires.at[index], index // 2 * 2, *total_parts[index])
        place = parts.at[index, total.inner(index // 2 * 2)]
        loads.append(pltpu.make_async_copy(source.at[:, lanes], place, keep_sems.at[index]))
        totals.append(total)
    for load in loads:
        load.start()
    events = Events(totals)
    greet_all(team, plane, False)
    for load in loads:
        load.wait()
    events.start()
    arrays = (
        (q_hbm, q_rot),
        (k_hbm, k_rot),
        (v_hbm, v_rot),
        (d_hbm, d_ref),
        (mixed_hbm, mixed_rot_ref),
        (log_hbm, log_ref),
    )
    fetches = loads_of(arrays, load_sems)
    for fetch in fetches:
        fetch.start()
    out_copy = team.copy(out_far, out_in, out_sems.at[0], out_sems.at[1], team.far)
    out_copy.start()

    def wo_rows(owner):
        return rows_at(owner * columns, columns, 64)

    wo_copies = [
        team.copy(wo_part.at[wo_rows(owner)], wo_near.at[slot], wo_sems.at[0, slot], wo_sems.at[1, slot], team.sibling)
        for slot, owner in enumerate((team.sibling, team.diagonal))
    ]
    for copy in wo_copies:
        copy.start()
    wo_across = team.copy(wo_far.at[0], wo_far.at[1], wo_sems.at[0, 2], wo_sems.at[1, 2], team.far)

    for fetch in fetches:
        fetch.wait()
    rotate_into(d_ref, d_rot, dq_turned, offset)
    q_all, k_all, d_all = q_rot[...], k_rot[...], d_rot[...]
    q_turned[...] = jnp.transpose(q_all)
    k_turned[...] = jnp.transpose(k_all)
    d_turned[...] = jnp.transpose(d_all)
    for head in range(head_count):
        q_heads[head] = keep_head(head, q_all)
        d_heads[head] = keep_head(head, d_all)
    products = jnp.transpose(d_all.astype(full) * mixed_rot_ref[0 : length // 8].reshape(length, width))
    for head in range(head_count):
        deltas[head : head + 1, :] = jnp.sum(products[head * HEAD : (head + 1) * HEAD, :], axis=0, keepdims=True)
    log_rows[...] = jnp.transpose(log_ref[...])[0:8, :]
    dq_side[...] = jnp.zeros_like(dq_side)

    def block(key_row, row_base, row_count, masked, before):
        keys = pl.ds(key_row, keys_of)
        dk_sum = jnp.zeros((keys_of, width), full)
        dv_sum = jnp.zeros((keys_of, width), full)
        for head in range(head_count):
            before(head)
            k_head = keep_head(head, k_rot[keys, :])
            v_head = keep_head(head, v_rot[keys, :])
            lanes = slice(head * HEAD, (head + 1) * HEAD)
            k_side = k_turned[lanes, keys]
            for chunk in range(row_count // rows_of):
                start = row_base + chunk * rows_of
                rows = slice(start, start + rows_of)
                scores = dot(k_head, q_turned[:, rows], NN)
                dprobs = dot(v_head, d_turned[:, rows], NN)
                probs = jnp.exp2(scores * LOG_SCALE - log_rows[head : head + 1, rows])
                if masked:
                    shape = (keys_of, rows_of)
                    key_id = lax.broadcasted_iota(jnp.int32, shape, 0) + (key_row - LONGEST)
                    row_id = lax.broadcasted_iota(jnp.int32, shape, 1) + chunk * rows_of
                    probs = jnp.where((row_id < border) == (key_id < border), probs, 0.0)
                dv_sum = dv_sum + dot(probs.astype(low), d_heads[head, rows, :], NN)
                draw = (probs * (dprobs - deltas[head : head + 1, rows])).astype(low)
                dk_sum = dk_sum + dot(draw, q_heads[head, rows, :], NN)
                dq_side[lanes, rows] += dot(k_side, draw, NN)
        groups = pl.ds(lax.div(key_row, 8), keys_of // 8)
        dk_rot[groups] = (dk_sum * SCALE).reshape(keys_of // 8, 8, width)
        dv_rot[groups] = dv_sum.reshape(keys_of // 8, 8, width)

    trips = LONGEST // keys_of

    def gather_wo():
        for copy in wo_copies:
            copy.wait()
        wo_far[0] = (wo_part[wo_rows(team.far), :].astype(full) + wo_near[1].astype(full)).astype(low)
        wo_across.start()

    def large(index, nothing):
        def before(head):
            for trip in range(trips):
                slot = trip * head_count + head
                limit = (slot * 2 + 3) // 5
                earlier = (slot * 2 + 1) // 5
                if limit > earlier:

                    @pl.when(index == trip)
                    def _(limit=limit, slot=slot):
                        events.waiting = [event for event in everything if event[0] >= earlier]
                        events.take(limit)
                        if slot == 1:
                            gather_wo()

        block(pl.multiple_of(index * keys_of, keys_of), 0, LONGEST, False, before)
        return nothing

    def little(index, nothing):
        block(
            pl.multiple_of(LONGEST + index * keys_of, keys_of), LONGEST, small, True, lambda head: None
        )
        return nothing

    everything = list(events.waiting)
    lax.fori_loop(0, trips, large, 0)
    slots = trips * head_count
    events.waiting = [event for event in everything if event[0] >= slots // 2]
    lax.fori_loop(0, small // keys_of, little, 0)

    def unrotate(buffer, target):
        wrap(buffer, length)

        def put(index, block_rows):
            target[rows_at(index * 256, 256, 256), :] = block_rows.astype(low)

        rotate(buffer, length - offset, length, put)

    unrotate(dk_rot, dk_ref)
    unrotate(dv_rot, dv_ref)
    dq_turned[0 : length // 8] = jnp.transpose(dq_side[...] * SCALE).reshape(length // 8, 8, width)
    unrotate(dq_turned, dq_ref)
    events.end()
    keeps = []
    for index, target in enumerate((up_sum, up_sum, down_sum, down_sum)):
        lanes = pl.ds((index % 2) * lanes_of, lanes_of)
        keeps.append(pltpu.make_async_copy(wires.at[index], target.at[:, lanes], keep_sems.at[index]))
    for keep in keeps:
        keep.start()
    wo_across.wait()
    mine = wo_part[wo_rows(team.me), :].astype(full) + wo_near[0].astype(full)
    wo_sum[...] = (mine + wo_far[1].astype(full)).astype(low)
    out_copy.wait()
    for keep in keeps:
        keep.wait()


def attend_backward(
    size, spans, q_rot, k_rot, v_rot, grad_mixed, mixed_rot, log_totals, up_part, down_part, wo_part, out_far
):
    length, width = q_rot.shape
    head_count = width // HEAD
    low, full = jnp.bfloat16, jnp.float32
    half = (up_part.shape[0], up_part.shape[1] // 2)
    whole = (2 * up_part.shape[0], up_part.shape[1])
    wo_shape = (wo_part.shape[0] // 4, wo_part.shape[1])

    def shape(dims):
        return jax.ShapeDtypeStruct(dims, low)

    grouped = (length // 8 + EXTRA, 8, width)
    return pl.pallas_call(
        functools.partial(backward_kernel, 256, 512, head_count, size),
        out_shape=(shape((length, width)),) * 3
        + (shape(whole), shape(whole), shape(wo_shape), shape(out_far.shape)),
        in_specs=[SMEM] + [ANY] * 8 + [VMEM, ANY],
        out_specs=(VMEM,) * 3 + (ANY, ANY, VMEM, ANY),
        scratch_shapes=[
            pltpu.VMEM((length, width), low),
            pltpu.VMEM((width, length), low),
            pltpu.VMEM((width, length), low),
            pltpu.VMEM((width, length), low),
            pltpu.VMEM((head_count, length, width), low),
            pltpu.VMEM((head_count, length, width), low),
            pltpu.VMEM(grouped, full),
            pltpu.VMEM(grouped, full),
            pltpu.VMEM(grouped, full),
            pltpu.VMEM((8, length), full),
            pltpu.VMEM((8, length), full),
            pltpu.VMEM((4, *half), full),
            pltpu.VMEM((4, 2 * half[0], half[1]), low),
            [halving_scratch(size, *half) for unused in range(4)],
            pltpu.VMEM((2, *wo_shape), low),
            pltpu.VMEM((2, *wo_shape), low),
            DMA((2, 3)),
            DMA((2,)),
            DMA((4,)),
            pltpu.VMEM((width, length), full),
            pltpu.VMEM((length, width), low),
            pltpu.VMEM((length, width), low),
            pltpu.VMEM((length, width), low),
            pltpu.VMEM((length, width), low),
            pltpu.VMEM(mixed_rot.shape, full),
            pltpu.VMEM(log_totals.shape, full),
            DMA((6,)),
        ],
        compiler_params=pltpu.CompilerParams(
            collective_id=3, has_side_effects=True, vmem_limit_bytes=63 << 20
        ),
        name="attend_backward",
    )(spans, q_rot, k_rot, v_rot, grad_mixed, mixed_rot, log_totals, up_part, down_part, wo_part, out_far)


def project_kernel(
    part,
    x_ref,
    gain,
    shift,
    wq,
    bq,
    wk,
    wv,
    bv,
    x_all,
    normed_hbm,
    q_hbm,
    k_hbm,
    v_hbm,
    landing,
    far_send,
    far_recv,
    near_send,
    near_recv,
    pass_send,
    pass_recv,
    keep_sem,
    normed,
    q_ref,
    k_ref,
    v_ref,
    store_sems,
):
    team = Team()
    own = x_ref.shape[0]
    count = own // part

    def piece(owner, index):
        return rows_at(owner * own + index * part, part, part)

    def far_copy(index):
        source = x_ref.at[rows_at(index * part, part, part)]
        return team.copy(
            source, landing.at[piece(team.me, index)], far_send.at[index], far_recv.at[index], team.far
        )

    def pass_copy(index):
        place = landing.at[piece(team.far, index)]
        return team.copy(place, place, pass_send.at[index], pass_recv.at[index], team.sibling)

    near = team.copy(
        x_ref, landing.at[rows_at(team.me * own, own, own)], near_send, near_recv, team.sibling
    )

    def keep(owner, source, slot):
        return pltpu.make_async_copy(source, x_all.at[rows_at(owner * own, own, own)], keep_sem.at[slot])

    team.greet((team.sibling, team.far))
    for index in range(count):
        far_copy(index).start()
    near.start()
    keep(team.me, x_ref, 0).start()

    gain_row, shift_row, bq_row, bv_row = as_row(gain), as_row(shift), as_row(bq), as_row(bv)

    def project(owner, index, values):
        standard, unused = standardize(values.astype(FULL))
        low = (standard * gain_row + shift_row).astype(LOW)
        rows = piece(owner, index)
        normed[rows, :] = low
        q_ref[rows, :] = (dot(low, wq[...], NT) + bq_row).astype(LOW)
        k_ref[rows, :] = dot(low, wk[...], NT).astype(LOW)
        v_ref[rows, :] = (dot(low, wv[...], NT) + bv_row).astype(LOW)

    def mine(index, nothing):
        project(team.me, index, x_ref[rows_at(index * part, part, part), :])
        return nothing

    def stores(slot, owner):
        rows = rows_at(owner * own, own, own)
        arrays = (normed, normed_hbm), (q_ref, q_hbm), (k_ref, k_hbm), (v_ref, v_hbm)
        return loads_of([(source.at[rows], target.at[rows]) for source, target in arrays], store_sems.at[slot])

    lax.fori_loop(0, count, mine, 0)
    for store in stores(0, team.me):
        store.start()
    near.wait()

    def next_to(index, nothing):
        project(team.sibling, index, landing[piece(team.sibling, index), :])
        return nothing

    lax.fori_loop(0, count, next_to, 0)
    for store in stores(1, team.sibling):
        store.start()

    def across(index, nothing):
        far_copy(index).wait_recv()
        pass_copy(index).start()
        project(team.far, index, landing[piece(team.far, index), :])
        pass_copy(index).wait_recv()
        project(team.diagonal, index, landing[piece(team.diagonal, index), :])
        return nothing

    lax.fori_loop(0, count, across, 0)
    for slot, owner in ((2, team.far), (3, team.diagonal)):
        for store in stores(slot, owner):
            store.start()
    for slot, owner in ((1, team.sibling), (2, team.far), (3, team.diagonal)):
        keep(owner, landing.at[rows_at(owner * own, own, own)], slot).start()
    for slot, owner in ((1, team.sibling), (2, team.far), (3, team.diagonal)):
        keep(owner, landing.at[rows_at(owner * own, own, own)], slot).wait()
    keep(team.me, x_ref, 0).wait()
    for slot, owner in enumerate((team.me, team.sibling, team.far, team.diagonal)):
        for store in stores(slot, owner):
            store.wait()
    for index in range(count):
        far_copy(index).wait_send()
        pass_copy(index).wait_send()


def gather_and_project(x, gain, shift, wq, bq, wk, wv, bv):
    own, width = x.shape
    length, columns, part = 4 * own, wq.shape[0], 128
    count = own // part
    narrow = jax.ShapeDtypeStruct((length, columns), LOW)
    wide = jax.ShapeDtypeStruct((length, width), LOW)
    return pl.pallas_call(
        functools.partial(project_kernel, part),
        out_shape=(wide, wide, narrow, narrow, narrow),
        in_specs=[VMEM] * 8,
        out_specs=(ANY,) * 5,
        scratch_shapes=[
            pltpu.VMEM((length, width), LOW),
            DMA((count,)),
            DMA((count,)),
            DMA,
            DMA,
            DMA((count,)),
            DMA((count,)),
            DMA((4,)),
            pltpu.VMEM((length, width), LOW),
            pltpu.VMEM((length, columns), LOW),
            pltpu.VMEM((length, columns), LOW),
            pltpu.VMEM((length, columns), LOW),
            DMA((4, 4)),
        ],
        compiler_params=pltpu.CompilerParams(
            collective_id=0, has_side_effects=True, vmem_limit_bytes=63 << 20
        ),
        name="gather_and_project",
    )(x, gain, shift, wq, bq, wk, wv, bv)


class Reduction:
    def __init__(self, team, near_out, near_in, far_out, far_in, sems):
        self.team = team
        self.near_out, self.near_in, self.far_out, self.far_in = near_out, near_in, far_out, far_in
        self.sems = sems

    def near(self, pair):
        return self.team.copy(
            self.near_out.at[pair % 2],
            self.near_in.at[pair],
            self.sems.at[0, pair],
            self.sems.at[1, pair],
            self.team.sibling,
        )

    def across(self, pair):
        return self.team.copy(
            self.far_out.at[pair], self.far_in.at[pair], self.sems.at[2, pair], self.sems.at[3, pair], self.team.far
        )

    def give(self, pair, values):
        @pl.when(pair >= 2)
        def _():
            self.near(pair - 2).wait_send()

        self.near_out[pair % 2] = values.astype(LOW)
        self.near(pair).start()

    def combine(self, pair, values):
        self.near(pair).wait_recv()
        return values + self.near_in[pair].astype(FULL)

    def send(self, pair, values):
        self.far_out[pair] = values.astype(LOW)
        self.across(pair).start()

    def arrived(self, pair):
        self.across(pair).wait_recv()
        return self.far_in[pair].astype(FULL)

    def finish(self, pairs):
        for pair in range(pairs // 2):
            self.across(pair).wait_send()
        for pair in (pairs - 2, pairs - 1):
            self.near(pair).wait_send()


def owner_at(team_me, step):
    half = lax.div(step, 4)
    odd = lax.rem(step, 2)
    one = flip(team_me, 0)
    base = one + odd * (team_me - one)
    return lax.rem(base + 2 * (1 - half), 4)


def part_at(step):
    return lax.rem(lax.div(step, 2), 2)


def ffn_kernel(
    part,
    size,
    mixed_hbm,
    pieces_hbm,
    x_hbm,
    cot_ref,
    wo_hbm,
    up_hbm,
    down_hbm,
    up_bias,
    out_bias,
    gain,
    shift,
    down_bias,
    far_hbm,
    own_hbm,
    grad_middle,
    grad_mixed,
    up_part,
    down_part,
    grad_wo,
    sums,
    middle_own,
    up_half,
    down_half,
    halves_out,
    halves_in,
    half_sems,
    halving_parts,
    keep_sems,
    cot_all,
    normed_all,
    hidden_all,
    gpre_all,
    out_slots,
    out_near,
    own_sum,
    near_out,
    near_in,
    far_out,
    far_in,
    mixed_out,
    branch_own,
    cot_sems,
    slot_sems,
    red_sems,
    a2a_sems,
    mixed_ref,
    pieces,
    x_all,
    wo,
    up,
    down,
    load_sems,
    out_far,
    out_own,
    store_sems,
):
    team = Team()
    length = mixed_ref.shape[0]
    width = x_all.shape[1]
    columns = mixed_ref.shape[1]
    own = length // 4
    steps = length // part

    def rows_of(owner, index):
        return rows_at(owner * own + index * part, part, part)

    def step_rows(device, step):
        return rows_of(owner_at(device, step), part_at(step))

    spreads = [
        Spread(
            team,
            cot_ref.at[pl.ds(index * part, part)],
            cot_all,
            lambda owner, index=index: rows_of(owner, index),
            cot_sems.at[index],
        )
        for index in range(own // part)
    ]
    reduction = Reduction(team, near_out, near_in, far_out, far_in, red_sems)

    def slot_copy(pair):
        slot = lax.rem(pair, 2)
        return team.copy(
            out_slots.at[slot], out_near.at[pair], slot_sems.at[0, slot], slot_sems.at[1, pair], team.sibling
        )

    plane = Plane(size)
    team.greet((team.sibling, team.far, team.diagonal), *[plane.partner(bit) for bit in range(3)])

    for spread in spreads:
        spread.start()
    arrays = (mixed_hbm, mixed_ref), (pieces_hbm, pieces), (x_hbm, x_all), (wo_hbm, wo), (up_hbm, up), (down_hbm, down)
    loads = loads_of(arrays, load_sems)
    for load in loads:
        load.start()
    for load in loads:
        load.wait()
    sums[...] = jnp.zeros_like(sums)
    gain_row, shift_row, bias_row = as_row(gain), as_row(shift), as_row(out_bias)
    up_row, down_row = as_row(up_bias), as_row(down_bias)

    def forward(step, keep_middle):
        rows = step_rows(team.me, step)

        def weights(owner):
            return wo[rows_at(owner * columns, columns, 64), :]

        branch = dot(mixed_ref[rows, :], weights(team.me), NN)
        branch = branch + dot(pieces[0, rows, :], weights(team.sibling), NN)
        branch = branch + dot(pieces[1, rows, :], weights(team.far), NN)
        branch = branch + dot(pieces[2, rows, :], weights(team.diagonal), NN)
        middle = x_all[rows, :].astype(FULL) + (branch + bias_row)
        if keep_middle:

            @pl.when(step >= steps // 2)
            def _():
                middle_own[rows_at(part_at(step) * part, part, part), :] = middle

        standard, unused = standardize(middle)
        low = (standard * gain_row + shift_row).astype(LOW)
        normed_all[rows, :] = low
        pre = dot(low, up[...], NN) + up_row
        bell = 0.5 * (1.0 + lax.erf(pre * 0.7071067811865476))
        hidden = (pre * bell).astype(LOW)
        hidden_all[rows, :] = hidden
        slope = bell + pre * (jnp.exp(pre * pre * -0.5) * 0.3989422804014327)
        gpre_all[rows, :] = slope.astype(LOW)

        out = dot(hidden, down[...], NN)
        pair = lax.div(step, 2)
        if keep_middle:
            place = rows_at(part_at(step) * part, part, part)

            @pl.when(step < steps // 2)
            def _():
                out_far[place, :] = out.astype(LOW)

            @pl.when(step >= steps // 2)
            def _():
                out_own[place, :] = middle + out + down_row
        else:

            @pl.when(pair >= 2)
            def _():
                slot_copy(pair - 2).wait_send()

            out_slots[lax.rem(pair, 2)] = out.astype(LOW)
            slot_copy(pair).start()
    def backward(step):
        rows = step_rows(team.me, step)
        slope = gpre_all[rows, :].astype(FULL)
        grad_pre = (dot(cot_all[rows, :], down[...], NT) * slope).astype(LOW)
        gpre_all[rows, :] = grad_pre
        sums[4:5, :] += column_sums(grad_pre.astype(FULL))
        return dot(grad_pre, up[...], NT)

    def pair_forward(pair, nothing):
        forward(2 * pair, False)
        forward(2 * pair + 1, True)
        return nothing

    half = width // 2
    down_total = Halving(plane, down_half, None, 0, *halving_parts)
    up_keep = pltpu.make_async_copy(up_half, up_part, keep_sems.at[0])
    down_keep = pltpu.make_async_copy(down_half.at[down_total.inner(2)], down_part, keep_sems.at[1])
    halves = (normed_all, gpre_all, up_half), (hidden_all, cot_all, down_half)
    side_copies = [
        plane.remote(halves_out.at[index], halves_in.at[index], half_sems, index, plane.partner(0))
        for index in range(2)
    ]
    def place_of(pair):
        return rows_at(part_at(2 * pair) * part, part, part)

    def add_out(pair):
        slot_copy(pair).wait_recv()
        place, given = place_of(pair), out_near[pair].astype(FULL)

        @pl.when(pair < steps // 4)
        def _():
            out_far[place, :] = (out_far[place, :].astype(FULL) + given).astype(LOW)

        @pl.when(pair >= steps // 4)
        def _():
            out_own[place, :] += given

    def combine(pair):
        reduction.near(pair).wait_recv()
        given = reduction.near_in[pair].astype(FULL)

        @pl.when(pair < steps // 4)
        def _():
            reduction.send(pair, reduction.far_out[lax.rem(pair, 2)].astype(FULL) + given)

        @pl.when(pair >= steps // 4)
        def _():
            own_sum[place_of(pair), :] += given

    def pair_backward(pair, nothing):
        first, second = 2 * pair, 2 * pair + 1
        for index, spread in enumerate(spreads):

            @pl.when(pair == index)
            def _(spread=spread):
                spread.middle()
                spread.passed().wait_recv()

        @pl.when(pair == len(spreads))
        def _():
            for spread in spreads:
                spread.near().wait_recv()
                spread.kept().wait()
            side_half(1)

        @pl.when(pair == len(spreads) + 1)
        def _():
            own_half(1)

        reduction.give(pair, backward(first))
        add_out(pair)

        @pl.when(pair >= 1)
        def _():
            combine(pair - 1)

        values = backward(second)

        @pl.when(pair < steps // 4)
        def _():
            far_out[lax.rem(pair, 2)] = values.astype(LOW)

        @pl.when(pair >= steps // 4)
        def _():
            own_sum[place_of(pair), :] = values

        return nothing

    def side_half(index):
        left, right, unused = halves[index]
        lanes = rows_at((1 - plane.side) * half, half, half)

        def one(slab, nothing):
            columns_of = rows_at(slab * 256, 256, 256)
            halves_out[index, :, columns_of] = dot(left[:, lanes], right[:, columns_of], TN).astype(LOW)
            return nothing

        lax.fori_loop(0, width // 256, one, 0)
        side_copies[index].start()

    def own_half(index):
        left, right, target = halves[index]
        lanes = rows_at(plane.side * half, half, half)

        def one(slab, nothing):
            columns_of = rows_at(slab * 256, 256, 256)
            target[:, columns_of] = dot(left[:, lanes], right[:, columns_of], TN)
            return nothing

        lax.fori_loop(0, width // 256, one, 0)

    def add_side(index):
        side_copies[index].wait()
        halves[index][2][...] += halves_in[index].astype(FULL)

    lax.fori_loop(0, steps // 2, pair_forward, 0)
    lax.fori_loop(0, steps // 2, pair_backward, 0)
    stores = loads_of(((out_far, far_hbm), (out_own, own_hbm)), store_sems)
    for store in stores:
        store.start()
    side_half(0)
    add_side(1)
    down_total.start(0)
    combine(steps // 2 - 1)

    def back(index, nothing):
        @pl.when(index == 1)
        def _():
            down_total.finish(0)
            down_total.start(1)

        rows = rows_at(index * part, part, part)
        own_rows = rows_of(team.me, index)
        grad = own_sum[rows, :] + reduction.arrived(index)
        standard, inverse = standardize(middle_own[rows, :])
        incoming = cot_all[own_rows, :].astype(FULL)
        grad_mid = incoming + norm_back(grad, gain_row, standard, inverse)
        grad_middle[rows, :] = grad_mid
        branch_low = grad_mid.astype(LOW)
        branch_own[rows, :] = branch_low
        for slot, owner in enumerate((team.sibling, team.far, team.diagonal)):
            side = wo[rows_at(owner * columns, columns, 64), :]
            mixed_out[slot, rows, :] = dot(branch_low, side, NT).astype(LOW)
            exchange(index, slot, owner).start()
        side = wo[rows_at(team.me * columns, columns, 64), :]
        grad_mixed[own_rows, :] = dot(branch_low, side, NT).astype(LOW)
        sums[0:1, :] += column_sums(grad * standard)
        sums[1:2, :] += column_sums(grad)
        sums[2:3, :] += column_sums(branch_low.astype(FULL))
        sums[3:4, :] += column_sums(incoming)
        return nothing

    def exchange(index, slot, owner):
        return team.copy(
            mixed_out.at[slot, rows_at(index * part, part, part)],
            grad_mixed.at[rows_of(team.me, index)],
            a2a_sems.at[2 * index, slot],
            a2a_sems.at[2 * index + 1, slot],
            owner,
        )

    lax.fori_loop(0, own // part, back, 0)
    own_half(0)
    own_rows = rows_at(team.me * own, own, own)
    for source, owner in (
        (mixed_ref.at[own_rows], team.me),
        (pieces.at[0, own_rows], team.sibling),
        (pieces.at[1, own_rows], team.far),
        (pieces.at[2, own_rows], team.diagonal),
    ):
        grad_wo[rows_at(owner * columns, columns, 64), :] = dot(source[...], branch_own[...], TN).astype(LOW)
    down_total.finish(1)
    down_keep.start()
    add_side(0)
    up_keep.start()
    for index in range(own // part):
        for slot, owner in enumerate((team.sibling, team.far, team.diagonal)):
            exchange(index, slot, owner).wait()
    down_keep.wait()
    up_keep.wait()
    for store in stores:
        store.wait()
    for spread in spreads:
        spread.sent()
    for pair in (steps // 2 - 2, steps // 2 - 1):
        slot_copy(pair).wait_send()
    reduction.finish(steps // 2)


def ffn(size, mixed, pieces, x_all, cotangent, wo, up, down, up_bias, out_bias, gain, shift, down_bias):
    length, columns = mixed.shape
    width = x_all.shape[1]
    hidden = up.shape[1]
    own, part = length // 4, 320
    steps = length // part
    pairs = steps // 2

    def shape(dims, kind):
        return jax.ShapeDtypeStruct(dims, kind)

    return pl.pallas_call(
        functools.partial(ffn_kernel, part, size),
        out_shape=(
            shape((own, width), LOW),
            shape((own, width), FULL),
            shape((own, width), FULL),
            shape((length, columns), LOW),
            shape((width // 2, hidden), FULL),
            shape((hidden // 8, width), FULL),
            shape((width, width), LOW),
            shape((8, width), FULL),
        ),
        in_specs=[ANY] * 7 + [VMEM] * 5,
        out_specs=(ANY, ANY, VMEM, VMEM, ANY, ANY, VMEM, VMEM),
        scratch_shapes=[
            pltpu.VMEM((own, width), FULL),
            pltpu.VMEM((width // 2, hidden), FULL),
            pltpu.VMEM((hidden // 2, width), FULL),
            pltpu.VMEM((2, width // 2, width), LOW),
            pltpu.VMEM((2, width // 2, width), LOW),
            DMA((2, 2)),
            halving_scratch(size, width // 2, width),
            DMA((2,)),
            pltpu.VMEM((length, width), LOW),
            pltpu.VMEM((length, width), LOW),
            pltpu.VMEM((length, hidden), LOW),
            pltpu.VMEM((length, hidden), LOW),
            pltpu.VMEM((2, part, width), LOW),
            pltpu.VMEM((pairs, part, width), LOW),
            pltpu.VMEM((own, width), FULL),
            pltpu.VMEM((2, part, width), LOW),
            pltpu.VMEM((pairs, part, width), LOW),
            pltpu.VMEM((pairs // 2, part, width), LOW),
            pltpu.VMEM((pairs // 2, part, width), LOW),
            pltpu.VMEM((3, own, columns), LOW),
            pltpu.VMEM((own, width), LOW),
            DMA((own // part, 7)),
            DMA((2, pairs)),
            DMA((4, pairs)),
            DMA((4, 3)),
            pltpu.VMEM(mixed.shape, LOW),
            pltpu.VMEM(pieces.shape, LOW),
            pltpu.VMEM(x_all.shape, LOW),
            pltpu.VMEM(wo.shape, LOW),
            pltpu.VMEM(up.shape, LOW),
            pltpu.VMEM(down.shape, LOW),
            DMA((6,)),
            pltpu.VMEM((own, width), LOW),
            pltpu.VMEM((own, width), FULL),
            DMA((2,)),
        ],
        compiler_params=pltpu.CompilerParams(
            collective_id=2, has_side_effects=True, vmem_limit_bytes=63 << 20
        ),
        name="ffn",
    )(mixed, pieces, x_all, cotangent, wo, up, down, up_bias, out_bias, gain, shift, down_bias)


def last_kernel(
    part,
    size,
    dq_hbm,
    dk_hbm,
    dv_hbm,
    wq,
    wk,
    wv,
    normed_hbm,
    x_hbm,
    grad_hbm,
    gain,
    wo_sum,
    wide,
    input_grad,
    grad_sum,
    vectors,
    own_grad,
    near_out,
    near_in,
    far_out,
    far_in,
    red_sems,
    sources,
    wires,
    total_parts,
    packed,
    packed_in,
    vec_sems,
    keep_sems,
    dq_ref,
    dk_ref,
    dv_ref,
    normed_all,
    x_all,
    grad_middle,
    load_sems,
):
    team, plane = Team(), Plane(size)
    arrays = (
        (dq_hbm, dq_ref),
        (dk_hbm, dk_ref),
        (dv_hbm, dv_ref),
        (normed_hbm, normed_all),
        (x_hbm, x_all),
        (grad_hbm, grad_middle),
    )
    loads = loads_of(arrays, load_sems)
    for load in loads:
        load.start()
    length, columns = dq_ref.shape
    width = normed_all.shape[1]
    own = length // 4
    pairs = length // part // 2
    grads = Reduction(team, near_out, near_in, far_out, far_in, red_sems)
    slabs = sources.shape[0]
    lanes_of = width // slabs
    totals = [Direct(plane, sources.at[slab], wires.at[slab], *total_parts[slab]) for slab in range(slabs)]
    others = greet_all(team, plane, True)
    events = Events(totals)

    def slab_grads(slab, nothing):
        lanes = rows_at(slab * lanes_of, lanes_of, lanes_of)
        for index, source in enumerate((dq_ref, dk_ref, dv_ref)):
            value = dot(source[...], normed_all[:, lanes], TN)
            sources[slab, index * columns : (index + 1) * columns, :] = value.astype(LOW)
        sources[slab, 3 * columns : 4 * columns, :] = wo_sum[:, lanes]
        for index, total in enumerate(totals):

            @pl.when(slab == index)
            def _(total=total):
                total.start(0)

        return nothing

    for load in loads[:4]:
        load.wait()
    lax.fori_loop(0, slabs, slab_grads, 0)
    for load in loads[4:]:
        load.wait()
    gain_row = as_row(gain)
    packed[...] = jnp.zeros_like(packed)
    packed[0:4, :] = wide[0:4, :]
    packed[8:9, :] = wide[4:5, :]
    packed[9:10, 0:columns] = column_sums(dq_ref[...].astype(FULL))
    packed[10:11, 0:columns] = column_sums(dv_ref[...].astype(FULL))

    def step_rows(step):
        return rows_at(owner_at(team.me, step) * own + part_at(step) * part, part, part)

    def compute(step):
        rows = step_rows(step)
        total = dot(dq_ref[rows, :], wq[...], NN) + dot(dk_ref[rows, :], wk[...], NN)
        return total + dot(dv_ref[rows, :], wv[...], NN)

    everything = list(events.waiting)

    def events_at(pair, plan):
        for when, (start, stop) in plan.items():

            @pl.when(pair == when)
            def _(start=start, stop=stop):
                events.waiting = everything[start:stop]
                events.take(1 << 20)

    def pair_step(pair, nothing):
        first, second = 2 * pair, 2 * pair + 1
        grads.give(pair, compute(first))
        standard, unused = standardize(x_all[step_rows(second), :].astype(FULL))
        events_at(pair, {1: (0, 1), 2: (1, 2), 3: (2, 4)})
        values = grads.combine(pair, compute(second))
        packed[4:5, :] += column_sums(values * standard)
        packed[5:6, :] += column_sums(values)

        @pl.when(pair < pairs // 2)
        def _():
            grads.send(pair, values)

        @pl.when(pair >= pairs // 2)
        def _():
            own_grad[rows_at(part_at(second) * part, part, part), :] = values

        events_at(pair, {3: (4, 5)})
        return nothing

    lax.fori_loop(0, pairs, pair_step, 0)
    events.waiting = everything[5:]

    def vector_copy(step):
        return pltpu.make_async_remote_copy(
            src_ref=packed.at[pl.ds(16 * step, 16)],
            dst_ref=packed_in.at[step],
            send_sem=vec_sems.at[0, step],
            recv_sem=vec_sems.at[1, step],
            device_id=others[step],
            device_id_type=MESH,
        )

    def finish_rows(index):
        rows = pl.ds(index * part, part)
        grad = own_grad[rows, :] + grads.arrived(index)
        standard, inverse = standardize(x_all[rows_at(team.me * own + index * part, part, part), :].astype(FULL))
        input_grad[rows, :] = grad_middle[rows, :] + norm_back(grad, gain_row, standard, inverse)

    for step in range(len(others)):
        vector_copy(step).start()
        events.next(1)
        vector_copy(step).wait()
        here = packed[16 * step : 16 * (step + 1), :]
        keep = 16 if step < plane.bits else 8
        row = lax.broadcasted_iota(jnp.int32, here.shape, 0)
        added = here + jnp.where(row < keep, packed_in[step], 0.0)
        packed[16 * (step + 1) : 16 * (step + 2), :] = added
    vectors[...] = packed[16 * len(others) : 16 * (len(others) + 1), :]
    events.take(1 << 20)
    for index in range(own // part):
        finish_rows(index)
    events.end()
    keeps = []
    for slab in range(slabs):
        lanes = pl.ds(slab * lanes_of, lanes_of)
        keeps.append(pltpu.make_async_copy(wires.at[slab], grad_sum.at[:, lanes], keep_sems.at[slab]))
    for keep in keeps:
        keep.start()
    for keep in keeps:
        keep.wait()
    grads.finish(pairs)


def last(size, dq, dk, dv, wq, wk, wv, normed_all, x_all, grad_middle, gain, wo_sum, wide):
    length, columns = dq.shape
    own, width = grad_middle.shape
    part, slabs = 320, 3
    pairs = length // part // 2
    bits = size.bit_length() - 1
    slab = (4 * columns, width // slabs)

    def shape(dims, kind):
        return jax.ShapeDtypeStruct(dims, kind)

    return pl.pallas_call(
        functools.partial(last_kernel, part, size),
        out_shape=(
            shape((own, width), FULL),
            shape((4 * columns, width), LOW),
            shape((16, width), FULL),
        ),
        in_specs=[ANY] * 3 + [VMEM] * 3 + [ANY] * 3 + [VMEM] * 3,
        out_specs=(VMEM, ANY, VMEM),
        scratch_shapes=[
            pltpu.VMEM((own, width), FULL),
            pltpu.VMEM((2, part, width), LOW),
            pltpu.VMEM((pairs, part, width), LOW),
            pltpu.VMEM((pairs // 2, part, width), LOW),
            pltpu.VMEM((pairs // 2, part, width), LOW),
            DMA((4, pairs)),
            pltpu.VMEM((slabs, *slab), LOW),
            pltpu.VMEM((slabs, *slab), LOW),
            [direct_scratch(size, *slab) for unused in range(slabs)],
            pltpu.VMEM((16 * (bits + 3), width), FULL),
            pltpu.VMEM((bits + 2, 16, width), FULL),
            DMA((2, bits + 2)),
            DMA((slabs,)),
            pltpu.VMEM(dq.shape, LOW),
            pltpu.VMEM(dk.shape, LOW),
            pltpu.VMEM(dv.shape, LOW),
            pltpu.VMEM(normed_all.shape, LOW),
            pltpu.VMEM(x_all.shape, LOW),
            pltpu.VMEM(grad_middle.shape, FULL),
            DMA((6,)),
        ],
        compiler_params=pltpu.CompilerParams(
            collective_id=4, has_side_effects=True, vmem_limit_bytes=60 << 20
        ),
        name="last",
    )(dq, dk, dv, wq, wk, wv, normed_all, x_all, grad_middle, gain, wo_sum, wide)


def local(
    size,
    layer_input,
    segment_ids,
    cotangent,
    attn_gain,
    attn_shift,
    query_weight,
    query_bias,
    key_weight,
    value_weight,
    value_bias,
    out_weight,
    out_bias,
    ffn_gain,
    ffn_shift,
    up_weight,
    up_bias,
    down_weight,
    down_bias,
):
    query_side, key_side, value_side = query_weight.T, key_weight.T, value_weight.T
    x_all, normed_rows, queries, key_rows, value_rows = gather_and_project(
        layer_input,
        attn_gain,
        attn_shift,
        query_side,
        query_bias,
        key_side,
        value_side,
        value_bias,
    )
    mixed, mixed_rot, log_totals, pieces, out_all, q_rot, k_rot, v_rot = attend_forward(
        segment_ids, queries, key_rows, value_rows, out_weight
    )
    out_far, out_own, grad_middle, grad_mixed, up_part, down_part, out_part, sums = ffn(
        size,
        mixed,
        pieces,
        x_all,
        cotangent,
        out_all,
        up_weight,
        down_weight,
        up_bias,
        out_bias,
        ffn_gain,
        ffn_shift,
        down_bias,
    )
    dq, dk, dv, grad_up, grad_down, wo_sum, out_in = attend_backward(
        size, segment_ids, q_rot, k_rot, v_rot, grad_mixed, mixed_rot, log_totals, up_part, down_part, out_part, out_far
    )
    layer_output = (out_own + out_in.astype(FULL)).astype(LOW)
    input_grad, grads, vectors = last(
        size,
        dq,
        dk,
        dv,
        query_side,
        key_side,
        value_side,
        normed_rows,
        x_all,
        grad_middle,
        attn_gain,
        wo_sum,
        sums,
    )
    columns = query_side.shape[0]
    grads = grads.astype(FULL)
    return (
        layer_output,
        input_grad,
        vectors[4],
        vectors[5],
        grads[0:columns].T,
        vectors[9, 0:columns],
        grads[columns : 2 * columns].T,
        grads[2 * columns : 3 * columns].T,
        vectors[10, 0:columns],
        grads[3 * columns :],
        vectors[2],
        vectors[0],
        vectors[1],
        grad_up.astype(FULL),
        vectors[8],
        grad_down.astype(FULL),
        vectors[3],
    )


def solution(mesh):
    return jax.shard_map(
        functools.partial(local, mesh.shape["dp"]),
        mesh=mesh,
        in_specs=(
            P(("dp", "seq"), None),
            P("dp", None),
            P(("dp", "seq"), None),
            P(),
            P(),
            P(None, "seq"),
            P("seq"),
            P(None, "seq"),
            P(None, "seq"),
            P("seq"),
            P("seq", None),
            P(),
            P(),
            P(),
            P(None, "seq"),
            P("seq"),
            P("seq", None),
            P(),
        ),
        out_specs=(
            P(("dp", "seq"), None),
            P(("dp", "seq"), None),
            P(),
            P(),
            P(None, "seq"),
            P("seq"),
            P(None, "seq"),
            P(None, "seq"),
            P("seq"),
            P("seq", None),
            P(),
            P(),
            P(),
            P(None, "seq"),
            P("seq"),
            P("seq", None),
            P(),
        ),
        check_vma=False,
    )
```
